32 devices in a mesh: dp: 8 (over z, x), tensor: 4 (over y, core).
Axes of the slice: x: 2, y: 2, z: 4, core: 2. Of those that a mesh axis runs over, the one named last changes fastest.
Arguments:
- frames: bfloat16 [2, 32768, 512], P(None, ('dp', 'tensor')), may hold values from -6 to 6
- cotangent: bfloat16 [2, 32768, 512], P(None, ('dp', 'tensor')), may hold values from -6 to 6
- clip_lengths: int32 [2, 32, 4], P(None, 'dp'), may hold values from 1 to 512, 1024 in all within a row
- in_proj: float32 [512, 8, 192], P('dp', 'tensor'), may hold values from -0.25 to 0.25
- out_proj: float32 [8, 64, 512], P('tensor', None, 'dp'), may hold values from -1 to 1
- up_proj: float32 [512, 2048], P('dp', 'tensor'), may hold values from -0.25 to 0.25
- down_proj: float32 [2048, 512], P('tensor', 'dp'), may hold values from -0.125 to 0.125
- small_params: float32 [6, 512], replicated, may hold values from 0.5 to 1.5
- in_first: float32 [512, 8, 192], P('dp', 'tensor'), may hold values from -384 to 384
- in_second: float32 [512, 8, 192], P('dp', 'tensor'), may hold values from 4194.304 to 16777.217
- out_first: float32 [8, 64, 512], P('tensor', None, 'dp'), may hold values from -128 to 128
- out_second: float32 [8, 64, 512], P('tensor', None, 'dp'), may hold values from 589.824 to 2359.296
- up_first: float32 [512, 2048], P('dp', 'tensor'), may hold values from -384 to 384
- up_second: float32 [512, 2048], P('dp', 'tensor'), may hold values from 4096 to 16384
- down_first: float32 [2048, 512], P('tensor', 'dp'), may hold values from -768 to 768
- down_second: float32 [2048, 512], P('tensor', 'dp'), may hold values from 16384 to 65536
- small_first: float32 [6, 512], replicated, may hold values from -1536 to 1536
- small_second: float32 [6, 512], replicated, may hold values from 65536 to 262144
Outputs:
- block_out: bfloat16 [2, 32768, 512], P(None, ('dp', 'tensor'))
- input_grad: bfloat16 [2, 32768, 512], P(None, ('dp', 'tensor'))
- in_new: float32 [512, 8, 192], P('dp', 'tensor')
- in_new_first: float32 [512, 8, 192], P('dp', 'tensor')
- in_new_second: float32 [512, 8, 192], P('dp', 'tensor')
- in_copy: bfloat16 [512, 8, 192], P('dp', 'tensor')
- out_new: float32 [8, 64, 512], P('tensor', None, 'dp')
- out_new_first: float32 [8, 64, 512], P('tensor', None, 'dp')
- out_new_second: float32 [8, 64, 512], P('tensor', None, 'dp')
- out_copy: bfloat16 [8, 64, 512], P('tensor', None, 'dp')
- up_new: float32 [512, 2048], P('dp', 'tensor')
- up_new_first: float32 [512, 2048], P('dp', 'tensor')
- up_new_second: float32 [512, 2048], P('dp', 'tensor')
- up_copy: bfloat16 [512, 2048], P('dp', 'tensor')
- down_new: float32 [2048, 512], P('tensor', 'dp')
- down_new_first: float32 [2048, 512], P('tensor', 'dp')
- down_new_second: float32 [2048, 512], P('tensor', 'dp')
- down_copy: bfloat16 [2048, 512], P('tensor', 'dp')
- small_grad: float32 [6, 512], replicated
- small_new: float32 [6, 512], replicated
- small_new_first: float32 [6, 512], replicated
- small_new_second: float32 [6, 512], replicated
- norms: float32 [2, 10], replicated
The draws below stay inside these ranges and needn't reach their ends.
Inputs may be any that keep to these rules, and one draw needn't show every extreme that they name: `clip_lengths`: each bucket's 4 runs are whole numbers that sum to 1024; the last run of each bucket is padding.
All inputs are finite; a program needn't handle non-finite values.
Results may differ from the reference program's by a relative error of at most 0.015.
Values may be sent and summed in bfloat16 or wider, within the bound.
A program may use at most 256 MiB of HBM per device.

```python
import math
import jax
import jax.numpy as jnp
import numpy as np
from jax import lax

D = 512
HEADS = 8
HEAD_DIM = 64
FF = 2048
WINDOW = 250
LEN = 1024
CLIPS = 4
MICRO = 2
STEP = 3
ROWS = 32768
BUCKETS = 32
GRAD_ROWS = 65536
CLIP_MOST = 512


def steps_of(rng, shape, shards, smallest, largest):
    level, own = 1.0, jax.random.fold_in(rng, 6)
    for dim, shards_of in shards:
        heights = jnp.exp(jax.random.uniform(jax.random.fold_in(own, dim), (shards_of,), jnp.float32, smallest / len(shards), largest / len(shards)))
        level = level * jnp.repeat(heights, shape[dim] // shards_of).reshape([-1 if axis == dim else 1 for axis in range(len(shape))])
    return level


def split_up(number_of, total, reach, lean):
    portions = [(1 << 20) // math.isqrt(standing ** lean) + 1 for standing in range(2, number_of + 1)]
    rest, counts = total - reach - (number_of - 1), [1] * (number_of - 1)
    while rest > 0:
        free = [i for i in range(number_of - 1) if counts[i] < reach]
        whole, remaining = sum([portions[i] for i in free]), rest
        for i in free:
            addition = min(reach - counts[i], max(1, remaining * portions[i] // whole), rest)
            counts[i] = counts[i] + addition
            rest = rest - addition
    return np.array([reach] + counts)


def uneven_parts(stream_key, amount, total, most, slope):
    if amount == 2:
        one = jax.random.randint(stream_key, (), max(1, total - most), min(most, total - 1) + 1)
        return jnp.stack([one, total - one])
    sizes = jnp.asarray(split_up(amount, total, most, slope), jnp.int32)
    pairs = (amount - 1) // 2
    giver, receiver = sizes[1:1 + 2 * pairs:2], sizes[2:2 + 2 * pairs:2]
    slack = jnp.minimum(giver - 1, most - receiver)
    moved = jax.random.randint(jax.random.fold_in(stream_key, 1), (pairs,), 0, 1 << 20) % (slack + 1)
    sizes = sizes.at[1:1 + 2 * pairs:2].set(giver - moved).at[2:2 + 2 * pairs:2].set(receiver + moved)
    return sizes[jax.random.permutation(jax.random.fold_in(stream_key, 2), amount)]


def noise(own_key, dims, spread, reach, shards=(), held_as=jnp.bfloat16):
    drawn = spread * jax.random.normal(own_key, dims, jnp.float32)
    if shards:
        drawn = drawn * steps_of(own_key, dims, shards, -0.22, 0.18)
    return jnp.clip(drawn, -reach, reach).astype(held_as)


def setup_inputs(seed: int = 0) -> dict:
    keys = jax.random.split(jax.random.key(seed), 19)
    frames = noise(keys[0], (MICRO, ROWS, D), 1.0, 6.0, ((1, 32),))
    cotangent = noise(keys[1], (MICRO, ROWS, D), 1.0, 6.0, ((1, 32),))
    clip_lengths = jax.vmap(lambda own: uneven_parts(own, CLIPS, LEN, CLIP_MOST, 2))(jax.random.split(keys[2], MICRO * BUCKETS)).reshape((MICRO, BUCKETS, CLIPS)).astype(jnp.int32)
    in_proj = noise(keys[3], (D, HEADS, 3 * HEAD_DIM), D ** -0.5, 0.25, ((0, 8), (1, 4)), jnp.float32)
    out_proj = noise(keys[4], (HEADS, HEAD_DIM, D), (D // 16) ** -0.5, 1.0, ((0, 4), (2, 8)), jnp.float32)
    up_proj = noise(keys[5], (D, FF), D ** -0.5, 0.25, ((0, 8), (1, 4)), jnp.float32)
    down_proj = noise(keys[6], (FF, D), FF ** -0.5, 0.125, ((0, 4), (1, 8)), jnp.float32)
    small_params = jnp.clip(1.0 + 0.1 * jax.random.normal(keys[7], (6, D), jnp.float32), 0.5, 1.5)
    in_first = noise(keys[8], (D, HEADS, 3 * HEAD_DIM), (4.0 * (GRAD_ROWS / WINDOW) ** 0.5), 384.0, ((0, 8), (1, 4)), jnp.float32)
    in_second = jnp.clip(jnp.exp(math.log(16777.217) - 1.3862944 * jax.random.uniform(keys[9], (D, HEADS, 3 * HEAD_DIM), jnp.float32) ** steps_of(keys[9], (D, HEADS, 3 * HEAD_DIM), ((0, 8), (1, 4)), -0.2, 0.2)), 4194.304, 16777.217)
    out_first = noise(keys[10], (HEADS, HEAD_DIM, D), (1.5 * (GRAD_ROWS / WINDOW) ** 0.5), 128.0, ((0, 4), (2, 8)), jnp.float32)
    out_second = jnp.clip(jnp.exp(math.log(2359.296) - 1.3862944 * jax.random.uniform(keys[11], (HEADS, HEAD_DIM, D), jnp.float32) ** steps_of(keys[11], (HEADS, HEAD_DIM, D), ((0, 4), (2, 8)), -0.2, 0.2)), 589.824, 2359.296)
    up_first = noise(keys[12], (D, FF), (0.25 * GRAD_ROWS ** 0.5), 384.0, ((0, 8), (1, 4)), jnp.float32)
    up_second = jnp.clip(jnp.exp(math.log(16384.0) - 1.3862944 * jax.random.uniform(keys[13], (D, FF), jnp.float32) ** steps_of(keys[13], (D, FF), ((0, 8), (1, 4)), -0.2, 0.2)), 4096.0, 16384.0)
    down_first = noise(keys[14], (FF, D), (0.5 * GRAD_ROWS ** 0.5), 768.0, ((0, 4), (1, 8)), jnp.float32)
    down_second = jnp.clip(jnp.exp(math.log(65536.0) - 1.3862944 * jax.random.uniform(keys[15], (FF, D), jnp.float32) ** steps_of(keys[15], (FF, D), ((0, 4), (1, 8)), -0.2, 0.2)), 16384.0, 65536.0)
    small_first = noise(keys[16], (6, D), (GRAD_ROWS ** 0.5), 1536.0, (), jnp.float32)
    small_second = jnp.clip(jnp.exp(jax.random.uniform(keys[17], (6, D), jnp.float32, math.log(65536.0), math.log(262144.0))), 65536.0, 262144.0)
    return dict(frames=frames, cotangent=cotangent, clip_lengths=clip_lengths, in_proj=in_proj, out_proj=out_proj, up_proj=up_proj, down_proj=down_proj, small_params=small_params, in_first=in_first, in_second=in_second, out_first=out_first, out_second=out_second, up_first=up_first, up_second=up_second, down_first=down_first, down_second=down_second, small_first=small_first, small_second=small_second)


@jax.custom_vjp
def low(v):
    return lax.optimization_barrier(v.astype(jnp.bfloat16)).astype(jnp.float32)

@jax.custom_vjp
def low_back(v):
    return v

def low_keep(v):
    return (low(v), None)

def low_pass(kept, grad):
    return (grad,)

def back_keep(v):
    return (v, None)

def back_low(kept, grad):
    return (low(grad),)
low.defvjp(low_keep, low_pass)
low_back.defvjp(back_keep, back_low)
beta_first = 0.5
beta_second = 0.5
adam_eps = 1e-06
decay_rate = 0.01
learn_rate = 0.3
highest = lax.Precision.HIGHEST

def clip_layout(lengths):
    clip_ends = jnp.cumsum(lengths).astype(jnp.int32)
    position = jnp.arange(LEN, dtype=jnp.int32)
    clip_of = lax.optimization_barrier(jnp.sum((position[:, None] >= clip_ends[None, :CLIPS - 1]).astype(jnp.int32), axis=1)).astype(jnp.int32)
    starts = (clip_ends - lengths).astype(jnp.int32)
    belongs = clip_of[:, None] == jnp.arange(CLIPS, dtype=jnp.int32)[None, :]
    clip_begin = lax.optimization_barrier(jnp.sum(jnp.where(belongs, starts[None, :], 0), axis=1)).astype(jnp.int32)
    return (clip_of, position - clip_begin)

def allowed_pairs(clip_of):
    position = jnp.arange(LEN, dtype=jnp.int32)
    causal = position[None, :] <= position[:, None]
    inside = position[:, None] - position[None, :] < WINDOW
    same_clip = clip_of[:, None] == clip_of[None, :]
    return causal & inside & same_clip

def rotate(values_in, offset):
    half_dim = HEAD_DIM // 2
    frequency = jnp.exp(jnp.arange(half_dim, dtype=jnp.float32) * (-2.0 * math.log(10000.0) / HEAD_DIM))
    angles = offset.astype(jnp.float32)[:, None] * frequency[None, :]
    broad_shape = (angles.shape[0],) + (1,) * (values_in.ndim - 2) + (half_dim,)
    cosine = jnp.cos(angles).reshape(broad_shape)
    sine = jnp.sin(angles).reshape(broad_shape)
    paired = values_in.reshape(values_in.shape[:-1] + (half_dim, 2))
    even_part = paired[..., 0]
    odd_part = paired[..., 1]
    turned = jnp.stack([even_part * cosine - odd_part * sine, even_part * sine + odd_part * cosine], axis=-1)
    return turned.reshape(values_in.shape)

def layer_norm(rows, gain, bias):
    centred = rows - lax.optimization_barrier(jnp.mean(rows, -1, keepdims=True))
    return centred * lax.rsqrt(lax.optimization_barrier(jnp.mean(centred * centred, -1, keepdims=True)) + 1e-05) * gain + bias

def bucket_forward(params, rows_in, lengths):
    in_w, out_w, up_w, down_w, small_now = params
    clip_of, offset = clip_layout(lengths)
    enter1 = low(layer_norm(rows_in, small_now[0], small_now[1]))
    projected = low_back(jnp.dot(enter1, in_w.reshape(D, -1), precision=highest))
    projected = projected.reshape(LEN, HEADS, 3, HEAD_DIM)
    queries = low(rotate(projected[:, :, 0], offset))
    keys_rot = low(rotate(projected[:, :, 1], offset))
    values = low(projected[:, :, 2])
    raw = low_back(jnp.einsum('qhd,khd->hqk', queries, keys_rot, precision=highest))
    scores = jnp.where(allowed_pairs(clip_of)[None], raw * HEAD_DIM ** (-0.5), -1e+30)
    top_score = lax.optimization_barrier(jnp.max(scores, -1, keepdims=True))
    expd = jnp.exp(scores - top_score)
    attn = expd / lax.optimization_barrier(jnp.sum(expd, -1, keepdims=True))
    mixed = low(low_back(jnp.einsum('hqk,khd->qhd', low(attn), values, precision=highest)))
    branch = low_back(jnp.dot(mixed.reshape(LEN, D), out_w.reshape(D, D), precision=highest))
    y_first = rows_in + small_now[4] * branch
    enter2 = low(layer_norm(y_first, small_now[2], small_now[3]))
    upval = low_back(jnp.dot(enter2, up_w, precision=highest))
    act = low(jax.nn.gelu(upval, approximate=False))
    mlp = low_back(jnp.dot(act, down_w, precision=highest))
    return y_first + small_now[5] * mlp

def lamb(weight, gradient, first, second, sum_axes):
    first = beta_first * first + (1.0 - beta_first) * gradient
    second = beta_second * second + (1.0 - beta_second) * gradient * gradient
    update = first / (1.0 - beta_first ** STEP) / (jnp.sqrt(second / (1.0 - beta_second ** STEP)) + adam_eps) + decay_rate * weight
    weight_sq = lax.optimization_barrier(jnp.sum(weight * weight, axis=sum_axes, keepdims=True))
    update_sq = lax.optimization_barrier(jnp.sum(update * update, axis=sum_axes, keepdims=True))
    new = weight - learn_rate * jnp.sqrt(weight_sq) * lax.rsqrt(update_sq + 1e-12) * update
    return (new, first, second, jnp.sqrt(weight_sq).reshape(-1), jnp.sqrt(update_sq).reshape(-1))

def reference(frames, cotangent, clip_lengths, in_proj, out_proj, up_proj, down_proj, small_params, in_first, in_second, out_first, out_second, up_first, up_second, down_first, down_second, small_first, small_second):
    bucket_count = MICRO * BUCKETS
    inputs = frames.astype(jnp.float32).reshape(bucket_count, LEN, D)
    lengths = clip_lengths.reshape(bucket_count, CLIPS)

    def forward(inputs, weights):
        rounded = tuple((low(w) for w in weights[:4])) + (weights[4],)

        def one_bucket(bucket_pair):
            return bucket_forward(rounded, bucket_pair[0], bucket_pair[1])
        return lax.map(jax.checkpoint(one_bucket), (inputs, lengths))
    weights = (in_proj, out_proj, up_proj, down_proj, small_params)
    result, pullback = jax.vjp(forward, inputs, weights)
    clip_of = jax.vmap(lambda length_row: clip_layout(length_row)[0])(lengths)
    valid_rows = (clip_of < CLIPS - 1).astype(jnp.float32)
    cotangent_rows = cotangent.astype(jnp.float32).reshape(bucket_count, LEN, D) * valid_rows[:, :, None]
    grad_inputs, grads = pullback(cotangent_rows)
    block_out = result.reshape(MICRO, ROWS, D).astype(jnp.bfloat16)
    input_grad = grad_inputs.reshape(MICRO, ROWS, D).astype(jnp.bfloat16)
    in_res = lamb(in_proj, grads[0], in_first, in_second, None)
    out_res = lamb(out_proj, grads[1], out_first, out_second, None)
    up_res = lamb(up_proj, grads[2], up_first, up_second, None)
    down_res = lamb(down_proj, grads[3], down_first, down_second, None)
    small_res = lamb(small_params, grads[4], small_first, small_second, (1,))
    weight_norms = jnp.concatenate([in_res[3], out_res[3], up_res[3], down_res[3], small_res[3]])
    update_norms = jnp.concatenate([in_res[4], out_res[4], up_res[4], down_res[4], small_res[4]])
    norms = jnp.stack([weight_norms, update_norms])
    return (block_out, input_grad, in_res[0], in_res[1], in_res[2], in_res[0].astype(jnp.bfloat16), out_res[0], out_res[1], out_res[2], out_res[0].astype(jnp.bfloat16), up_res[0], up_res[1], up_res[2], up_res[0].astype(jnp.bfloat16), down_res[0], down_res[1], down_res[2], down_res[0].astype(jnp.bfloat16), grads[4], small_res[0], small_res[1], small_res[2], norms)
```

```python
import functools
import math

import jax
import jax.numpy as jnp
from jax import lax
from jax.experimental import pallas as pl
from jax.experimental.pallas import tpu as pltpu
from jax.sharding import PartitionSpec as P

D = 512
HEADS = 8
HEAD_DIM = 64
FF = 2048
PAIRS = HEADS // 2
WINDOW = 250
LEN = 1024
CLIPS = 4
MICRO = 2
STEP = 3

BQ = 256
MLP_ROWS = 256
VMEM_LIMIT = 62 * 1024 * 1024

beta_first = 0.5
beta_second = 0.5
adam_eps = 1e-06
decay_rate = 0.01
learn_rate = 0.3

NT = (((1,), (1,)), ((), ()))
NN = (((1,), (0,)), ((), ()))
TN = (((0,), (0,)), ((), ()))


def dot(a, b, dims=NN):
    return lax.dot_general(a, b, dims, preferred_element_type=jnp.float32)


def norm_parts(rows):
    mean = jnp.mean(rows, -1, keepdims=True)
    centred = rows - mean
    inverse = lax.rsqrt(jnp.mean(centred * centred, -1, keepdims=True) + 1e-05)
    return centred * inverse, inverse


def norm_back(scaled, normal, inverse):
    return inverse * (
        scaled
        - jnp.mean(scaled, -1, keepdims=True)
        - normal * jnp.mean(scaled * normal, -1, keepdims=True)
    )


def lane_ids(shape):
    return lax.broadcasted_iota(jnp.int32, shape, len(shape) - 1)


def swap_pairs(rows):
    even = (lane_ids(rows.shape) & 1) == 0
    return jnp.where(even, pltpu.roll(rows, 127, 1), pltpu.roll(rows, 1, 1))


def run_starts(lengths_ref, bucket, position):
    end0 = lengths_ref[bucket, 0]
    end1 = end0 + lengths_ref[bucket, 1]
    end2 = end1 + lengths_ref[bucket, 2]
    start = jnp.where(position >= end0, end0, 0)
    start = jnp.where(position >= end1, end1, start)
    return jnp.where(position >= end2, end2, start), position < end2


def block_bias(lengths_ref, bucket, first_row, first_key, keys):
    position = first_row + lax.broadcasted_iota(jnp.int32, (BQ, 1), 0)
    start, _ = run_starts(lengths_ref, bucket, position)
    lowest = jnp.maximum(start, position - (WINDOW - 1))
    key = first_key + lax.broadcasted_iota(jnp.int32, (BQ, keys), 1)
    return jnp.where((key >= lowest) & (key <= position), 0.0, -1e30)


def head_lanes(tile, head):
    return jnp.where((lane_ids(tile.shape) // HEAD_DIM) == head, tile, jnp.zeros_like(tile))


def forward_kernel(lengths_ref, x_ref, small_ref, cos_ref, sin_ref, in_ref, qkv_ref, mixed_ref, total_ref, enter_ref):
    bucket = pl.program_id(0)

    def project(chunk, carry):
        rows = pl.ds(pl.multiple_of(chunk * BQ, BQ), BQ)
        normal, _ = norm_parts(x_ref[0, rows, :].astype(jnp.float32))
        enter = (normal * small_ref[0:1, :] + small_ref[1:2, :]).astype(jnp.bfloat16)
        enter_ref[0, rows, :] = enter
        cosine = cos_ref[0, rows, :]
        sine = sin_ref[0, rows, :]
        for pair in range(PAIRS):
            part = dot(enter, in_ref[:, pair * 384 : pair * 384 + 384])
            for which in range(2):
                piece = part[:, which * 128 : which * 128 + 128]
                turned = piece * cosine + swap_pairs(piece) * sine
                if which == 0:
                    turned = turned * (HEAD_DIM**-0.5)
                qkv_ref[0, rows, pair * 384 + which * 128 : pair * 384 + which * 128 + 128] = turned.astype(jnp.bfloat16)
            qkv_ref[0, rows, pair * 384 + 256 : pair * 384 + 384] = part[:, 256:].astype(jnp.bfloat16)
        return carry

    lax.fori_loop(0, LEN // BQ, project, 0)

    def attend(first_row, first_key, keys):
        rows = pl.ds(first_row, BQ)
        key_rows = pl.ds(first_key, keys)
        bias = block_bias(lengths_ref, bucket, first_row, first_key, keys)
        for pair in range(PAIRS):
            base = pair * 384
            queries = qkv_ref[0, rows, base : base + 128]
            keys_rot = qkv_ref[0, key_rows, base + 128 : base + 256]
            values = qkv_ref[0, key_rows, base + 256 : base + 384]
            outs = []
            totals = []
            for head in range(2):
                scores = dot(head_lanes(queries, head), keys_rot, NT) + bias
                top = jnp.max(scores, -1, keepdims=True)
                powers = jnp.exp(scores - top)
                total = jnp.sum(powers, -1, keepdims=True)
                outs.append(dot(powers.astype(jnp.bfloat16), values) / total)
                totals.append(jnp.broadcast_to(top + jnp.log(total), (BQ, 128)))
            low = lane_ids((BQ, 128)) < HEAD_DIM
            mixed_ref[0, rows, pair * 128 : pair * 128 + 128] = jnp.where(low, outs[0], outs[1]).astype(jnp.bfloat16)
            total_ref[0, rows, pair * 128 : pair * 128 + 128] = jnp.where(low, totals[0], totals[1])

    attend(0, 0, BQ)

    def later(step, carry):
        first_row = pl.multiple_of(step * BQ, BQ)
        attend(first_row, pl.multiple_of(first_row - BQ, BQ), 2 * BQ)
        return carry

    lax.fori_loop(1, LEN // BQ, later, 0)


def mlp_kernel(
    lengths_ref, x_ref, cot_ref, mixed_ref, small_ref, out_ref, up_ref, down_ref,
    block_ref, act_ref, gup_ref, gmlp_ref, enter_ref, gy1_ref, gbranch_ref, gmixed_ref, sums_ref,
):
    bucket = pl.program_id(0)
    chunk = pl.program_id(1)

    @pl.when((bucket == 0) & (chunk == 0))
    def _():
        sums_ref[...] = jnp.zeros_like(sums_ref)

    small = [small_ref[row : row + 1, :] for row in range(6)]
    x = x_ref[0].astype(jnp.float32)
    branch = dot(mixed_ref[0], out_ref[...], NT)
    y_first = x + small[4] * branch
    normal, inverse = norm_parts(y_first)
    enter = (normal * small[2] + small[3]).astype(jnp.bfloat16)
    enter_ref[0] = enter
    position = chunk * MLP_ROWS + lax.broadcasted_iota(jnp.int32, (MLP_ROWS, 1), 0)
    _, valid = run_starts(lengths_ref, bucket, position)
    grad_y = jnp.where(valid, cot_ref[0].astype(jnp.float32), 0.0)
    grad_mlp = (small[5] * grad_y).astype(jnp.bfloat16)
    gmlp_ref[0] = grad_mlp
    mlp = jnp.zeros((MLP_ROWS, D), jnp.float32)
    grad_enter = jnp.zeros((MLP_ROWS, D), jnp.float32)
    for part in range(FF // 512):
        cols = slice(part * 512, part * 512 + 512)
        upval = dot(enter, up_ref[:, cols])
        grad_act = dot(grad_mlp, down_ref[:, cols])
        cumulative = 0.5 + 0.5 * lax.erf(upval * (1.0 / math.sqrt(2.0)))
        act = (upval * cumulative).astype(jnp.bfloat16)
        act_ref[0, :, cols] = act
        density = jnp.exp(-0.5 * upval * upval) * (1.0 / math.sqrt(2.0 * math.pi))
        grad_up = (grad_act * (cumulative + upval * density)).astype(jnp.bfloat16)
        gup_ref[0, :, cols] = grad_up
        mlp = mlp + dot(act, down_ref[:, cols], NT)
        grad_enter = grad_enter + dot(grad_up, up_ref[:, cols], NT)
    block_ref[0] = (y_first + small[5] * mlp).astype(jnp.bfloat16)
    grad_y_first = grad_y + norm_back(grad_enter * small[2], normal, inverse)
    gy1_ref[0] = grad_y_first
    grad_branch = (small[4] * grad_y_first).astype(jnp.bfloat16)
    gbranch_ref[0] = grad_branch
    gmixed_ref[0] = dot(grad_branch, out_ref[...]).astype(jnp.bfloat16)

    def fold(terms):
        return jnp.sum(terms.reshape(MLP_ROWS // 8, 8, D), 0)

    sums_ref[0] += fold(grad_enter * normal)
    sums_ref[1] += fold(grad_enter)
    sums_ref[2] += fold(grad_y_first * branch)
    sums_ref[3] += fold(grad_y * mlp)


def backward_kernel(lengths_ref, qkv_ref, mixed_ref, gmixed_ref, total_ref, cos_ref, sin_ref, gproj_ref, dk_ref, dv_ref):
    bucket = pl.program_id(0)

    def attend(first_row, first_key, keys):
        rows = pl.ds(first_row, BQ)
        key_rows = pl.ds(first_key, keys)
        bias = block_bias(lengths_ref, bucket, first_row, first_key, keys)
        low = lane_ids((BQ, 128)) < HEAD_DIM
        for pair in range(PAIRS):
            base = pair * 384
            queries = qkv_ref[0, rows, base : base + 128]
            keys_rot = qkv_ref[0, key_rows, base + 128 : base + 256]
            values = qkv_ref[0, key_rows, base + 256 : base + 384]
            grad = gmixed_ref[0, rows, pair * 128 : pair * 128 + 128]
            totals = total_ref[0, rows, pair * 128 : pair * 128 + 128]
            product = grad.astype(jnp.float32) * mixed_ref[0, rows, pair * 128 : pair * 128 + 128].astype(jnp.float32)
            grad_q = jnp.zeros((BQ, 128), jnp.float32)
            grad_k = jnp.zeros((keys, 128), jnp.float32)
            grad_v = jnp.zeros((keys, 128), jnp.float32)
            for head in range(2):
                query = head_lanes(queries, head)
                grad_head = head_lanes(grad, head)
                inner = jnp.sum(jnp.where(low == (head == 0), product, 0.0), -1, keepdims=True)
                total = totals[:, head * HEAD_DIM : head * HEAD_DIM + 1]
                attn = jnp.exp(dot(query, keys_rot, NT) + bias - total)
                grad_attn = dot(grad_head, values, NT)
                grad_scores = (attn * (grad_attn - inner)).astype(jnp.bfloat16)
                grad_v = grad_v + dot(attn.astype(jnp.bfloat16), grad_head, TN)
                grad_k = grad_k + dot(grad_scores, query, TN)
                grad_q = grad_q + dot(grad_scores, head_lanes(keys_rot, head))
            cosine = cos_ref[0, rows, :]
            sine = sin_ref[0, rows, :]
            grad_q = grad_q * (HEAD_DIM**-0.5)
            gproj_ref[0, rows, base : base + 128] = (grad_q * cosine - swap_pairs(grad_q) * sine).astype(jnp.bfloat16)
            lanes = slice(pair * 128, pair * 128 + 128)
            if keys > BQ:
                before = pl.ds(first_key, BQ)
                dk_ref[before, lanes] += grad_k[:BQ]
                dv_ref[before, lanes] += grad_v[:BQ]
                dk_ref[rows, lanes] = grad_k[BQ:]
                dv_ref[rows, lanes] = grad_v[BQ:]
            else:
                dk_ref[rows, lanes] = grad_k
                dv_ref[rows, lanes] = grad_v

    attend(0, 0, BQ)

    def later(step, carry):
        first_row = pl.multiple_of(step * BQ, BQ)
        attend(first_row, pl.multiple_of(first_row - BQ, BQ), 2 * BQ)
        return carry

    lax.fori_loop(1, LEN // BQ, later, 0)

    def finish(chunk, carry):
        rows = pl.ds(pl.multiple_of(chunk * BQ, BQ), BQ)
        cosine = cos_ref[0, rows, :]
        sine = sin_ref[0, rows, :]
        for pair in range(PAIRS):
            grad_k = dk_ref[rows, pair * 128 : pair * 128 + 128]
            turned = grad_k * cosine - swap_pairs(grad_k) * sine
            gproj_ref[0, rows, pair * 384 + 128 : pair * 384 + 256] = turned.astype(jnp.bfloat16)
            gproj_ref[0, rows, pair * 384 + 256 : pair * 384 + 384] = dv_ref[rows, pair * 128 : pair * 128 + 128].astype(jnp.bfloat16)
        return carry

    lax.fori_loop(0, LEN // BQ, finish, 0)


def whole(shape):
    return pl.BlockSpec(shape, lambda *ids: (0,) * len(shape))


def per_bucket(*shape):
    return pl.BlockSpec((1,) + shape, lambda b: (b, 0, 0))


def bf16(*shape):
    return jax.ShapeDtypeStruct(shape, jnp.bfloat16)


def f32(*shape):
    return jax.ShapeDtypeStruct(shape, jnp.float32)


SCALARS = pl.BlockSpec(memory_space=pltpu.SMEM)


def params(count):
    return pltpu.CompilerParams(dimension_semantics=("arbitrary",) * count, vmem_limit_bytes=VMEM_LIMIT)


def turn_tables(lengths):
    ends = jnp.cumsum(lengths, axis=1)
    position = jnp.arange(LEN, dtype=jnp.int32)
    passed = position[None, :, None] >= ends[:, None, : CLIPS - 1]
    start = jnp.max(jnp.where(passed, ends[:, None, : CLIPS - 1], 0), axis=2)
    offset = (position[None, :] - start).astype(jnp.float32)
    frequency = jnp.exp(jnp.arange(HEAD_DIM // 2, dtype=jnp.float32) * (-2.0 * math.log(10000.0) / HEAD_DIM))
    angles = offset[:, :, None] * frequency
    cosine = jnp.repeat(jnp.cos(angles), 2, axis=-1)
    sine = jnp.sin(angles)
    sine = jnp.stack([-sine, sine], axis=-1).reshape(cosine.shape)
    return jnp.concatenate([cosine, cosine], -1), jnp.concatenate([sine, sine], -1)


def attention_forward(lengths, x, small, cosine, sine, in_mat):
    count = x.shape[0]
    return pl.pallas_call(
        forward_kernel,
        grid=(count,),
        in_specs=[SCALARS, per_bucket(LEN, D), whole((6, D)), per_bucket(LEN, 128), per_bucket(LEN, 128), whole((D, 3 * D))],
        out_specs=[per_bucket(LEN, 3 * D), per_bucket(LEN, D), per_bucket(LEN, D), per_bucket(LEN, D)],
        out_shape=[bf16(count, LEN, 3 * D), bf16(count, LEN, D), f32(count, LEN, D), bf16(count, LEN, D)],
        compiler_params=params(1),
        name="attention_forward",
    )(lengths, x, small, cosine, sine, in_mat)


def mlp_both(lengths, x, cot, mixed, small, out_mat, up_mat, down_mat):
    count = x.shape[0]

    def chunked(width):
        return pl.BlockSpec((1, MLP_ROWS, width), lambda b, i: (b, i, 0))

    return pl.pallas_call(
        mlp_kernel,
        grid=(count, LEN // MLP_ROWS),
        in_specs=[SCALARS, chunked(D), chunked(D), chunked(D), whole((6, D)), whole((D, D)), whole((D, FF)), whole((D, FF))],
        out_specs=[chunked(D), chunked(FF), chunked(FF), chunked(D), chunked(D), chunked(D), chunked(D), chunked(D), whole((4, 8, D))],
        out_shape=[
            bf16(count, LEN, D), bf16(count, LEN, FF), bf16(count, LEN, FF), bf16(count, LEN, D), bf16(count, LEN, D),
            f32(count, LEN, D), bf16(count, LEN, D), bf16(count, LEN, D), f32(4, 8, D),
        ],
        compiler_params=params(2),
        name="mlp_both",
    )(lengths, x, cot, mixed, small, out_mat, up_mat, down_mat)


def attention_backward(lengths, qkv, mixed, gmixed, totals, cosine, sine):
    count = qkv.shape[0]
    return pl.pallas_call(
        backward_kernel,
        grid=(count,),
        in_specs=[SCALARS, per_bucket(LEN, 3 * D), per_bucket(LEN, D), per_bucket(LEN, D), per_bucket(LEN, D), per_bucket(LEN, 128), per_bucket(LEN, 128)],
        out_specs=per_bucket(LEN, 3 * D),
        out_shape=bf16(count, LEN, 3 * D),
        scratch_shapes=[pltpu.VMEM((LEN, D), jnp.float32), pltpu.VMEM((LEN, D), jnp.float32)],
        compiler_params=params(1),
        name="attention_backward",
    )(lengths, qkv, mixed, gmixed, totals, cosine, sine)


def on_device(
    frames, cotangent, clip_lengths, in_proj, out_proj, up_proj, down_proj, small_params,
    in_first, in_second, out_first, out_second, up_first, up_second, down_first, down_second,
    small_first, small_second,
):
    rows_here = frames.shape[1]
    own_buckets = rows_here // LEN
    first_bucket = lax.axis_index("tensor") * own_buckets
    lengths = lax.dynamic_slice_in_dim(clip_lengths, first_bucket, own_buckets, 1).reshape(-1, CLIPS)
    count = MICRO * own_buckets
    x = frames.reshape(count, LEN, D)
    cot = cotangent.reshape(count, LEN, D)
    tensor_size = lax.axis_size("tensor")
    dp_size = lax.axis_size("dp")
    depth = in_proj.shape[0]
    heads_here = in_proj.shape[1]
    ff_here = up_proj.shape[1]

    def column_major(out_like, down_like):
        return out_like.reshape(heads_here * HEAD_DIM, depth).T, down_like.T

    out_cols, down_cols = column_major(out_proj, down_proj)
    shard = jnp.concatenate([in_proj.reshape(depth, -1), out_cols, up_proj, down_cols], axis=1).astype(jnp.bfloat16)
    gathered = lax.all_gather(shard, ("dp", "tensor"), axis=0)
    gathered = gathered.reshape(dp_size, tensor_size, depth, shard.shape[1])
    gathered = jnp.moveaxis(gathered, 1, 2).reshape(D, tensor_size, shard.shape[1])
    edge0 = heads_here * 192
    edge1 = edge0 + heads_here * HEAD_DIM
    edge2 = edge1 + ff_here
    in_mat = gathered[:, :, :edge0].reshape(D, PAIRS, 2, 3, HEAD_DIM).transpose(0, 1, 3, 2, 4).reshape(D, 3 * D)
    out_mat = gathered[:, :, edge0:edge1].reshape(D, D)
    up_mat = gathered[:, :, edge1:edge2].reshape(D, FF)
    down_mat = gathered[:, :, edge2:].reshape(D, FF)

    cosine, sine = turn_tables(lengths)
    qkv, mixed, totals, enter1 = attention_forward(lengths, x, small_params, cosine, sine, in_mat)
    block_out, act, grad_up, grad_mlp, enter2, grad_y_first, grad_branch, grad_mixed, sums = mlp_both(
        lengths, x, cot, mixed, small_params, out_mat, up_mat, down_mat
    )

    def weight_grad(left, right):
        return dot(left.reshape(-1, left.shape[-1]), right.reshape(-1, right.shape[-1]), TN).astype(jnp.bfloat16)

    grad_down = weight_grad(grad_mlp, act)
    grad_upw = weight_grad(enter2, grad_up)
    grad_out = weight_grad(grad_branch, mixed)
    grad_proj = attention_backward(lengths, qkv, mixed, grad_mixed, totals, cosine, sine)
    grad_in = weight_grad(enter1, grad_proj)
    grad_in = grad_in.reshape(D, PAIRS, 3, 2, HEAD_DIM).transpose(0, 1, 3, 2, 4)

    def by_owner(mat):
        return jnp.moveaxis(mat.reshape(dp_size, depth, tensor_size, -1), 2, 1)

    stacked = jnp.concatenate([by_owner(grad_in), by_owner(grad_out), by_owner(grad_upw), by_owner(grad_down)], axis=-1)
    owned = lax.psum_scatter(
        stacked.reshape(dp_size * tensor_size, depth, -1), ("dp", "tensor"), scatter_dimension=0, tiled=False
    ).astype(jnp.float32)

    grad_enter1 = dot(grad_proj.reshape(-1, 3 * D), in_mat, NT).reshape(count, LEN, D)
    normal1, inverse1 = norm_parts(x.astype(jnp.float32))
    input_grad = (grad_y_first + norm_back(grad_enter1 * small_params[0], normal1, inverse1)).astype(jnp.bfloat16)
    late = jnp.sum(sums, axis=1)
    small_terms = jnp.stack(
        [jnp.sum(grad_enter1 * normal1, (0, 1)), jnp.sum(grad_enter1, (0, 1)), late[0], late[1], late[2], late[3]]
    )

    grads = (
        owned[:, :edge0].reshape(in_proj.shape),
        owned[:, edge0:edge1].T.reshape(out_proj.shape),
        owned[:, edge1:edge2],
        owned[:, edge2:].T,
    )
    weights_in = (in_proj, out_proj, up_proj, down_proj)
    firsts = (in_first, out_first, up_first, down_first)
    seconds = (in_second, out_second, up_second, down_second)
    own_squares = jnp.stack([jnp.sum(weight * weight) for weight in weights_in])
    small_grad, weight_squares = lax.psum((small_terms, own_squares), ("dp", "tensor"))
    new_firsts = []
    new_seconds = []
    updates = []
    for weight, gradient, first, second in zip(weights_in, grads, firsts, seconds):
        first = beta_first * first + (1.0 - beta_first) * gradient
        second = beta_second * second + (1.0 - beta_second) * gradient * gradient
        update = (
            first / (1.0 - beta_first**STEP) / (jnp.sqrt(second / (1.0 - beta_second**STEP)) + adam_eps)
            + decay_rate * weight
        )
        new_firsts.append(first)
        new_seconds.append(second)
        updates.append(update)
    update_squares = lax.psum(jnp.stack([jnp.sum(update * update) for update in updates]), ("dp", "tensor"))
    trust_ratio = jnp.sqrt(weight_squares) * lax.rsqrt(update_squares + 1e-12)
    new_weights = [weights_in[index] - learn_rate * trust_ratio[index] * updates[index] for index in range(4)]
    small_first_new = beta_first * small_first + (1.0 - beta_first) * small_grad
    small_second_new = beta_second * small_second + (1.0 - beta_second) * small_grad * small_grad
    small_update = (
        small_first_new / (1.0 - beta_first**STEP) / (jnp.sqrt(small_second_new / (1.0 - beta_second**STEP)) + adam_eps)
        + decay_rate * small_params
    )
    small_weight_sq = jnp.sum(small_params * small_params, axis=1, keepdims=True)
    small_update_sq = jnp.sum(small_update * small_update, axis=1, keepdims=True)
    small_new = small_params - learn_rate * jnp.sqrt(small_weight_sq) * lax.rsqrt(small_update_sq + 1e-12) * small_update
    norms = jnp.stack(
        [
            jnp.concatenate([jnp.sqrt(weight_squares), jnp.sqrt(small_weight_sq).reshape(-1)]),
            jnp.concatenate([jnp.sqrt(update_squares), jnp.sqrt(small_update_sq).reshape(-1)]),
        ]
    )
    outputs = [block_out.reshape(frames.shape), input_grad.reshape(frames.shape)]
    for new, first, second in zip(new_weights, new_firsts, new_seconds):
        outputs += [new, first, second, new.astype(jnp.bfloat16)]
    return tuple(outputs + [small_grad, small_new, small_first_new, small_second_new, norms])


def solution(mesh):
    rows = P(None, ("dp", "tensor"), None)
    in_spec = P("dp", "tensor", None)
    out_spec = P("tensor", None, "dp")
    up_spec = P("dp", "tensor")
    down_spec = P("tensor", "dp")
    return jax.shard_map(
        on_device,
        mesh=mesh,
        in_specs=(
            rows, rows, P(None, "dp", None), in_spec, out_spec, up_spec, down_spec, P(),
            in_spec, in_spec, out_spec, out_spec, up_spec, up_spec, down_spec, down_spec, P(), P(),
        ),
        out_specs=(rows, rows) + (in_spec,) * 4 + (out_spec,) * 4 + (up_spec,) * 4 + (down_spec,) * 4 + (P(),) * 5,
        check_vma=False,
    )
```

```python
import functools
import math

import jax
import jax.numpy as jnp
from jax import lax
from jax.experimental import pallas as pl
from jax.experimental.pallas import tpu as pltpu
from jax.sharding import PartitionSpec as P

D = 512
HEADS = 8
HEAD_DIM = 64
FF = 2048
PAIRS = HEADS // 2
WINDOW = 250
LEN = 1024
CLIPS = 4
MICRO = 2
STEP = 3

BQ = 256
MLP_ROWS = 256
VMEM_LIMIT = 62 * 1024 * 1024

beta_first = 0.5
beta_second = 0.5
adam_eps = 1e-06
decay_rate = 0.01
learn_rate = 0.3

NT = (((1,), (1,)), ((), ()))
NN = (((1,), (0,)), ((), ()))
TN = (((0,), (0,)), ((), ()))


def dot(a, b, dims=NN):
    return lax.dot_general(a, b, dims, preferred_element_type=jnp.float32)


def norm_parts(rows):
    mean = jnp.mean(rows, -1, keepdims=True)
    centred = rows - mean
    inverse = lax.rsqrt(jnp.mean(centred * centred, -1, keepdims=True) + 1e-05)
    return centred * inverse, inverse


def norm_back(scaled, normal, inverse):
    return inverse * (
        scaled
        - jnp.mean(scaled, -1, keepdims=True)
        - normal * jnp.mean(scaled * normal, -1, keepdims=True)
    )


def lane_ids(shape):
    return lax.broadcasted_iota(jnp.int32, shape, len(shape) - 1)


def swap_pairs(rows):
    even = (lane_ids(rows.shape) & 1) == 0
    return jnp.where(even, pltpu.roll(rows, 127, 1), pltpu.roll(rows, 1, 1))


def run_starts(lengths_ref, bucket, position):
    end0 = lengths_ref[bucket, 0]
    end1 = end0 + lengths_ref[bucket, 1]
    end2 = end1 + lengths_ref[bucket, 2]
    start = jnp.where(position >= end0, end0, 0)
    start = jnp.where(position >= end1, end1, start)
    return jnp.where(position >= end2, end2, start), position < end2


def block_bias(lengths_ref, bucket, first_row, first_key, keys):
    position = first_row + lax.broadcasted_iota(jnp.int32, (BQ, 1), 0)
    start, _ = run_starts(lengths_ref, bucket, position)
    lowest = jnp.maximum(start, position - (WINDOW - 1))
    key = first_key + lax.broadcasted_iota(jnp.int32, (BQ, keys), 1)
    return jnp.where((key >= lowest) & (key <= position), 0.0, -1e30)


def head_lanes(tile, head):
    return jnp.where((lane_ids(tile.shape) // HEAD_DIM) == head, tile, jnp.zeros_like(tile))


MESH = pl.DeviceIdType.MESH
HERE_DP = 8
HERE_TENSOR = 4
IN_W, OUT_W, FF_W = 384, 128, 512
SHARD_W = IN_W + OUT_W + 2 * FF_W
CORE, ALONG_Y, ALONG_X = "core", "y", "x"

GATHERED = (
    (0, 0, 32, IN_W, 0, "xy"),
    (0, 32, 32, IN_W, 0, "yx"),
    (1, 0, 64, OUT_W, IN_W, "xy"),
    (2, 0, 64, FF_W, IN_W + OUT_W, "xy"),
    (3, 0, 64, FF_W, IN_W + OUT_W + FF_W, "yx"),
)
SUMMED = (
    (1, 0, 64, OUT_W, "yx"),
    (2, 0, 64, FF_W, "yx"),
    (3, 0, 64, FF_W, "xy"),
    (0, 0, 32, IN_W, "xy"),
    (0, 32, 32, IN_W, "yx"),
)


class Place:
    def __init__(self):
        dp = lax.axis_index("dp")
        tensor = lax.axis_index("tensor")
        self.z, self.x = dp // 2, dp % 2
        self.y, self.c = tensor // 2, tensor % 2

    def device(self, dz=0, x=None, y=None, c=None):
        x = self.x if x is None else x
        y = self.y if y is None else y
        c = self.c if c is None else c
        return {"dp": (self.z + dz) % 4 * 2 + x, "tensor": y * 2 + c}

    def peers(self):
        return {
            CORE: self.device(c=1 - self.c),
            ALONG_Y: self.device(y=1 - self.y),
            ALONG_X: self.device(x=1 - self.x),
            1: self.device(dz=1),
            2: self.device(dz=2),
            3: self.device(dz=3),
        }


def tile_cols(tensor, width):
    return pl.ds(pl.multiple_of(tensor * width, 128), width)


def remote(source, target, send, recv, device):
    return pltpu.make_async_remote_copy(
        src_ref=source, dst_ref=target, send_sem=send, recv_sem=recv, device_id=device, device_id_type=MESH
    )


def meet(place):
    barrier = pltpu.get_barrier_semaphore()
    peers = place.peers()
    for device in peers.values():
        pl.semaphore_signal(barrier, inc=1, device_id=device, device_id_type=MESH)
    pl.semaphore_wait(barrier, len(peers))


def start_all(copies):
    for copy in copies:
        copy.start()


def arrive_all(copies):
    for copy in copies:
        copy.wait_recv()


def sent_all(copies):
    for copy in copies:
        copy.wait_send()


def gather_copies(index, stage, place, shard, weights, send, recv):
    weight, row, count, width, offset, order = GATHERED[index]
    full = weights[weight]
    rows = pl.ds(row, count)
    peers = place.peers()

    def copy(source, target, slot, peer):
        return remote(source, target, send.at[index, slot], recv.at[index, slot], peers[peer])

    def cols(y):
        return tile_cols(y * 2 + place.c, width)

    mine = cols(place.y)
    if stage == 0:
        return [
            copy(shard.at[rows, offset : offset + width], full.at[place.z, place.x, rows, mine], step - 1, step)
            for step in (1, 2, 3)
        ]
    if stage == 3:
        parts = [full.at[:, :, rows, cols(y)] for y in range(2)]
        return [copy(part, part, 6 + y, CORE) for y, part in enumerate(parts)]
    if stage == 1:
        part = full.at[:, place.x, rows, mine]
        return [copy(part, part, 3, ALONG_X if order == "xy" else ALONG_Y)]
    if order == "xy":
        part = full.at[:, :, rows, mine]
        return [copy(part, part, 4, ALONG_Y)]
    parts = [full.at[:, place.x, rows, cols(y)] for y in range(2)]
    return [copy(part, part, 4 + y, ALONG_X) for y, part in enumerate(parts)]


def project_rows(rows, enter, cosine, sine, weight, qkv_ref):
    for pair in range(PAIRS):
        part = dot(enter, weight(pair))
        for which in range(2):
            piece = part[:, which * 128 : which * 128 + 128]
            turned = piece * cosine + swap_pairs(piece) * sine
            if which == 0:
                turned = turned * (HEAD_DIM**-0.5)
            qkv_ref[0, rows, pair * 384 + which * 128 : pair * 384 + which * 128 + 128] = turned.astype(jnp.bfloat16)
        qkv_ref[0, rows, pair * 384 + 256 : pair * 384 + 384] = part[:, 256:].astype(jnp.bfloat16)


def attend_forward(lengths_ref, bucket, first_row, first_key, keys, qkv_ref, mixed_ref, total_ref):
    rows = pl.ds(first_row, BQ)
    key_rows = pl.ds(first_key, keys)
    bias = block_bias(lengths_ref, bucket, first_row, first_key, keys)
    for pair in range(PAIRS):
        base = pair * 384
        queries = qkv_ref[0, rows, base : base + 128]
        keys_rot = qkv_ref[0, key_rows, base + 128 : base + 256]
        values = qkv_ref[0, key_rows, base + 256 : base + 384]
        outs = []
        totals = []
        for head in range(2):
            scores = dot(head_lanes(queries, head), keys_rot, NT) + bias
            top = jnp.max(scores, -1, keepdims=True)
            powers = jnp.exp(scores - top)
            total = jnp.sum(powers, -1, keepdims=True)
            outs.append(dot(powers.astype(jnp.bfloat16), values) / total)
            totals.append(jnp.broadcast_to(top + jnp.log(total), (BQ, 128)))
        low = lane_ids((BQ, 128)) < HEAD_DIM
        mixed_ref[0, rows, pair * 128 : pair * 128 + 128] = jnp.where(low, outs[0], outs[1]).astype(jnp.bfloat16)
        total_ref[0, rows, pair * 128 : pair * 128 + 128] = jnp.where(low, totals[0], totals[1])


def enter_rows(x_ref, small_ref, rows, bucket=0):
    normal, _ = norm_parts(x_ref[bucket, rows, :].astype(jnp.float32))
    return (normal * small_ref[0:1, :] + small_ref[1:2, :]).astype(jnp.bfloat16)


def chunk_rows(chunk):
    return pl.ds(pl.multiple_of(chunk * BQ, BQ), BQ)


def forward_kernel(
    lengths_ref, x_ref, small_ref, cos_ref, sin_ref, *refs, alone
):
    bucket = pl.program_id(0)
    if alone:
        in_ref, qkv_ref, mixed_ref, total_ref, enter_ref = refs
    else:
        shard_ref, qkv_ref, mixed_ref, total_ref = refs[:4]
        kept = refs[4:8]
        full = refs[8:12]
        enter_ref, send, recv, own_sem, keep_sem = refs[12:]
        place = Place()

        def copies(which, stage):
            found = []
            for index in which:
                found += gather_copies(index, stage, place, shard_ref, full, send, recv)
            return found

        def own_tiles():
            tiles = []
            for weight, width, offset in ((0, IN_W, 0), (1, OUT_W, IN_W), (2, FF_W, IN_W + OUT_W), (3, FF_W, IN_W + OUT_W + FF_W)):
                target = full[weight].at[place.z, place.x, :, tile_cols(place.y * 2 + place.c, width)]
                tiles.append(pltpu.make_async_copy(shard_ref.at[:, offset : offset + width], target, own_sem.at[weight]))
            return tiles

        def keeps():
            return [pltpu.make_async_copy(full[weight], kept[weight], keep_sem.at[weight]) for weight in range(4)]

        early, late = (0, 1), (2, 3, 4)

        @pl.when(bucket == 0)
        def _():
            meet(place)
            start_all(copies(early, 0))
            start_all(own_tiles())
            start_all(copies(late, 0))

    def normalise(chunk, carry):
        rows = chunk_rows(chunk)
        enter_ref[0, rows, :] = enter_rows(x_ref, small_ref, rows)
        return carry

    lax.fori_loop(0, LEN // BQ, normalise, 0)

    if not alone:

        @pl.when(bucket == 0)
        def _():
            for tile in own_tiles():
                tile.wait()
            for stage in range(3):
                arrive_all(copies(early, stage))
                start_all(copies(early, stage + 1))
            arrive_all(copies(early, 3))
            arrive_all(copies(late, 0))
            start_all(copies(late, 1))

        @pl.when(bucket == 1)
        def _():
            arrive_all(copies(late, 3))
            start_all(keeps())

    def weight(pair):
        cols = slice(pair * 384, pair * 384 + 384)
        return in_ref[:, cols] if alone else full[0][:, :, :, cols].reshape(D, 384)

    def project(chunk, carry):
        rows = chunk_rows(chunk)
        project_rows(rows, enter_ref[0, rows, :], cos_ref[0, rows, :], sin_ref[0, rows, :], weight, qkv_ref)
        return carry

    lax.fori_loop(0, LEN // BQ, project, 0)
    attend_forward(lengths_ref, bucket, 0, 0, BQ, qkv_ref, mixed_ref, total_ref)

    def later(step, carry):
        if not alone:

            @pl.when((bucket == 0) & (step == 1))
            def _():
                arrive_all(copies(late, 1))
                start_all(copies(late, 2))

            @pl.when((bucket == 0) & (step == 3))
            def _():
                arrive_all(copies(late, 2))
                start_all(copies(late, 3))

        first_row = pl.multiple_of(step * BQ, BQ)
        attend_forward(lengths_ref, bucket, first_row, pl.multiple_of(first_row - BQ, BQ), 2 * BQ, qkv_ref, mixed_ref, total_ref)
        return carry

    lax.fori_loop(1, LEN // BQ, later, 0)

    if not alone:

        @pl.when(bucket == 1)
        def _():
            for keep in keeps():
                keep.wait()
            for stage in range(4):
                sent_all(copies(early + late, stage))


def mlp_kernel(
    lengths_ref, x_ref, cot_ref, mixed_ref, small_ref, out_ref, up_ref, down_ref,
    block_ref, gy1_ref, gmixed_ref, sums_ref, gout_ref, gup_out_ref, gdown_ref,
    act_ref, gup_ref, keep_ref, enter_t, gmlp_t, gbranch_t,
):
    bucket = pl.program_id(0)
    chunk = pl.program_id(1)
    buckets = pl.num_programs(0)
    chunks = pl.num_programs(1)

    @pl.when((bucket == 0) & (chunk == 0))
    def _():
        sums_ref[...] = jnp.zeros_like(sums_ref)

    index = bucket * chunks + chunk
    rows = pl.ds(pl.multiple_of(index * MLP_ROWS, MLP_ROWS), MLP_ROWS)
    small = [small_ref[row : row + 1, :] for row in range(6)]
    x = x_ref[0].astype(jnp.float32)
    mixed = mixed_ref[0]
    keep_ref[rows, :] = mixed
    branch = dot(mixed, out_ref[...], NT)
    y_first = x + small[4] * branch
    normal, inverse = norm_parts(y_first)
    enter = (normal * small[2] + small[3]).astype(jnp.bfloat16)
    enter_t[:, rows] = enter.T
    position = chunk * MLP_ROWS + lax.broadcasted_iota(jnp.int32, (MLP_ROWS, 1), 0)
    _, valid = run_starts(lengths_ref, bucket, position)
    grad_y = jnp.where(valid, cot_ref[0].astype(jnp.float32), 0.0)
    grad_mlp = (small[5] * grad_y).astype(jnp.bfloat16)
    gmlp_t[:, rows] = grad_mlp.T
    mlp = jnp.zeros((MLP_ROWS, D), jnp.float32)
    grad_enter = jnp.zeros((MLP_ROWS, D), jnp.float32)
    for part in range(FF // 512):
        cols = slice(part * 512, part * 512 + 512)
        upval = dot(enter, up_ref[:, cols])
        grad_act = dot(grad_mlp, down_ref[:, cols])
        cumulative = 0.5 + 0.5 * lax.erf(upval * (1.0 / math.sqrt(2.0)))
        act = (upval * cumulative).astype(jnp.bfloat16)
        act_ref[rows, cols] = act
        density = jnp.exp(-0.5 * upval * upval) * (1.0 / math.sqrt(2.0 * math.pi))
        grad_up = (grad_act * (cumulative + upval * density)).astype(jnp.bfloat16)
        gup_ref[rows, cols] = grad_up
        mlp = mlp + dot(act, down_ref[:, cols], NT)
        grad_enter = grad_enter + dot(grad_up, up_ref[:, cols], NT)
    block_ref[0] = (y_first + small[5] * mlp).astype(jnp.bfloat16)
    grad_y_first = grad_y + norm_back(grad_enter * small[2], normal, inverse)
    gy1_ref[0] = grad_y_first
    grad_branch = (small[4] * grad_y_first).astype(jnp.bfloat16)
    gbranch_t[:, rows] = grad_branch.T
    gmixed_ref[0] = dot(grad_branch, out_ref[...]).astype(jnp.bfloat16)

    def fold(terms):
        return jnp.sum(terms.reshape(MLP_ROWS // 8, 8, D), 0)

    sums_ref[0] += fold(grad_enter * normal)
    sums_ref[1] += fold(grad_enter)
    sums_ref[2] += fold(grad_y_first * branch)
    sums_ref[3] += fold(grad_y * mlp)

    @pl.when(index == buckets * chunks - 1)
    def _():
        gout_ref[...] = dot(gbranch_t[...], keep_ref[...]).astype(jnp.bfloat16)

        def weight_grads(part, carry):
            cols = pl.ds(pl.multiple_of(part * 256, 256), 256)
            gup_out_ref[:, cols] = dot(enter_t[...], gup_ref[:, cols]).astype(jnp.bfloat16)
            gdown_ref[:, cols] = dot(gmlp_t[...], act_ref[:, cols]).astype(jnp.bfloat16)
            return carry

        lax.fori_loop(0, FF // 256, weight_grads, 0)


def attend_backward(
    lengths_ref, bucket, slot, first_row, first_key, keys, qkv_ref, mixed_ref, gmixed_ref, total_ref, cos_ref, sin_ref, gproj_ref, dk_ref, dv_ref
):
    rows = pl.ds(first_row, BQ)
    key_rows = pl.ds(first_key, keys)
    bias = block_bias(lengths_ref, bucket, first_row, first_key, keys)
    low = lane_ids((BQ, 128)) < HEAD_DIM
    for pair in range(PAIRS):
        base = pair * 384
        queries = qkv_ref[0, rows, base : base + 128]
        keys_rot = qkv_ref[0, key_rows, base + 128 : base + 256]
        values = qkv_ref[0, key_rows, base + 256 : base + 384]
        grad = gmixed_ref[0, rows, pair * 128 : pair * 128 + 128]
        totals = total_ref[0, rows, pair * 128 : pair * 128 + 128]
        product = grad.astype(jnp.float32) * mixed_ref[0, rows, pair * 128 : pair * 128 + 128].astype(jnp.float32)
        grad_q = jnp.zeros((BQ, 128), jnp.float32)
        grad_k = jnp.zeros((keys, 128), jnp.float32)
        grad_v = jnp.zeros((keys, 128), jnp.float32)
        for head in range(2):
            query = head_lanes(queries, head)
            grad_head = head_lanes(grad, head)
            inner = jnp.sum(jnp.where(low == (head == 0), product, 0.0), -1, keepdims=True)
            total = totals[:, head * HEAD_DIM : head * HEAD_DIM + 1]
            attn = jnp.exp(dot(query, keys_rot, NT) + bias - total)
            grad_attn = dot(grad_head, values, NT)
            grad_scores = (attn * (grad_attn - inner)).astype(jnp.bfloat16)
            grad_v = grad_v + dot(attn.astype(jnp.bfloat16), grad_head, TN)
            grad_k = grad_k + dot(grad_scores, query, TN)
            grad_q = grad_q + dot(grad_scores, head_lanes(keys_rot, head))
        cosine = cos_ref[0, rows, :]
        sine = sin_ref[0, rows, :]
        grad_q = grad_q * (HEAD_DIM**-0.5)
        gproj_ref[slot, rows, base : base + 128] = (grad_q * cosine - swap_pairs(grad_q) * sine).astype(jnp.bfloat16)
        lanes = slice(pair * 128, pair * 128 + 128)
        if keys > BQ:
            before = pl.ds(first_key, BQ)
            dk_ref[before, lanes] += grad_k[:BQ]
            dv_ref[before, lanes] += grad_v[:BQ]
            dk_ref[rows, lanes] = grad_k[BQ:]
            dv_ref[rows, lanes] = grad_v[BQ:]
        else:
            dk_ref[rows, lanes] = grad_k
            dv_ref[rows, lanes] = grad_v


def finish_keys(slot, cos_ref, sin_ref, gproj_ref, dk_ref, dv_ref):
    def finish(chunk, carry):
        rows = chunk_rows(chunk)
        cosine = cos_ref[0, rows, :]
        sine = sin_ref[0, rows, :]
        for pair in range(PAIRS):
            grad_k = dk_ref[rows, pair * 128 : pair * 128 + 128]
            turned = grad_k * cosine - swap_pairs(grad_k) * sine
            gproj_ref[slot, rows, pair * 384 + 128 : pair * 384 + 256] = turned.astype(jnp.bfloat16)
            gproj_ref[slot, rows, pair * 384 + 256 : pair * 384 + 384] = dv_ref[rows, pair * 128 : pair * 128 + 128].astype(jnp.bfloat16)
        return carry

    lax.fori_loop(0, LEN // BQ, finish, 0)


def backward_kernel(lengths_ref, qkv_ref, mixed_ref, gmixed_ref, total_ref, cos_ref, sin_ref, gproj_ref, dk_ref, dv_ref):
    bucket = pl.program_id(0)
    shared = (qkv_ref, mixed_ref, gmixed_ref, total_ref, cos_ref, sin_ref, gproj_ref, dk_ref, dv_ref)
    attend_backward(lengths_ref, bucket, 0, 0, 0, BQ, *shared)

    def later(step, carry):
        first_row = pl.multiple_of(step * BQ, BQ)
        attend_backward(lengths_ref, bucket, 0, first_row, pl.multiple_of(first_row - BQ, BQ), 2 * BQ, *shared)
        return carry

    lax.fori_loop(1, LEN // BQ, later, 0)
    finish_keys(0, cos_ref, sin_ref, gproj_ref, dk_ref, dv_ref)


def moments(weight, gradient, first, second):
    first = beta_first * first + (1.0 - beta_first) * gradient
    second = beta_second * second + (1.0 - beta_second) * gradient * gradient
    update = (
        first / (1.0 - beta_first**STEP) / (jnp.sqrt(second / (1.0 - beta_second**STEP)) + adam_eps)
        + decay_rate * weight
    )
    return first, second, update


def planes(which):
    if which == 0:
        return [(slice(None), head, slice(None)) for head in range(2)]
    if which == 1:
        return [(head, slice(None), slice(None)) for head in range(2)]
    return [(slice(None), slice(None))]


def total_of(values_in):
    return jnp.sum(jnp.sum(values_in, 1, keepdims=True), 0, keepdims=True)


def sums_of_squares(tables):
    lanes = lane_ids((1, 512))
    row = jnp.zeros((1, 512), jnp.float32)
    for which, squares in enumerate(tables):
        amount = sum((total_of(plane) for plane in squares[1:]), total_of(squares[0]))
        row = row + jnp.where(lanes == which, amount, 0.0)
    return row


class Everywhere:
    def __init__(self, place, held, got, last, send, recv):
        self.place, self.held, self.got, self.last = place, held, got, last
        self.send, self.recv = send, recv

    def copies(self, stage):
        peers = self.place.peers()
        if stage < 3:
            peer = (CORE, ALONG_Y, ALONG_X)[stage]
            return [remote(self.held.at[stage], self.got.at[stage], self.send.at[stage], self.recv.at[stage], peers[peer])]
        return [
            remote(self.held.at[3], self.last.at[self.place.z], self.send.at[2 + step], self.recv.at[2 + step], peers[step])
            for step in (1, 2, 3)
        ]

    def start(self, stage):
        start_all(self.copies(stage))

    def step(self, stage):
        arrive_all(self.copies(stage))
        if stage == 3:
            return
        total = self.held[stage] + self.got[stage]
        self.held[stage + 1] = total
        if stage == 2:
            self.last[self.place.z] = total
        self.start(stage + 1)

    def total(self):
        return (self.last[0] + self.last[1]) + (self.last[2] + self.last[3])

    def sent(self):
        for stage in range(4):
            sent_all(self.copies(stage))


class Summing:
    def __init__(self, index, place, away, held, got, middle, near, last, send, recv):
        self.weight, self.row, self.count, self.width, self.order = SUMMED[index]
        self.index, self.place = index, place
        self.away, self.held, self.got = away, held, got
        self.middle, self.near, self.last = middle, near, last
        self.send, self.recv = send, recv
        self.rows = pl.ds(self.row, self.count)

    def copies(self, stage):
        place = self.place
        peers = place.peers()

        def copy(source, target, slot, peer):
            return remote(source, target, self.send.at[self.index, slot], self.recv.at[self.index, slot], peers[peer])

        held, rows = self.held, self.rows
        if stage == 0:
            return [copy(self.away(y, rows), self.got.at[y, :, :, rows, :], y, CORE) for y in range(2)]
        if stage == 1:
            if self.order == "yx":
                return [copy(held.at[1 - place.y, :, :, rows, :], self.middle, 2, ALONG_Y)]
            return [copy(held.at[:, :, 1 - place.x, rows, :], self.middle, 2, ALONG_X)]
        if stage == 2:
            if self.order == "yx":
                return [copy(held.at[place.y, :, 1 - place.x, rows, :], self.near, 3, ALONG_X)]
            return [copy(held.at[1 - place.y, :, place.x, rows, :], self.near, 3, ALONG_Y)]
        return [
            copy(held.at[place.y, (place.z + step) % 4, place.x, rows, :], self.last.at[step - 1], 3 + step, step)
            for step in (1, 2, 3)
        ]

    def start(self, stage):
        start_all(self.copies(stage))

    def add(self, where, more):
        held = self.held
        held[where] = (held[where].astype(jnp.float32) + more.astype(jnp.float32)).astype(jnp.bfloat16)

    def arrive(self, stage):
        arrive_all(self.copies(stage))
        place, rows = self.place, self.rows

        def block(z, carry):
            if stage == 0:
                for y in range(2):
                    for x in range(2):
                        self.add((y, z, x, rows, slice(None)), self.got[y, z, x, rows, :])
            elif stage == 1:
                for other in range(2):
                    if self.order == "yx":
                        self.add((place.y, z, other, rows, slice(None)), self.middle[z, other])
                    else:
                        self.add((other, z, place.x, rows, slice(None)), self.middle[other, z])
            else:
                self.add((place.y, z, place.x, rows, slice(None)), self.near[z])
            return carry

        lax.fori_loop(0, 4, block, 0)

    def result(self):
        arrive_all(self.copies(3))
        place = self.place
        own = self.held[place.y, place.z, place.x, self.rows, :].astype(jnp.float32)
        for step in range(3):
            own = own + self.last[step].astype(jnp.float32)
        return own

    def sent(self):
        for stage in range(4):
            sent_all(self.copies(stage))


def middle_shape(index):
    _, _, count, width, order = SUMMED[index]
    return (4, 2, count, width) if order == "yx" else (2, 4, count, width)


def tail_kernel(
    lengths_ref, qkv_ref, mixed_ref, gmixed_ref, total_ref, cos_ref, sin_ref, x_ref, small_ref, gy1_ref, sums_ref, in_ref,
    gout_hbm, gup_hbm, gdown_hbm, *refs,
):
    state, refs = refs[:12], refs[12:]
    grad_refs, (xgrad_ref, all_ref, norm_ref), refs = refs[:4], refs[4:7], refs[7:]
    gproj_ref, dk_ref, dv_ref, enter_t, away_in, small_acc, refs = *refs[:6], refs[6:]
    held, got, refs = refs[:4], refs[4:8], refs[8:]
    middle, near, last, refs = refs[:5], refs[5:10], refs[10:15], refs[15:]
    small_held, small_got, small_last, norm_held, norm_got, norm_last, refs = *refs[:6], refs[6:]
    send, recv, small_send, small_recv, norm_send, norm_recv, load_sem = refs
    bucket = pl.program_id(0)
    place = Place()
    sources = (None, gout_hbm, gup_hbm, gdown_hbm)

    def away(weight, width):
        if weight == 0:
            return lambda y, rows: away_in.at[y, :, :, rows, :]
        return lambda y, rows: sources[weight].at[:, :, rows, tile_cols(y * 2 + (1 - place.c), width)]

    def summing(which):
        return [
            Summing(
                index, place, away(SUMMED[index][0], SUMMED[index][3]), held[SUMMED[index][0]], got[SUMMED[index][0]],
                middle[index], near[index], last[index], send, recv,
            )
            for index in which
        ]

    early, late = summing((0, 1, 2)), summing((3, 4))
    small_sum = Everywhere(place, small_held, small_got, small_last, small_send, small_recv)
    norm_sum = Everywhere(place, norm_held, norm_got, norm_last, norm_send, norm_recv)

    def loads():
        found = []
        for weight, width in ((1, OUT_W), (2, FF_W), (3, FF_W)):
            for y in range(2):
                source = sources[weight].at[:, :, :, tile_cols(y * 2 + place.c, width)]
                found.append(pltpu.make_async_copy(source, held[weight].at[y], load_sem.at[weight - 1, y]))
        return found

    @pl.when(bucket == 0)
    def _():
        meet(place)
        for item in early:
            item.start(0)
        start_all(loads())
        for index in range(MICRO):

            def normalise(chunk, carry):
                rows = chunk_rows(chunk)
                cols = pl.ds(pl.multiple_of(index * LEN + chunk * BQ, BQ), BQ)
                enter_t[:, cols] = enter_rows(x_ref, small_ref, rows, index).T
                return carry

            lax.fori_loop(0, LEN // BQ, normalise, 0)

    @pl.when(bucket == 1)
    def _():
        for item in early:
            item.arrive(1)
        for item in early:
            item.start(2)

    shared = (qkv_ref, mixed_ref, gmixed_ref, total_ref, cos_ref, sin_ref, gproj_ref, dk_ref, dv_ref)
    attend_backward(lengths_ref, bucket, bucket, 0, 0, BQ, *shared)

    def later(step, carry):
        @pl.when((bucket == 0) & (step == 2))
        def _():
            for load in loads():
                load.wait()
            for item in early:
                item.arrive(0)
            for item in early:
                item.start(1)

        @pl.when((bucket == 1) & (step == 2))
        def _():
            for item in early:
                item.arrive(2)
            for item in early:
                item.start(3)

        first_row = pl.multiple_of(step * BQ, BQ)
        attend_backward(lengths_ref, bucket, bucket, first_row, pl.multiple_of(first_row - BQ, BQ), 2 * BQ, *shared)
        return carry

    lax.fori_loop(1, LEN // BQ, later, 0)
    finish_keys(bucket, cos_ref, sin_ref, gproj_ref, dk_ref, dv_ref)

    @pl.when(bucket == 1)
    def _():
        def grad_tile(tensor):
            right = gproj_ref[:, :, tile_cols(tensor, IN_W)].reshape(MICRO * LEN, IN_W)
            return dot(enter_t[...], right).astype(jnp.bfloat16).reshape(4, 2, 64, IN_W)

        def tiles(step, carry):
            @pl.when(step < 2)
            def _():
                away_in[step] = grad_tile(step * 2 + 1 - place.c)

            @pl.when(step == 1)
            def _():
                for item in late:
                    item.start(0)

            @pl.when(step >= 2)
            def _():
                held[0][step - 2] = grad_tile((step - 2) * 2 + place.c)

            return carry

        lax.fori_loop(0, 4, tiles, 0)
        small_acc[...] = jnp.zeros_like(small_acc)
        in_full = in_ref[...]

        def data_grad(step, carry):
            for stage, moment in ((0, 1), (1, 4), (2, 7)):

                @pl.when(step == moment)
                def _():
                    for item in late:
                        item.arrive(stage)
                    for item in late:
                        item.start(stage + 1)

            index = step // (LEN // BQ)
            rows = chunk_rows(step % (LEN // BQ))
            grad_enter = dot(gproj_ref[index, rows, :], in_full, NT)
            normal, inverse = norm_parts(x_ref[index, rows, :].astype(jnp.float32))
            back = norm_back(grad_enter * small_ref[0:1, :], normal, inverse)
            xgrad_ref[index, rows, :] = (gy1_ref[index, rows, :] + back).astype(jnp.bfloat16)
            small_acc[0] += jnp.sum((grad_enter * normal).reshape(BQ // 8, 8, D), 0)
            small_acc[1] += jnp.sum(grad_enter.reshape(BQ // 8, 8, D), 0)
            return carry

        lax.fori_loop(0, MICRO * LEN // BQ, data_grad, 0)

        rows = [jnp.sum(small_acc[row], 0, keepdims=True) for row in range(2)]
        rows += [jnp.sum(sums_ref[row], 0, keepdims=True) for row in range(4)]
        weights_sq = []
        for which in range(4):
            weights_sq.append([state[3 * which][plane] * state[3 * which][plane] for plane in planes(which)])
        rows.append(sums_of_squares(weights_sq))
        rows.append(jnp.zeros((1, D), jnp.float32))
        small_held[0] = jnp.concatenate(rows, 0)
        small_sum.start(0)

        grads = [None, early[0].result().T, early[1].result(), early[2].result().T]
        grad_refs[1][0] = grads[1][:HEAD_DIM]
        grad_refs[1][1] = grads[1][HEAD_DIM:]
        grad_refs[2][...] = grads[2]
        grad_refs[3][...] = grads[3]
        small_sum.step(0)
        parts = [item.result() for item in late]
        part = jnp.concatenate(parts, 0)
        for head in range(2):
            pieces = [part[:, which * 128 + head * HEAD_DIM : which * 128 + head * HEAD_DIM + HEAD_DIM] for which in range(3)]
            grad_refs[0][:, head, :] = jnp.concatenate(pieces, 1)
        updates_sq = []
        for which in range(4):
            squares = []
            for plane in planes(which):
                weight, first, second = (state[3 * which + kind][plane] for kind in range(3))
                update = moments(weight, grad_refs[which][plane], first, second)[2]
                squares.append(update * update)
            updates_sq.append(squares)
        norm_held[0] = jnp.broadcast_to(sums_of_squares(updates_sq)[:, :128], (8, 128))
        norm_sum.start(0)
        small_sum.step(1)
        norm_sum.step(0)
        small_sum.step(2)
        norm_sum.step(1)
        small_sum.step(3)
        norm_sum.step(2)
        norm_sum.step(3)
        all_ref[...] = small_sum.total()
        norm_ref[...] = norm_sum.total()
        for item in early + late:
            item.sent()
        small_sum.sent()
        norm_sum.sent()


def lamb_kernel(*refs):
    state, grads, refs = refs[:12], refs[12:16], refs[16:]
    small_ref, small_first_ref, small_second_ref, all_ref, norm_ref, refs = *refs[:5], refs[5:]
    outs, (grad_ref, new_ref, first_ref, second_ref, norms_ref) = refs[:16], refs[16:]
    weight_norm = jnp.sqrt(all_ref[6:7, 0:128])
    update_sq = norm_ref[0:1, :]
    ratio = learn_rate * weight_norm * lax.rsqrt(update_sq + 1e-12)
    for which in range(4):
        scale = ratio[:, which : which + 1]
        for plane in planes(which):
            weight, first, second = (state[3 * which + kind][plane] for kind in range(3))
            first, second, update = moments(weight, grads[which][plane], first, second)
            new = weight - scale * update
            outs[4 * which][plane] = new
            outs[4 * which + 1][plane] = first
            outs[4 * which + 2][plane] = second
            outs[4 * which + 3][plane] = new.astype(jnp.bfloat16)
    small = small_ref[...]
    small_grad = all_ref[0:6, :]
    grad_ref[...] = small_grad
    first, second, update = moments(small, small_grad, small_first_ref[...], small_second_ref[...])
    small_sq = jnp.sum(small * small, 1, keepdims=True)
    change_sq = jnp.sum(update * update, 1, keepdims=True)
    new_ref[...] = small - learn_rate * jnp.sqrt(small_sq) * lax.rsqrt(change_sq + 1e-12) * update
    first_ref[...] = first
    second_ref[...] = second
    lanes = lane_ids((1, 128))
    top = jnp.where(lanes < 4, weight_norm, 0.0)
    bottom = jnp.where(lanes < 4, jnp.sqrt(update_sq), 0.0)
    for row in range(6):
        top = top + jnp.where(lanes == 4 + row, jnp.sqrt(small_sq[row : row + 1]), 0.0)
        bottom = bottom + jnp.where(lanes == 4 + row, jnp.sqrt(change_sq[row : row + 1]), 0.0)
    norms_ref[0:1, :] = top[:, :10]
    norms_ref[1:2, :] = bottom[:, :10]


def whole(shape):
    return pl.BlockSpec(shape, lambda *ids: (0,) * len(shape), pipeline_mode=pl.Buffered(1))


def per_bucket(*shape):
    return pl.BlockSpec((1,) + shape, lambda b: (b, 0, 0))


def bf16(*shape):
    return jax.ShapeDtypeStruct(shape, jnp.bfloat16)


def f32(*shape):
    return jax.ShapeDtypeStruct(shape, jnp.float32)


def vmem16(*shape):
    return pltpu.VMEM(shape, jnp.bfloat16)


def vmem32(*shape):
    return pltpu.VMEM(shape, jnp.float32)


SCALARS = pl.BlockSpec(memory_space=pltpu.SMEM)
ANYWHERE = pl.BlockSpec(memory_space=pl.ANY)


def params(count, collective=None):
    more = {} if collective is None else dict(collective_id=collective, has_side_effects=True)
    return pltpu.CompilerParams(dimension_semantics=("arbitrary",) * count, vmem_limit_bytes=VMEM_LIMIT, **more)


def turn_tables(lengths):
    ends = jnp.cumsum(lengths, axis=1)
    position = jnp.arange(LEN, dtype=jnp.int32)
    passed = position[None, :, None] >= ends[:, None, : CLIPS - 1]
    start = jnp.max(jnp.where(passed, ends[:, None, : CLIPS - 1], 0), axis=2)
    offset = (position[None, :] - start).astype(jnp.float32)
    frequency = jnp.exp(jnp.arange(HEAD_DIM // 2, dtype=jnp.float32) * (-2.0 * math.log(10000.0) / HEAD_DIM))
    angles = offset[:, :, None] * frequency
    cosine = jnp.repeat(jnp.cos(angles), 2, axis=-1)
    sine = jnp.sin(angles)
    sine = jnp.stack([-sine, sine], axis=-1).reshape(cosine.shape)
    return jnp.concatenate([cosine, cosine], -1), jnp.concatenate([sine, sine], -1)


def attention_forward(lengths, x, small, cosine, sine, in_mat):
    count = x.shape[0]
    return pl.pallas_call(
        functools.partial(forward_kernel, alone=True),
        grid=(count,),
        in_specs=[SCALARS, per_bucket(LEN, D), whole((6, D)), per_bucket(LEN, 128), per_bucket(LEN, 128), whole((D, 3 * D))],
        out_specs=[per_bucket(LEN, 3 * D), per_bucket(LEN, D), per_bucket(LEN, D), per_bucket(LEN, D)],
        out_shape=[bf16(count, LEN, 3 * D), bf16(count, LEN, D), f32(count, LEN, D), bf16(count, LEN, D)],
        compiler_params=params(1),
        name="attention_forward",
    )(lengths, x, small, cosine, sine, in_mat)


def gather_forward(lengths, x, small, cosine, sine, shard):
    shapes = [(4, 2, 64, 4 * width) for width in (IN_W, OUT_W, FF_W, FF_W)]
    return pl.pallas_call(
        functools.partial(forward_kernel, alone=False),
        grid=(MICRO,),
        in_specs=[
            SCALARS, per_bucket(LEN, D), whole((6, D)), per_bucket(LEN, 128), per_bucket(LEN, 128), whole((64, SHARD_W)),
        ],
        out_specs=[per_bucket(LEN, 3 * D), per_bucket(LEN, D), per_bucket(LEN, D)] + [ANYWHERE] * 4,
        out_shape=[bf16(MICRO, LEN, 3 * D), bf16(MICRO, LEN, D), f32(MICRO, LEN, D)] + [bf16(*shape) for shape in shapes],
        scratch_shapes=[vmem16(*shape) for shape in shapes]
        + [
            vmem16(1, LEN, D),
            pltpu.SemaphoreType.DMA((5, 8)),
            pltpu.SemaphoreType.DMA((5, 8)),
            pltpu.SemaphoreType.DMA((4,)),
            pltpu.SemaphoreType.DMA((4,)),
        ],
        compiler_params=params(1, 1),
        name="gather_forward",
    )(lengths, x, small, cosine, sine, shard)


def mlp_both(lengths, x, cot, mixed, small, out_mat, up_mat, down_mat):
    count = x.shape[0]
    rows = count * LEN

    def chunked(width):
        return pl.BlockSpec((1, MLP_ROWS, width), lambda b, i: (b, i, 0))

    return pl.pallas_call(
        mlp_kernel,
        grid=(count, LEN // MLP_ROWS),
        in_specs=[SCALARS, chunked(D), chunked(D), chunked(D), whole((6, D)), whole((D, D)), whole((D, FF)), whole((D, FF))],
        out_specs=[chunked(D), chunked(D), chunked(D), whole((4, 8, D)), whole((D, D)), whole((D, FF)), whole((D, FF))],
        out_shape=[
            bf16(count, LEN, D), f32(count, LEN, D), bf16(count, LEN, D), f32(4, 8, D), bf16(D, D), bf16(D, FF), bf16(D, FF),
        ],
        scratch_shapes=[
            vmem16(rows, FF), vmem16(rows, FF), vmem16(rows, D), vmem16(D, rows), vmem16(D, rows), vmem16(D, rows),
        ],
        compiler_params=params(2),
        name="mlp_both",
    )(lengths, x, cot, mixed, small, out_mat, up_mat, down_mat)


def attention_backward(lengths, qkv, mixed, gmixed, totals, cosine, sine):
    count = qkv.shape[0]
    return pl.pallas_call(
        backward_kernel,
        grid=(count,),
        in_specs=[SCALARS, per_bucket(LEN, 3 * D), per_bucket(LEN, D), per_bucket(LEN, D), per_bucket(LEN, D), per_bucket(LEN, 128), per_bucket(LEN, 128)],
        out_specs=per_bucket(LEN, 3 * D),
        out_shape=bf16(count, LEN, 3 * D),
        scratch_shapes=[vmem32(LEN, D), vmem32(LEN, D)],
        compiler_params=params(1),
        name="attention_backward",
    )(lengths, qkv, mixed, gmixed, totals, cosine, sine)


def backward_tail(lengths, qkv, mixed, gmixed, totals, cosine, sine, x, small, gy1, sums, in_mat, gout, gup, gdown, state):
    widths = (IN_W, OUT_W, FF_W, FF_W)
    dma = pltpu.SemaphoreType.DMA
    grad_shapes = [f32(*state[3 * which].shape) for which in range(4)]
    return pl.pallas_call(
        tail_kernel,
        grid=(MICRO,),
        in_specs=[
            SCALARS, per_bucket(LEN, 3 * D), per_bucket(LEN, D), per_bucket(LEN, D), per_bucket(LEN, D),
            per_bucket(LEN, 128), per_bucket(LEN, 128), whole((MICRO, LEN, D)), whole((6, D)), whole((MICRO, LEN, D)),
            whole((4, 8, D)), whole((D, 3 * D)), ANYWHERE, ANYWHERE, ANYWHERE,
        ]
        + [whole(item.shape) for item in state],
        out_specs=[whole(item.shape) for item in grad_shapes] + [whole((MICRO, LEN, D)), whole((8, D)), whole((8, 128))],
        out_shape=grad_shapes + [bf16(MICRO, LEN, D), f32(8, D), f32(8, 128)],
        scratch_shapes=[
            vmem16(MICRO, LEN, 3 * D), vmem32(LEN, D), vmem32(LEN, D), vmem16(D, MICRO * LEN), vmem16(2, 4, 2, 64, IN_W), vmem32(2, 8, D),
        ]
        + [vmem16(2, 4, 2, 64, width) for width in widths]
        + [vmem16(2, 4, 2, 64, width) for width in widths]
        + [vmem16(*middle_shape(index)) for index in range(5)]
        + [vmem16(4, SUMMED[index][2], SUMMED[index][3]) for index in range(5)]
        + [vmem16(3, SUMMED[index][2], SUMMED[index][3]) for index in range(5)]
        + [vmem32(4, 8, D), vmem32(3, 8, D), vmem32(4, 8, D), vmem32(4, 8, 128), vmem32(3, 8, 128), vmem32(4, 8, 128)]
        + [dma((5, 7)), dma((5, 7)), dma((6,)), dma((6,)), dma((6,)), dma((6,)), dma((3, 2))],
        compiler_params=params(1, 2),
        name="backward_tail",
    )(lengths, qkv, mixed, gmixed, totals, cosine, sine, x, small, gy1, sums, in_mat, gout, gup, gdown, *state)


def lamb_all(state, grads, small, small_first, small_second, everything, norm_squares):
    outs = []
    for which in range(4):
        shape = state[3 * which].shape
        outs += [f32(*shape)] * 3 + [bf16(*shape)]
    outs += [f32(6, D)] * 4 + [f32(2, 10)]
    return pl.pallas_call(
        lamb_kernel,
        out_shape=outs,
        compiler_params=pltpu.CompilerParams(vmem_limit_bytes=VMEM_LIMIT),
        name="lamb_all",
    )(*state, *grads, small, small_first, small_second, everything, norm_squares)


def tile_shard(in_proj, out_proj, up_proj, down_proj, paired):
    depth, heads_here, _ = in_proj.shape
    in_cols = in_proj.reshape(depth, heads_here, 3, HEAD_DIM)
    if paired:
        in_cols = in_cols.transpose(0, 2, 1, 3)
    out_cols = out_proj.reshape(heads_here * HEAD_DIM, depth).T
    parts = [in_cols.reshape(depth, -1), out_cols, up_proj, down_proj.T]
    return jnp.concatenate(parts, axis=1).astype(jnp.bfloat16)


def on_device(
    frames, cotangent, clip_lengths, in_proj, out_proj, up_proj, down_proj, small_params,
    in_first, in_second, out_first, out_second, up_first, up_second, down_first, down_second,
    small_first, small_second,
):
    lengths = lax.dynamic_slice_in_dim(clip_lengths, lax.axis_index("tensor"), 1, 1).reshape(MICRO, CLIPS)
    cosine, sine = turn_tables(lengths)
    shard = tile_shard(in_proj, out_proj, up_proj, down_proj, True)
    qkv, mixed, totals, in_full, out_full, up_full, down_full = gather_forward(lengths, frames, small_params, cosine, sine, shard)
    block_out, gy1, gmixed, sums, gout, gup, gdown = mlp_both(
        lengths, frames, cotangent, mixed, small_params, out_full.reshape(D, D), up_full.reshape(D, FF), down_full.reshape(D, FF)
    )
    state = (
        in_proj, in_first, in_second, out_proj, out_first, out_second, up_proj, up_first, up_second, down_proj, down_first, down_second,
    )
    *grads, input_grad, everything, norm_squares = backward_tail(
        lengths, qkv, mixed, gmixed, totals, cosine, sine, frames, small_params, gy1, sums, in_full.reshape(D, 3 * D),
        gout.reshape(4, 2, 64, D), gup.reshape(4, 2, 64, FF), gdown.reshape(4, 2, 64, FF), state,
    )
    outs = lamb_all(state, grads, small_params, small_first, small_second, everything, norm_squares)
    return (block_out, input_grad, *outs)


def on_any_mesh(
    frames, cotangent, clip_lengths, in_proj, out_proj, up_proj, down_proj, small_params,
    in_first, in_second, out_first, out_second, up_first, up_second, down_first, down_second,
    small_first, small_second,
):
    rows_here = frames.shape[1]
    own_buckets = rows_here // LEN
    first_bucket = lax.axis_index("tensor") * own_buckets
    lengths = lax.dynamic_slice_in_dim(clip_lengths, first_bucket, own_buckets, 1).reshape(-1, CLIPS)
    count = MICRO * own_buckets
    x = frames.reshape(count, LEN, D)
    cot = cotangent.reshape(count, LEN, D)
    tensor_size = lax.axis_size("tensor")
    dp_size = lax.axis_size("dp")
    depth = in_proj.shape[0]
    heads_here = in_proj.shape[1]
    ff_here = up_proj.shape[1]

    shard = tile_shard(in_proj, out_proj, up_proj, down_proj, False)
    gathered = lax.all_gather(shard, ("dp", "tensor"), axis=0)
    gathered = gathered.reshape(dp_size, tensor_size, depth, shard.shape[1])
    gathered = jnp.moveaxis(gathered, 1, 2).reshape(D, tensor_size, shard.shape[1])
    edge0 = heads_here * 192
    edge1 = edge0 + heads_here * HEAD_DIM
    edge2 = edge1 + ff_here
    in_mat = gathered[:, :, :edge0].reshape(D, PAIRS, 2, 3, HEAD_DIM).transpose(0, 1, 3, 2, 4).reshape(D, 3 * D)
    out_mat = gathered[:, :, edge0:edge1].reshape(D, D)
    up_mat = gathered[:, :, edge1:edge2].reshape(D, FF)
    down_mat = gathered[:, :, edge2:].reshape(D, FF)

    cosine, sine = turn_tables(lengths)
    qkv, mixed, totals, enter1 = attention_forward(lengths, x, small_params, cosine, sine, in_mat)
    block_out, grad_y_first, grad_mixed, sums, grad_out, grad_upw, grad_down = mlp_both(
        lengths, x, cot, mixed, small_params, out_mat, up_mat, down_mat
    )

    def weight_grad(left, right):
        return dot(left.reshape(-1, left.shape[-1]), right.reshape(-1, right.shape[-1]), TN).astype(jnp.bfloat16)

    grad_proj = attention_backward(lengths, qkv, mixed, grad_mixed, totals, cosine, sine)
    grad_in = weight_grad(enter1, grad_proj)
    grad_in = grad_in.reshape(D, PAIRS, 3, 2, HEAD_DIM).transpose(0, 1, 3, 2, 4)

    def by_owner(mat):
        return jnp.moveaxis(mat.reshape(dp_size, depth, tensor_size, -1), 2, 1)

    stacked = jnp.concatenate([by_owner(grad_in), by_owner(grad_out), by_owner(grad_upw), by_owner(grad_down)], axis=-1)
    owned = lax.psum_scatter(
        stacked.reshape(dp_size * tensor_size, depth, -1), ("dp", "tensor"), scatter_dimension=0, tiled=False
    ).astype(jnp.float32)

    grad_enter1 = dot(grad_proj.reshape(-1, 3 * D), in_mat, NT).reshape(count, LEN, D)
    normal1, inverse1 = norm_parts(x.astype(jnp.float32))
    input_grad = (grad_y_first + norm_back(grad_enter1 * small_params[0], normal1, inverse1)).astype(jnp.bfloat16)
    late = jnp.sum(sums, axis=1)
    small_terms = jnp.stack(
        [jnp.sum(grad_enter1 * normal1, (0, 1)), jnp.sum(grad_enter1, (0, 1)), late[0], late[1], late[2], late[3]]
    )

    grads = (
        owned[:, :edge0].reshape(in_proj.shape),
        owned[:, edge0:edge1].T.reshape(out_proj.shape),
        owned[:, edge1:edge2],
        owned[:, edge2:].T,
    )
    weights_in = (in_proj, out_proj, up_proj, down_proj)
    firsts = (in_first, out_first, up_first, down_first)
    seconds = (in_second, out_second, up_second, down_second)
    own_squares = jnp.stack([jnp.sum(weight * weight) for weight in weights_in])
    small_grad, weight_squares = lax.psum((small_terms, own_squares), ("dp", "tensor"))
    new_firsts = []
    new_seconds = []
    updates = []
    for weight, gradient, first, second in zip(weights_in, grads, firsts, seconds):
        first = beta_first * first + (1.0 - beta_first) * gradient
        second = beta_second * second + (1.0 - beta_second) * gradient * gradient
        update = (
            first / (1.0 - beta_first**STEP) / (jnp.sqrt(second / (1.0 - beta_second**STEP)) + adam_eps)
            + decay_rate * weight
        )
        new_firsts.append(first)
        new_seconds.append(second)
        updates.append(update)
    update_squares = lax.psum(jnp.stack([jnp.sum(update * update) for update in updates]), ("dp", "tensor"))
    trust_ratio = jnp.sqrt(weight_squares) * lax.rsqrt(update_squares + 1e-12)
    new_weights = [weights_in[index] - learn_rate * trust_ratio[index] * updates[index] for index in range(4)]
    small_first_new = beta_first * small_first + (1.0 - beta_first) * small_grad
    small_second_new = beta_second * small_second + (1.0 - beta_second) * small_grad * small_grad
    small_update = (
        small_first_new / (1.0 - beta_first**STEP) / (jnp.sqrt(small_second_new / (1.0 - beta_second**STEP)) + adam_eps)
        + decay_rate * small_params
    )
    small_weight_sq = jnp.sum(small_params * small_params, axis=1, keepdims=True)
    small_update_sq = jnp.sum(small_update * small_update, axis=1, keepdims=True)
    small_new = small_params - learn_rate * jnp.sqrt(small_weight_sq) * lax.rsqrt(small_update_sq + 1e-12) * small_update
    norms = jnp.stack(
        [
            jnp.concatenate([jnp.sqrt(weight_squares), jnp.sqrt(small_weight_sq).reshape(-1)]),
            jnp.concatenate([jnp.sqrt(update_squares), jnp.sqrt(small_update_sq).reshape(-1)]),
        ]
    )
    outputs = [block_out.reshape(frames.shape), input_grad.reshape(frames.shape)]
    for new, first, second in zip(new_weights, new_firsts, new_seconds):
        outputs += [new, first, second, new.astype(jnp.bfloat16)]
    return tuple(outputs + [small_grad, small_new, small_first_new, small_second_new, norms])


def solution(mesh):
    rows = P(None, ("dp", "tensor"), None)
    in_spec = P("dp", "tensor", None)
    out_spec = P("tensor", None, "dp")
    up_spec = P("dp", "tensor")
    down_spec = P("tensor", "dp")
    shape = dict(mesh.shape)
    small_slice = shape["dp"] == HERE_DP and shape["tensor"] == HERE_TENSOR
    return jax.shard_map(
        on_device if small_slice else on_any_mesh,
        mesh=mesh,
        in_specs=(
            rows, rows, P(None, "dp", None), in_spec, out_spec, up_spec, down_spec, P(),
            in_spec, in_spec, out_spec, out_spec, up_spec, up_spec, down_spec, down_spec, P(), P(),
        ),
        out_specs=(rows, rows) + (in_spec,) * 4 + (out_spec,) * 4 + (up_spec,) * 4 + (down_spec,) * 4 + (P(),) * 5,
        check_vma=False,
    )
```

```python
import functools
import math

import jax
import jax.numpy as jnp
import numpy as np
from jax import lax
from jax.experimental import pallas as pl
from jax.experimental.pallas import tpu as pltpu
from jax.sharding import PartitionSpec as P

D = 512
HEADS = 8
HEAD_DIM = 64
FF = 2048
PAIRS = HEADS // 2
WINDOW = 250
LEN = 1024
CLIPS = 4
MICRO = 2
STEP = 3

BQ = 256
MLP_ROWS = 256
VMEM_LIMIT = 62 * 1024 * 1024

beta_first = 0.5
beta_second = 0.5
adam_eps = 1e-06
decay_rate = 0.01
learn_rate = 0.3

NT = (((1,), (1,)), ((), ()))
NN = (((1,), (0,)), ((), ()))
TN = (((0,), (0,)), ((), ()))


def dot(a, b, dims=NN):
    return lax.dot_general(a, b, dims, preferred_element_type=jnp.float32)


def norm_parts(rows):
    mean = jnp.mean(rows, -1, keepdims=True)
    centred = rows - mean
    inverse = lax.rsqrt(jnp.mean(centred * centred, -1, keepdims=True) + 1e-05)
    return centred * inverse, inverse


def norm_back(scaled, normal, inverse):
    return inverse * (
        scaled
        - jnp.mean(scaled, -1, keepdims=True)
        - normal * jnp.mean(scaled * normal, -1, keepdims=True)
    )


def lane_ids(shape):
    return lax.broadcasted_iota(jnp.int32, shape, len(shape) - 1)


def swap_pairs(rows):
    even = (lane_ids(rows.shape) & 1) == 0
    return jnp.where(even, pltpu.roll(rows, 127, 1), pltpu.roll(rows, 1, 1))


def run_starts(lengths_ref, bucket, position):
    end0 = lengths_ref[bucket, 0]
    end1 = end0 + lengths_ref[bucket, 1]
    end2 = end1 + lengths_ref[bucket, 2]
    start = jnp.where(position >= end0, end0, 0)
    start = jnp.where(position >= end1, end1, start)
    return jnp.where(position >= end2, end2, start), position < end2


def block_bias(lengths_ref, bucket, first_row, first_key, keys):
    position = first_row + lax.broadcasted_iota(jnp.int32, (BQ, 1), 0)
    start, _ = run_starts(lengths_ref, bucket, position)
    lowest = jnp.maximum(start, position - (WINDOW - 1))
    key = first_key + lax.broadcasted_iota(jnp.int32, (BQ, keys), 1)
    return jnp.where((key >= lowest) & (key <= position), 0.0, -1e30)


def head_lanes(tile, head):
    return jnp.where((lane_ids(tile.shape) // HEAD_DIM) == head, tile, jnp.zeros_like(tile))


MESH = pl.DeviceIdType.MESH
HERE_DP = 8
HERE_TENSOR = 4
IN_W, OUT_W, FF_W = 384, 128, 512
SHARD_W = IN_W + OUT_W + 2 * FF_W
CORE, ALONG_Y, ALONG_X = "core", "y", "x"

GATHERED = (
    (0, 0, 32, IN_W, 0, "xy"),
    (0, 32, 32, IN_W, 0, "yx"),
    (1, 0, 64, OUT_W, IN_W, "xy"),
    (2, 0, 64, FF_W, IN_W + OUT_W, "xy"),
    (3, 0, 64, FF_W, IN_W + OUT_W + FF_W, "yx"),
)
SUMMED = (
    (1, 0, 64, OUT_W, "yx"),
    (2, 0, 64, FF_W, "yx"),
    (3, 0, 64, FF_W, "xy"),
    (0, 0, 32, IN_W, "xy"),
    (0, 32, 32, IN_W, "yx"),
)


class Place:
    def __init__(self):
        dp = lax.axis_index("dp")
        tensor = lax.axis_index("tensor")
        self.z, self.x = dp // 2, dp % 2
        self.y, self.c = tensor // 2, tensor % 2

    def device(self, dz=0, x=None, y=None, c=None):
        x = self.x if x is None else x
        y = self.y if y is None else y
        c = self.c if c is None else c
        return {"dp": (self.z + dz) % 4 * 2 + x, "tensor": y * 2 + c}

    def peers(self):
        return {
            CORE: self.device(c=1 - self.c),
            ALONG_Y: self.device(y=1 - self.y),
            ALONG_X: self.device(x=1 - self.x),
            1: self.device(dz=1),
            2: self.device(dz=2),
            3: self.device(dz=3),
        }


def tile_cols(tensor, width):
    return pl.ds(pl.multiple_of(tensor * width, 128), width)


def remote(source, target, send, recv, device):
    return pltpu.make_async_remote_copy(
        src_ref=source, dst_ref=target, send_sem=send, recv_sem=recv, device_id=device, device_id_type=MESH
    )


def meet(place):
    barrier = pltpu.get_barrier_semaphore()
    peers = place.peers()
    for device in peers.values():
        pl.semaphore_signal(barrier, inc=1, device_id=device, device_id_type=MESH)
    pl.semaphore_wait(barrier, len(peers))


def start_all(copies):
    for copy in copies:
        copy.start()


def arrive_all(copies):
    for copy in copies:
        copy.wait_recv()


def sent_all(copies):
    for copy in copies:
        copy.wait_send()


def gather_copies(index, stage, place, shard, weights, send, recv):
    weight, row, count, width, offset, order = GATHERED[index]
    full = weights[weight]
    rows = pl.ds(row, count)
    peers = place.peers()

    def copy(source, target, slot, peer):
        return remote(source, target, send.at[index, slot], recv.at[index, slot], peers[peer])

    def cols(y):
        return tile_cols(y * 2 + place.c, width)

    mine = cols(place.y)
    if stage == 0:
        return [
            copy(shard.at[rows, offset : offset + width], full.at[place.z, place.x, rows, mine], step - 1, step)
            for step in (1, 2, 3)
        ]
    if stage == 3:
        parts = [full.at[:, :, rows, cols(y)] for y in range(2)]
        return [copy(part, part, 6 + y, CORE) for y, part in enumerate(parts)]
    if stage == 1:
        part = full.at[:, place.x, rows, mine]
        return [copy(part, part, 3, ALONG_X if order == "xy" else ALONG_Y)]
    if order == "xy":
        part = full.at[:, :, rows, mine]
        return [copy(part, part, 4, ALONG_Y)]
    parts = [full.at[:, place.x, rows, cols(y)] for y in range(2)]
    return [copy(part, part, 4 + y, ALONG_X) for y, part in enumerate(parts)]


def project_rows(rows, enter, cosine, sine, weight, qkv_ref):
    for pair in range(PAIRS):
        part = dot(enter, weight(pair))
        for which in range(2):
            piece = part[:, which * 128 : which * 128 + 128]
            turned = piece * cosine + swap_pairs(piece) * sine
            if which == 0:
                turned = turned * (HEAD_DIM**-0.5)
            qkv_ref[0, rows, pair * 384 + which * 128 : pair * 384 + which * 128 + 128] = turned.astype(jnp.bfloat16)
        qkv_ref[0, rows, pair * 384 + 256 : pair * 384 + 384] = part[:, 256:].astype(jnp.bfloat16)


def attend_forward(lengths_ref, bucket, first_row, first_key, keys, qkv_ref, mixed_ref, total_ref):
    rows = pl.ds(first_row, BQ)
    key_rows = pl.ds(first_key, keys)
    bias = block_bias(lengths_ref, bucket, first_row, first_key, keys)
    for pair in range(PAIRS):
        base = pair * 384
        queries = qkv_ref[0, rows, base : base + 128]
        keys_rot = qkv_ref[0, key_rows, base + 128 : base + 256]
        values = qkv_ref[0, key_rows, base + 256 : base + 384]
        outs = []
        totals = []
        for head in range(2):
            scores = dot(head_lanes(queries, head), keys_rot, NT) + bias
            top = jnp.max(scores, -1, keepdims=True)
            powers = jnp.exp(scores - top)
            total = jnp.sum(powers, -1, keepdims=True)
            outs.append(dot(powers.astype(jnp.bfloat16), values) / total)
            totals.append(jnp.broadcast_to(top + jnp.log(total), (BQ, 128)))
        low = lane_ids((BQ, 128)) < HEAD_DIM
        mixed_ref[0, rows, pair * 128 : pair * 128 + 128] = jnp.where(low, outs[0], outs[1]).astype(jnp.bfloat16)
        total_ref[0, rows, pair * 128 : pair * 128 + 128] = jnp.where(low, totals[0], totals[1])


def turn_tables_here(lengths_ref, steps_ref, cos_ref, sin_ref):
    lanes = lane_ids((8, 128))
    frequency = jnp.exp(((lanes & (HEAD_DIM - 1)) // 2).astype(jnp.float32) * (-2.0 * math.log(10000.0) / HEAD_DIM))
    sign = jnp.where((lane_ids((1, 128)) & 1) == 0, -1.0, 1.0)
    fine_cos, fine_sin = steps_ref[2:3], steps_ref[3:4]
    for bucket in range(MICRO):
        end0 = lengths_ref[bucket, 0]
        end1 = end0 + lengths_ref[bucket, 1]
        end2 = end1 + lengths_ref[bucket, 2]
        row = lax.broadcasted_iota(jnp.int32, (8, 128), 0)
        start = jnp.where(row == 0, 0, jnp.where(row == 1, end0, jnp.where(row == 2, end1, end2)))
        angle = start.astype(jnp.float32) * frequency
        run_cos, run_sin = jnp.cos(angle), jnp.sin(angle)

        def chunk_tables(chunk, carry):
            coarse = pl.ds(pl.multiple_of(chunk * 8, 8), 8)
            coarse_cos, coarse_sin = steps_ref[0, coarse, :][:, None, :], steps_ref[1, coarse, :][:, None, :]
            at_cos = (coarse_cos * fine_cos - coarse_sin * fine_sin).reshape(BQ, 128)
            at_sin = (coarse_sin * fine_cos + coarse_cos * fine_sin).reshape(BQ, 128)
            position = chunk * BQ + lax.broadcasted_iota(jnp.int32, (BQ, 128), 0)
            first_cos, first_sin = run_cos[0:1], run_sin[0:1]
            for run, end in enumerate((end0, end1, end2)):
                first_cos = jnp.where(position >= end, run_cos[run + 1 : run + 2], first_cos)
                first_sin = jnp.where(position >= end, run_sin[run + 1 : run + 2], first_sin)
            rows = chunk_rows(chunk)
            cos_ref[bucket, rows, :] = at_cos * first_cos + at_sin * first_sin
            sin_ref[bucket, rows, :] = (at_sin * first_cos - at_cos * first_sin) * sign
            return carry

        lax.fori_loop(0, LEN // BQ, chunk_tables, 0)


def position_steps():
    lane = np.arange(128) % HEAD_DIM // 2
    frequency = np.exp(lane.astype(np.float32) * np.float32(-2.0 * math.log(10000.0) / HEAD_DIM)).astype(np.float64)
    step = np.arange(32)[:, None]
    coarse, fine = step * 32 * frequency, step * frequency
    return jnp.asarray(np.stack([np.cos(coarse), np.sin(coarse), np.cos(fine), np.sin(fine)]).astype(np.float32))


def enter_rows(x_ref, small_ref, rows, bucket=0):
    normal, _ = norm_parts(x_ref[bucket, rows, :].astype(jnp.float32))
    return (normal * small_ref[0:1, :] + small_ref[1:2, :]).astype(jnp.bfloat16)


def chunk_rows(chunk):
    return pl.ds(pl.multiple_of(chunk * BQ, BQ), BQ)


def forward_kernel(lengths_ref, x_ref, small_ref, *refs, alone):
    bucket = pl.program_id(0)
    table = 0 if alone else bucket
    if alone:
        cos_ref, sin_ref, in_ref, qkv_ref, mixed_ref, total_ref, enter_ref = refs
    else:
        steps_ref, shard_ref, qkv_ref, mixed_ref, total_ref, cos_ref, sin_ref = refs[:7]
        kept = refs[7:11]
        full = refs[11:15]
        enter_ref, send, recv, own_sem, keep_sem = refs[15:]
        place = Place()

        def copies(which, stage):
            found = []
            for index in which:
                found += gather_copies(index, stage, place, shard_ref, full, send, recv)
            return found

        def own_tiles():
            tiles = []
            for weight, width, offset in ((0, IN_W, 0), (1, OUT_W, IN_W), (2, FF_W, IN_W + OUT_W), (3, FF_W, IN_W + OUT_W + FF_W)):
                target = full[weight].at[place.z, place.x, :, tile_cols(place.y * 2 + place.c, width)]
                tiles.append(pltpu.make_async_copy(shard_ref.at[:, offset : offset + width], target, own_sem.at[weight]))
            return tiles

        def keeps():
            return [pltpu.make_async_copy(full[weight], kept[weight], keep_sem.at[weight]) for weight in range(4)]

        early, late = (0, 1), (2, 3, 4)

        @pl.when(bucket == 0)
        def _():
            meet(place)
            start_all(copies(early, 0))
            start_all(own_tiles())
            start_all(copies(late, 0))
            turn_tables_here(lengths_ref, steps_ref, cos_ref, sin_ref)

    def normalise(chunk, carry):
        rows = chunk_rows(chunk)
        enter_ref[0, rows, :] = enter_rows(x_ref, small_ref, rows)
        return carry

    lax.fori_loop(0, LEN // BQ, normalise, 0)

    if not alone:

        @pl.when(bucket == 0)
        def _():
            for tile in own_tiles():
                tile.wait()
            for stage in range(3):
                arrive_all(copies(early, stage))
                start_all(copies(early, stage + 1))
            arrive_all(copies(early, 3))
            arrive_all(copies(late, 0))
            start_all(copies(late, 1))

    def weight(pair):
        cols = slice(pair * 384, pair * 384 + 384)
        return in_ref[:, cols] if alone else full[0][:, :, :, cols].reshape(D, 384)

    def project(chunk, carry):
        rows = chunk_rows(chunk)
        project_rows(rows, enter_ref[0, rows, :], cos_ref[table, rows, :], sin_ref[table, rows, :], weight, qkv_ref)
        return carry

    lax.fori_loop(0, LEN // BQ, project, 0)
    attend_forward(lengths_ref, bucket, 0, 0, BQ, qkv_ref, mixed_ref, total_ref)

    def later(step, carry):
        if not alone:

            @pl.when((bucket == 0) & (step == 2))
            def _():
                arrive_all(copies(late, 1))
                start_all(copies(late, 2))

            @pl.when((bucket == 1) & (step == 1))
            def _():
                arrive_all(copies(late, 2))
                start_all(copies(late, 3))

            @pl.when((bucket == 1) & (step == 3))
            def _():
                arrive_all(copies(late, 3))
                start_all(keeps())

        first_row = pl.multiple_of(step * BQ, BQ)
        attend_forward(lengths_ref, bucket, first_row, pl.multiple_of(first_row - BQ, BQ), 2 * BQ, qkv_ref, mixed_ref, total_ref)
        return carry

    lax.fori_loop(1, LEN // BQ, later, 0)

    if not alone:

        @pl.when(bucket == 1)
        def _():
            for keep in keeps():
                keep.wait()
            for stage in range(4):
                sent_all(copies(early + late, stage))


def mlp_kernel(
    lengths_ref, x_ref, cot_ref, mixed_ref, small_ref, out_ref, up_ref, down_ref,
    block_ref, gy1_ref, gmixed_ref, sums_ref, gout_ref, gup_out_ref, gdown_ref,
    act_ref, gup_ref, keep_ref, enter_t, gmlp_t, gbranch_t,
):
    bucket = pl.program_id(0)
    chunk = pl.program_id(1)
    buckets = pl.num_programs(0)
    chunks = pl.num_programs(1)

    @pl.when((bucket == 0) & (chunk == 0))
    def _():
        sums_ref[...] = jnp.zeros_like(sums_ref)

    index = bucket * chunks + chunk
    rows = pl.ds(pl.multiple_of(index * MLP_ROWS, MLP_ROWS), MLP_ROWS)
    small = [small_ref[row : row + 1, :] for row in range(6)]
    x = x_ref[0].astype(jnp.float32)
    mixed = mixed_ref[0]
    keep_ref[rows, :] = mixed
    branch = dot(mixed, out_ref[...], NT)
    y_first = x + small[4] * branch
    normal, inverse = norm_parts(y_first)
    enter = (normal * small[2] + small[3]).astype(jnp.bfloat16)
    enter_t[:, rows] = enter.T
    position = chunk * MLP_ROWS + lax.broadcasted_iota(jnp.int32, (MLP_ROWS, 1), 0)
    _, valid = run_starts(lengths_ref, bucket, position)
    grad_y = jnp.where(valid, cot_ref[0].astype(jnp.float32), 0.0)
    grad_mlp = (small[5] * grad_y).astype(jnp.bfloat16)
    gmlp_t[:, rows] = grad_mlp.T
    mlp = jnp.zeros((MLP_ROWS, D), jnp.float32)
    grad_enter = jnp.zeros((MLP_ROWS, D), jnp.float32)
    for part in range(FF // 512):
        cols = slice(part * 512, part * 512 + 512)
        upval = dot(enter, up_ref[:, cols])
        grad_act = dot(grad_mlp, down_ref[:, cols])
        cumulative = 0.5 + 0.5 * lax.erf(upval * (1.0 / math.sqrt(2.0)))
        act = (upval * cumulative).astype(jnp.bfloat16)
        act_ref[rows, cols] = act
        density = jnp.exp(-0.5 * upval * upval) * (1.0 / math.sqrt(2.0 * math.pi))
        grad_up = (grad_act * (cumulative + upval * density)).astype(jnp.bfloat16)
        gup_ref[rows, cols] = grad_up
        mlp = mlp + dot(act, down_ref[:, cols], NT)
        grad_enter = grad_enter + dot(grad_up, up_ref[:, cols], NT)
    block_ref[0] = (y_first + small[5] * mlp).astype(jnp.bfloat16)
    grad_y_first = grad_y + norm_back(grad_enter * small[2], normal, inverse)
    gy1_ref[0] = grad_y_first
    grad_branch = (small[4] * grad_y_first).astype(jnp.bfloat16)
    gbranch_t[:, rows] = grad_branch.T
    gmixed_ref[0] = dot(grad_branch, out_ref[...]).astype(jnp.bfloat16)

    def fold(terms):
        return jnp.sum(terms.reshape(MLP_ROWS // 8, 8, D), 0)

    sums_ref[0] += fold(grad_enter * normal)
    sums_ref[1] += fold(grad_enter)
    sums_ref[2] += fold(grad_y_first * branch)
    sums_ref[3] += fold(grad_y * mlp)

    @pl.when(index == buckets * chunks - 1)
    def _():
        gout_ref[...] = dot(gbranch_t[...], keep_ref[...]).astype(jnp.bfloat16)

        def weight_grads(part, carry):
            cols = pl.ds(pl.multiple_of(part * 256, 256), 256)
            gup_out_ref[:, cols] = dot(enter_t[...], gup_ref[:, cols]).astype(jnp.bfloat16)
            gdown_ref[:, cols] = dot(gmlp_t[...], act_ref[:, cols]).astype(jnp.bfloat16)
            return carry

        lax.fori_loop(0, FF // 256, weight_grads, 0)


def attend_backward(
    lengths_ref, bucket, slot, first_row, first_key, keys, qkv_ref, mixed_ref, gmixed_ref, total_ref, cos_ref, sin_ref, gproj_ref, dk_ref, dv_ref
):
    rows = pl.ds(first_row, BQ)
    key_rows = pl.ds(first_key, keys)
    bias = block_bias(lengths_ref, bucket, first_row, first_key, keys)
    low = lane_ids((BQ, 128)) < HEAD_DIM
    for pair in range(PAIRS):
        base = pair * 384
        queries = qkv_ref[0, rows, base : base + 128]
        keys_rot = qkv_ref[0, key_rows, base + 128 : base + 256]
        values = qkv_ref[0, key_rows, base + 256 : base + 384]
        grad = gmixed_ref[0, rows, pair * 128 : pair * 128 + 128]
        totals = total_ref[0, rows, pair * 128 : pair * 128 + 128]
        product = grad.astype(jnp.float32) * mixed_ref[0, rows, pair * 128 : pair * 128 + 128].astype(jnp.float32)
        grad_q = jnp.zeros((BQ, 128), jnp.float32)
        grad_k = jnp.zeros((keys, 128), jnp.float32)
        grad_v = jnp.zeros((keys, 128), jnp.float32)
        for head in range(2):
            query = head_lanes(queries, head)
            grad_head = head_lanes(grad, head)
            inner = jnp.sum(jnp.where(low == (head == 0), product, 0.0), -1, keepdims=True)
            total = totals[:, head * HEAD_DIM : head * HEAD_DIM + 1]
            attn = jnp.exp(dot(query, keys_rot, NT) + bias - total)
            grad_attn = dot(grad_head, values, NT)
            grad_scores = (attn * (grad_attn - inner)).astype(jnp.bfloat16)
            grad_v = grad_v + dot(attn.astype(jnp.bfloat16), grad_head, TN)
            grad_k = grad_k + dot(grad_scores, query, TN)
            grad_q = grad_q + dot(grad_scores, head_lanes(keys_rot, head))
        cosine = cos_ref[0, rows, :]
        sine = sin_ref[0, rows, :]
        grad_q = grad_q * (HEAD_DIM**-0.5)
        gproj_ref[slot, rows, base : base + 128] = (grad_q * cosine - swap_pairs(grad_q) * sine).astype(jnp.bfloat16)
        lanes = slice(pair * 128, pair * 128 + 128)
        if keys > BQ:
            before = pl.ds(first_key, BQ)
            dk_ref[before, lanes] += grad_k[:BQ]
            dv_ref[before, lanes] += grad_v[:BQ]
            dk_ref[rows, lanes] = grad_k[BQ:]
            dv_ref[rows, lanes] = grad_v[BQ:]
        else:
            dk_ref[rows, lanes] = grad_k
            dv_ref[rows, lanes] = grad_v


def finish_keys(slot, cos_ref, sin_ref, gproj_ref, dk_ref, dv_ref):
    def finish(chunk, carry):
        rows = chunk_rows(chunk)
        cosine = cos_ref[0, rows, :]
        sine = sin_ref[0, rows, :]
        for pair in range(PAIRS):
            grad_k = dk_ref[rows, pair * 128 : pair * 128 + 128]
            turned = grad_k * cosine - swap_pairs(grad_k) * sine
            gproj_ref[slot, rows, pair * 384 + 128 : pair * 384 + 256] = turned.astype(jnp.bfloat16)
            gproj_ref[slot, rows, pair * 384 + 256 : pair * 384 + 384] = dv_ref[rows, pair * 128 : pair * 128 + 128].astype(jnp.bfloat16)
        return carry

    lax.fori_loop(0, LEN // BQ, finish, 0)


def backward_kernel(lengths_ref, qkv_ref, mixed_ref, gmixed_ref, total_ref, cos_ref, sin_ref, gproj_ref, dk_ref, dv_ref):
    bucket = pl.program_id(0)
    shared = (qkv_ref, mixed_ref, gmixed_ref, total_ref, cos_ref, sin_ref, gproj_ref, dk_ref, dv_ref)
    attend_backward(lengths_ref, bucket, 0, 0, 0, BQ, *shared)

    def later(step, carry):
        first_row = pl.multiple_of(step * BQ, BQ)
        attend_backward(lengths_ref, bucket, 0, first_row, pl.multiple_of(first_row - BQ, BQ), 2 * BQ, *shared)
        return carry

    lax.fori_loop(1, LEN // BQ, later, 0)
    finish_keys(0, cos_ref, sin_ref, gproj_ref, dk_ref, dv_ref)


def moments(weight, gradient, first, second):
    first = beta_first * first + (1.0 - beta_first) * gradient
    second = beta_second * second + (1.0 - beta_second) * gradient * gradient
    update = (
        first / (1.0 - beta_first**STEP) / (jnp.sqrt(second / (1.0 - beta_second**STEP)) + adam_eps)
        + decay_rate * weight
    )
    return first, second, update


def planes(which):
    if which == 0:
        return [(slice(None), head, slice(None)) for head in range(2)]
    if which == 1:
        return [(head, slice(None), slice(None)) for head in range(2)]
    return [(slice(None), slice(None))]


def total_of(values_in):
    return jnp.sum(jnp.sum(values_in, 1, keepdims=True), 0, keepdims=True)


def sums_of_squares(tables):
    lanes = lane_ids((1, 512))
    row = jnp.zeros((1, 512), jnp.float32)
    for which, squares in enumerate(tables):
        amount = sum((total_of(plane) for plane in squares[1:]), total_of(squares[0]))
        row = row + jnp.where(lanes == which, amount, 0.0)
    return row


class Everywhere:
    def __init__(self, place, held, got, last, send, recv):
        self.place, self.held, self.got, self.last = place, held, got, last
        self.send, self.recv = send, recv

    def copies(self, stage):
        peers = self.place.peers()
        if stage < 3:
            peer = (CORE, ALONG_Y, ALONG_X)[stage]
            return [remote(self.held.at[stage], self.got.at[stage], self.send.at[stage], self.recv.at[stage], peers[peer])]
        return [
            remote(self.held.at[3], self.last.at[self.place.z], self.send.at[2 + step], self.recv.at[2 + step], peers[step])
            for step in (1, 2, 3)
        ]

    def start(self, stage):
        start_all(self.copies(stage))

    def step(self, stage):
        arrive_all(self.copies(stage))
        if stage == 3:
            return
        total = self.held[stage] + self.got[stage]
        self.held[stage + 1] = total
        if stage == 2:
            self.last[self.place.z] = total
        self.start(stage + 1)

    def total(self):
        return (self.last[0] + self.last[1]) + (self.last[2] + self.last[3])

    def sent(self):
        for stage in range(4):
            sent_all(self.copies(stage))


class Summing:
    def __init__(self, index, place, away, held, got, middle, near, last, send, recv):
        self.weight, self.row, self.count, self.width, self.order = SUMMED[index]
        self.index, self.place = index, place
        self.away, self.held, self.got = away, held, got
        self.middle, self.near, self.last = middle, near, last
        self.send, self.recv = send, recv
        self.rows = pl.ds(self.row, self.count)

    def copies(self, stage):
        place = self.place
        peers = place.peers()

        def copy(source, target, slot, peer):
            return remote(source, target, self.send.at[self.index, slot], self.recv.at[self.index, slot], peers[peer])

        held, rows = self.held, self.rows
        if stage == 0:
            return [copy(self.away(y, rows), self.got.at[y, :, :, rows, :], y, CORE) for y in range(2)]
        if stage == 1:
            if self.order == "yx":
                return [copy(held.at[1 - place.y, :, :, rows, :], self.middle, 2, ALONG_Y)]
            return [copy(held.at[:, :, 1 - place.x, rows, :], self.middle, 2, ALONG_X)]
        if stage == 2:
            if self.order == "yx":
                return [copy(held.at[place.y, :, 1 - place.x, rows, :], self.near, 3, ALONG_X)]
            return [copy(held.at[1 - place.y, :, place.x, rows, :], self.near, 3, ALONG_Y)]
        return [
            copy(held.at[place.y, (place.z + step) % 4, place.x, rows, :], self.last.at[step - 1], 3 + step, step)
            for step in (1, 2, 3)
        ]

    def start(self, stage):
        start_all(self.copies(stage))

    def add(self, where, more):
        held = self.held
        held[where] = (held[where].astype(jnp.float32) + more.astype(jnp.float32)).astype(jnp.bfloat16)

    def arrive(self, stage):
        arrive_all(self.copies(stage))
        place, rows = self.place, self.rows

        def block(z, carry):
            if stage == 0:
                for y in range(2):
                    for x in range(2):
                        self.add((y, z, x, rows, slice(None)), self.got[y, z, x, rows, :])
            elif stage == 1:
                for other in range(2):
                    if self.order == "yx":
                        self.add((place.y, z, other, rows, slice(None)), self.middle[z, other])
                    else:
                        self.add((other, z, place.x, rows, slice(None)), self.middle[other, z])
            else:
                self.add((place.y, z, place.x, rows, slice(None)), self.near[z])
            return carry

        lax.fori_loop(0, 4, block, 0)

    def result(self):
        arrive_all(self.copies(3))
        place = self.place
        own = self.held[place.y, place.z, place.x, self.rows, :].astype(jnp.float32)
        for step in range(3):
            own = own + self.last[step].astype(jnp.float32)
        return own

    def sent(self):
        for stage in range(4):
            sent_all(self.copies(stage))


def middle_shape(index):
    _, _, count, width, order = SUMMED[index]
    return (4, 2, count, width) if order == "yx" else (2, 4, count, width)


def tail_kernel(
    lengths_ref, qkv_ref, mixed_ref, gmixed_ref, total_ref, cos_ref, sin_ref, x_ref, small_ref, gy1_ref, sums_ref, in_ref,
    gout_hbm, gup_hbm, gdown_hbm, *refs,
):
    state, refs = refs[:12], refs[12:]
    grad_refs, (xgrad_ref, all_ref, norm_ref), refs = refs[:4], refs[4:7], refs[7:]
    gproj_ref, dk_ref, dv_ref, enter_t, away_in, small_acc, refs = *refs[:6], refs[6:]
    held, got, refs = refs[:4], refs[4:8], refs[8:]
    middle, near, last, refs = refs[:5], refs[5:10], refs[10:15], refs[15:]
    small_held, small_got, small_last, norm_held, norm_got, norm_last, refs = *refs[:6], refs[6:]
    send, recv, small_send, small_recv, norm_send, norm_recv, load_sem = refs
    bucket = pl.program_id(0)
    place = Place()
    sources = (None, gout_hbm, gup_hbm, gdown_hbm)

    def away(weight, width):
        if weight == 0:
            return lambda y, rows: away_in.at[y, :, :, rows, :]
        return lambda y, rows: sources[weight].at[:, :, rows, tile_cols(y * 2 + (1 - place.c), width)]

    def summing(which):
        return [
            Summing(
                index, place, away(SUMMED[index][0], SUMMED[index][3]), held[SUMMED[index][0]], got[SUMMED[index][0]],
                middle[index], near[index], last[index], send, recv,
            )
            for index in which
        ]

    early, late = summing((0, 1, 2)), summing((3, 4))
    small_sum = Everywhere(place, small_held, small_got, small_last, small_send, small_recv)
    norm_sum = Everywhere(place, norm_held, norm_got, norm_last, norm_send, norm_recv)

    def loads():
        found = []
        for weight, width in ((1, OUT_W), (2, FF_W), (3, FF_W)):
            for y in range(2):
                source = sources[weight].at[:, :, :, tile_cols(y * 2 + place.c, width)]
                found.append(pltpu.make_async_copy(source, held[weight].at[y], load_sem.at[weight - 1, y]))
        return found

    @pl.when(bucket == 0)
    def _():
        meet(place)
        for item in early:
            item.start(0)
        start_all(loads())
        for index in range(MICRO):

            def normalise(chunk, carry):
                rows = chunk_rows(chunk)
                cols = pl.ds(pl.multiple_of(index * LEN + chunk * BQ, BQ), BQ)
                enter_t[:, cols] = enter_rows(x_ref, small_ref, rows, index).T
                return carry

            lax.fori_loop(0, LEN // BQ, normalise, 0)

    shared = (qkv_ref, mixed_ref, gmixed_ref, total_ref, cos_ref, sin_ref, gproj_ref, dk_ref, dv_ref)
    attend_backward(lengths_ref, bucket, bucket, 0, 0, BQ, *shared)

    def later(step, carry):
        @pl.when((bucket == 0) & (step == 2))
        def _():
            for load in loads():
                load.wait()
            for item in early:
                item.arrive(0)
            for item in early:
                item.start(1)

        @pl.when((bucket == 1) & (step == 1))
        def _():
            for item in early:
                item.arrive(1)
            for item in early:
                item.start(2)

        @pl.when((bucket == 1) & (step == 3))
        def _():
            for item in early:
                item.arrive(2)
            for item in early:
                item.start(3)

        first_row = pl.multiple_of(step * BQ, BQ)
        attend_backward(lengths_ref, bucket, bucket, first_row, pl.multiple_of(first_row - BQ, BQ), 2 * BQ, *shared)
        return carry

    lax.fori_loop(1, LEN // BQ, later, 0)
    finish_keys(bucket, cos_ref, sin_ref, gproj_ref, dk_ref, dv_ref)

    @pl.when(bucket == 1)
    def _():
        def grad_tile(tensor):
            right = gproj_ref[:, :, tile_cols(tensor, IN_W)].reshape(MICRO * LEN, IN_W)
            return dot(enter_t[...], right).astype(jnp.bfloat16).reshape(4, 2, 64, IN_W)

        def tiles(step, carry):
            @pl.when(step < 2)
            def _():
                away_in[step] = grad_tile(step * 2 + 1 - place.c)

            @pl.when(step == 1)
            def _():
                for item in late:
                    item.start(0)

            @pl.when(step >= 2)
            def _():
                held[0][step - 2] = grad_tile((step - 2) * 2 + place.c)

            return carry

        lax.fori_loop(0, 4, tiles, 0)
        small_acc[...] = jnp.zeros_like(small_acc)
        in_full = in_ref[...]

        def data_grad(step, carry):
            for stage, moment in ((0, 1), (1, 4), (2, 7)):

                @pl.when(step == moment)
                def _():
                    for item in late:
                        item.arrive(stage)
                    for item in late:
                        item.start(stage + 1)

            index = step // (LEN // BQ)
            rows = chunk_rows(step % (LEN // BQ))
            grad_enter = dot(gproj_ref[index, rows, :], in_full, NT)
            normal, inverse = norm_parts(x_ref[index, rows, :].astype(jnp.float32))
            back = norm_back(grad_enter * small_ref[0:1, :], normal, inverse)
            xgrad_ref[index, rows, :] = (gy1_ref[index, rows, :] + back).astype(jnp.bfloat16)
            small_acc[0] += jnp.sum((grad_enter * normal).reshape(BQ // 8, 8, D), 0)
            small_acc[1] += jnp.sum(grad_enter.reshape(BQ // 8, 8, D), 0)
            return carry

        lax.fori_loop(0, MICRO * LEN // BQ, data_grad, 0)

        rows = [jnp.sum(small_acc[row], 0, keepdims=True) for row in range(2)]
        rows += [jnp.sum(sums_ref[row], 0, keepdims=True) for row in range(4)]
        weights_sq = []
        for which in range(4):
            weights_sq.append([state[3 * which][plane] * state[3 * which][plane] for plane in planes(which)])
        rows.append(sums_of_squares(weights_sq))
        rows.append(jnp.zeros((1, D), jnp.float32))
        small_held[0] = jnp.concatenate(rows, 0)
        small_sum.start(0)

        grads = [None, early[0].result().T, early[1].result(), early[2].result()]
        grad_refs[1][0] = grads[1][:HEAD_DIM]
        grad_refs[1][1] = grads[1][HEAD_DIM:]
        grad_refs[2][...] = grads[2]
        grad_refs[3][...] = grads[3]
        small_sum.step(0)
        parts = [item.result() for item in late]
        part = jnp.concatenate(parts, 0)
        for head in range(2):
            pieces = [part[:, which * 128 + head * HEAD_DIM : which * 128 + head * HEAD_DIM + HEAD_DIM] for which in range(3)]
            grad_refs[0][:, head, :] = jnp.concatenate(pieces, 1)
        updates_sq = []
        for which in range(4):
            squares = []
            for plane in planes(which):
                weight, first, second = (state[3 * which + kind][plane] for kind in range(3))
                update = moments(weight, grad_refs[which][plane], first, second)[2]
                squares.append(update * update)
            updates_sq.append(squares)
        norm_held[0] = jnp.broadcast_to(sums_of_squares(updates_sq)[:, :128], (8, 128))
        norm_sum.start(0)
        small_sum.step(1)
        norm_sum.step(0)
        small_sum.step(2)
        norm_sum.step(1)
        small_sum.step(3)
        norm_sum.step(2)
        norm_sum.step(3)
        all_ref[...] = small_sum.total()
        norm_ref[...] = norm_sum.total()
        for item in early + late:
            item.sent()
        small_sum.sent()
        norm_sum.sent()


def lamb_kernel(*refs):
    state, grads, refs = refs[:12], refs[12:16], refs[16:]
    small_ref, small_first_ref, small_second_ref, all_ref, norm_ref, refs = *refs[:5], refs[5:]
    outs, (grad_ref, new_ref, first_ref, second_ref, norms_ref) = refs[:16], refs[16:]
    weight_norm = jnp.sqrt(all_ref[6:7, 0:128])
    update_sq = norm_ref[0:1, :]
    ratio = learn_rate * weight_norm * lax.rsqrt(update_sq + 1e-12)
    for which in range(4):
        scale = ratio[:, which : which + 1]
        for plane in planes(which):
            weight, first, second = (state[3 * which + kind][plane] for kind in range(3))
            first, second, update = moments(weight, grads[which][plane], first, second)
            new = weight - scale * update
            outs[4 * which][plane] = new
            outs[4 * which + 1][plane] = first
            outs[4 * which + 2][plane] = second
            outs[4 * which + 3][plane] = new.astype(jnp.bfloat16)
    small = small_ref[...]
    small_grad = all_ref[0:6, :]
    grad_ref[...] = small_grad
    first, second, update = moments(small, small_grad, small_first_ref[...], small_second_ref[...])
    small_sq = jnp.sum(small * small, 1, keepdims=True)
    change_sq = jnp.sum(update * update, 1, keepdims=True)
    new_ref[...] = small - learn_rate * jnp.sqrt(small_sq) * lax.rsqrt(change_sq + 1e-12) * update
    first_ref[...] = first
    second_ref[...] = second
    lanes = lane_ids((1, 128))
    top = jnp.where(lanes < 4, weight_norm, 0.0)
    bottom = jnp.where(lanes < 4, jnp.sqrt(update_sq), 0.0)
    for row in range(6):
        top = top + jnp.where(lanes == 4 + row, jnp.sqrt(small_sq[row : row + 1]), 0.0)
        bottom = bottom + jnp.where(lanes == 4 + row, jnp.sqrt(change_sq[row : row + 1]), 0.0)
    norms_ref[0:1, :] = top[:, :10]
    norms_ref[1:2, :] = bottom[:, :10]


def whole(shape):
    return pl.BlockSpec(shape, lambda *ids: (0,) * len(shape), pipeline_mode=pl.Buffered(1))


def per_bucket(*shape):
    return pl.BlockSpec((1,) + shape, lambda b: (b, 0, 0))


def bf16(*shape):
    return jax.ShapeDtypeStruct(shape, jnp.bfloat16)


def f32(*shape):
    return jax.ShapeDtypeStruct(shape, jnp.float32)


def vmem16(*shape):
    return pltpu.VMEM(shape, jnp.bfloat16)


def vmem32(*shape):
    return pltpu.VMEM(shape, jnp.float32)


SCALARS = pl.BlockSpec(memory_space=pltpu.SMEM)
ANYWHERE = pl.BlockSpec(memory_space=pl.ANY)


def params(count, collective=None):
    more = {} if collective is None else dict(collective_id=collective, has_side_effects=True)
    return pltpu.CompilerParams(dimension_semantics=("arbitrary",) * count, vmem_limit_bytes=VMEM_LIMIT, **more)


def turn_tables(lengths):
    ends = jnp.cumsum(lengths, axis=1)
    position = jnp.arange(LEN, dtype=jnp.int32)
    passed = position[None, :, None] >= ends[:, None, : CLIPS - 1]
    start = jnp.max(jnp.where(passed, ends[:, None, : CLIPS - 1], 0), axis=2)
    offset = (position[None, :] - start).astype(jnp.float32)
    frequency = jnp.exp(jnp.arange(HEAD_DIM // 2, dtype=jnp.float32) * (-2.0 * math.log(10000.0) / HEAD_DIM))
    angles = offset[:, :, None] * frequency
    cosine = jnp.repeat(jnp.cos(angles), 2, axis=-1)
    sine = jnp.sin(angles)
    sine = jnp.stack([-sine, sine], axis=-1).reshape(cosine.shape)
    return jnp.concatenate([cosine, cosine], -1), jnp.concatenate([sine, sine], -1)


def attention_forward(lengths, x, small, cosine, sine, in_mat):
    count = x.shape[0]
    return pl.pallas_call(
        functools.partial(forward_kernel, alone=True),
        grid=(count,),
        in_specs=[SCALARS, per_bucket(LEN, D), whole((6, D)), per_bucket(LEN, 128), per_bucket(LEN, 128), whole((D, 3 * D))],
        out_specs=[per_bucket(LEN, 3 * D), per_bucket(LEN, D), per_bucket(LEN, D), per_bucket(LEN, D)],
        out_shape=[bf16(count, LEN, 3 * D), bf16(count, LEN, D), f32(count, LEN, D), bf16(count, LEN, D)],
        compiler_params=params(1),
        name="attention_forward",
    )(lengths, x, small, cosine, sine, in_mat)


def gather_forward(lengths, x, small, shard):
    shapes = [(4, 2, 64, 4 * width) for width in (IN_W, OUT_W, FF_W, FF_W)]
    return pl.pallas_call(
        functools.partial(forward_kernel, alone=False),
        grid=(MICRO,),
        in_specs=[SCALARS, per_bucket(LEN, D), whole((6, D)), whole((4, 32, 128)), whole((64, SHARD_W))],
        out_specs=[per_bucket(LEN, 3 * D), per_bucket(LEN, D), per_bucket(LEN, D)]
        + [whole((MICRO, LEN, 128))] * 2
        + [ANYWHERE] * 4,
        out_shape=[bf16(MICRO, LEN, 3 * D), bf16(MICRO, LEN, D), f32(MICRO, LEN, D)]
        + [f32(MICRO, LEN, 128)] * 2
        + [bf16(*shape) for shape in shapes],
        scratch_shapes=[vmem16(*shape) for shape in shapes]
        + [
            vmem16(1, LEN, D),
            pltpu.SemaphoreType.DMA((5, 8)),
            pltpu.SemaphoreType.DMA((5, 8)),
            pltpu.SemaphoreType.DMA((4,)),
            pltpu.SemaphoreType.DMA((4,)),
        ],
        compiler_params=params(1, 1),
        name="gather_forward",
    )(lengths, x, small, position_steps(), shard)


def mlp_both(lengths, x, cot, mixed, small, out_mat, up_mat, down_mat):
    count = x.shape[0]
    rows = count * LEN

    def chunked(width):
        return pl.BlockSpec((1, MLP_ROWS, width), lambda b, i: (b, i, 0))

    return pl.pallas_call(
        mlp_kernel,
        grid=(count, LEN // MLP_ROWS),
        in_specs=[SCALARS, chunked(D), chunked(D), chunked(D), whole((6, D)), whole((D, D)), whole((D, FF)), whole((D, FF))],
        out_specs=[chunked(D), chunked(D), chunked(D), whole((4, 8, D)), whole((D, D)), whole((D, FF)), whole((D, FF))],
        out_shape=[
            bf16(count, LEN, D), f32(count, LEN, D), bf16(count, LEN, D), f32(4, 8, D), bf16(D, D), bf16(D, FF), bf16(D, FF),
        ],
        scratch_shapes=[
            vmem16(rows, FF), vmem16(rows, FF), vmem16(rows, D), vmem16(D, rows), vmem16(D, rows), vmem16(D, rows),
        ],
        compiler_params=params(2),
        name="mlp_both",
    )(lengths, x, cot, mixed, small, out_mat, up_mat, down_mat)


def attention_backward(lengths, qkv, mixed, gmixed, totals, cosine, sine):
    count = qkv.shape[0]
    return pl.pallas_call(
        backward_kernel,
        grid=(count,),
        in_specs=[SCALARS, per_bucket(LEN, 3 * D), per_bucket(LEN, D), per_bucket(LEN, D), per_bucket(LEN, D), per_bucket(LEN, 128), per_bucket(LEN, 128)],
        out_specs=per_bucket(LEN, 3 * D),
        out_shape=bf16(count, LEN, 3 * D),
        scratch_shapes=[vmem32(LEN, D), vmem32(LEN, D)],
        compiler_params=params(1),
        name="attention_backward",
    )(lengths, qkv, mixed, gmixed, totals, cosine, sine)


def backward_tail(lengths, qkv, mixed, gmixed, totals, cosine, sine, x, small, gy1, sums, in_mat, gout, gup, gdown, state):
    widths = (IN_W, OUT_W, FF_W, FF_W)
    dma = pltpu.SemaphoreType.DMA
    grad_shapes = [f32(*state[3 * which].shape) for which in range(4)]
    return pl.pallas_call(
        tail_kernel,
        grid=(MICRO,),
        in_specs=[
            SCALARS, per_bucket(LEN, 3 * D), per_bucket(LEN, D), per_bucket(LEN, D), per_bucket(LEN, D),
            per_bucket(LEN, 128), per_bucket(LEN, 128), whole((MICRO, LEN, D)), whole((6, D)), whole((MICRO, LEN, D)),
            whole((4, 8, D)), whole((D, 3 * D)), ANYWHERE, ANYWHERE, ANYWHERE,
        ]
        + [whole(item.shape) for item in state],
        out_specs=[whole(item.shape) for item in grad_shapes] + [whole((MICRO, LEN, D)), whole((8, D)), whole((8, 128))],
        out_shape=grad_shapes + [bf16(MICRO, LEN, D), f32(8, D), f32(8, 128)],
        scratch_shapes=[
            vmem16(MICRO, LEN, 3 * D), vmem32(LEN, D), vmem32(LEN, D), vmem16(D, MICRO * LEN), vmem16(2, 4, 2, 64, IN_W), vmem32(2, 8, D),
        ]
        + [vmem16(2, 4, 2, 64, width) for width in widths]
        + [vmem16(2, 4, 2, 64, width) for width in widths]
        + [vmem16(*middle_shape(index)) for index in range(5)]
        + [vmem16(4, SUMMED[index][2], SUMMED[index][3]) for index in range(5)]
        + [vmem16(3, SUMMED[index][2], SUMMED[index][3]) for index in range(5)]
        + [vmem32(4, 8, D), vmem32(3, 8, D), vmem32(4, 8, D), vmem32(4, 8, 128), vmem32(3, 8, 128), vmem32(4, 8, 128)]
        + [dma((5, 7)), dma((5, 7)), dma((6,)), dma((6,)), dma((6,)), dma((6,)), dma((3, 2))],
        compiler_params=params(1, 2),
        name="backward_tail",
    )(lengths, qkv, mixed, gmixed, totals, cosine, sine, x, small, gy1, sums, in_mat, gout, gup, gdown, *state)


def lamb_all(state, grads, small, small_first, small_second, everything, norm_squares):
    outs = []
    for which in range(4):
        shape = state[3 * which].shape
        outs += [f32(*shape)] * 3 + [bf16(*shape)]
    outs += [f32(6, D)] * 4 + [f32(2, 10)]
    return pl.pallas_call(
        lamb_kernel,
        out_shape=outs,
        compiler_params=pltpu.CompilerParams(vmem_limit_bytes=VMEM_LIMIT),
        name="lamb_all",
    )(*state, *grads, small, small_first, small_second, everything, norm_squares)


def tile_shard(in_proj, out_proj, up_proj, down_proj, paired):
    depth, heads_here, _ = in_proj.shape
    in_cols = in_proj.reshape(depth, heads_here, 3, HEAD_DIM)
    if paired:
        in_cols = in_cols.transpose(0, 2, 1, 3)
    out_cols = out_proj.reshape(heads_here * HEAD_DIM, depth).T
    parts = [in_cols.reshape(depth, -1), out_cols, up_proj, down_proj.T]
    return jnp.concatenate(parts, axis=1).astype(jnp.bfloat16)


def on_device(
    frames, cotangent, clip_lengths, in_proj, out_proj, up_proj, down_proj, small_params,
    in_first, in_second, out_first, out_second, up_first, up_second, down_first, down_second,
    small_first, small_second,
):
    lengths = lax.dynamic_slice_in_dim(clip_lengths, lax.axis_index("tensor"), 1, 1).reshape(MICRO, CLIPS)
    shard = tile_shard(in_proj, out_proj, up_proj, down_proj, True)
    qkv, mixed, totals, cosine, sine, in_full, out_full, up_full, down_full = gather_forward(lengths, frames, small_params, shard)
    block_out, gy1, gmixed, sums, gout, gup, gdown = mlp_both(
        lengths, frames, cotangent, mixed, small_params, out_full.reshape(D, D), up_full.reshape(D, FF), down_full.reshape(D, FF)
    )
    state = (
        in_proj, in_first, in_second, out_proj, out_first, out_second, up_proj, up_first, up_second, down_proj.T, down_first.T, down_second.T,
    )
    *grads, input_grad, everything, norm_squares = backward_tail(
        lengths, qkv, mixed, gmixed, totals, cosine, sine, frames, small_params, gy1, sums, in_full.reshape(D, 3 * D),
        gout.reshape(4, 2, 64, D), gup.reshape(4, 2, 64, FF), gdown.reshape(4, 2, 64, FF), state,
    )
    outs = list(lamb_all(state, grads, small_params, small_first, small_second, everything, norm_squares))
    outs[12:16] = [item.T for item in outs[12:16]]
    return (block_out, input_grad, *outs)


def on_any_mesh(
    frames, cotangent, clip_lengths, in_proj, out_proj, up_proj, down_proj, small_params,
    in_first, in_second, out_first, out_second, up_first, up_second, down_first, down_second,
    small_first, small_second,
):
    rows_here = frames.shape[1]
    own_buckets = rows_here // LEN
    first_bucket = lax.axis_index("tensor") * own_buckets
    lengths = lax.dynamic_slice_in_dim(clip_lengths, first_bucket, own_buckets, 1).reshape(-1, CLIPS)
    count = MICRO * own_buckets
    x = frames.reshape(count, LEN, D)
    cot = cotangent.reshape(count, LEN, D)
    tensor_size = lax.axis_size("tensor")
    dp_size = lax.axis_size("dp")
    depth = in_proj.shape[0]
    heads_here = in_proj.shape[1]
    ff_here = up_proj.shape[1]

    shard = tile_shard(in_proj, out_proj, up_proj, down_proj, False)
    gathered = lax.all_gather(shard, ("dp", "tensor"), axis=0)
    gathered = gathered.reshape(dp_size, tensor_size, depth, shard.shape[1])
    gathered = jnp.moveaxis(gathered, 1, 2).reshape(D, tensor_size, shard.shape[1])
    edge0 = heads_here * 192
    edge1 = edge0 + heads_here * HEAD_DIM
    edge2 = edge1 + ff_here
    in_mat = gathered[:, :, :edge0].reshape(D, PAIRS, 2, 3, HEAD_DIM).transpose(0, 1, 3, 2, 4).reshape(D, 3 * D)
    out_mat = gathered[:, :, edge0:edge1].reshape(D, D)
    up_mat = gathered[:, :, edge1:edge2].reshape(D, FF)
    down_mat = gathered[:, :, edge2:].reshape(D, FF)

    cosine, sine = turn_tables(lengths)
    qkv, mixed, totals, enter1 = attention_forward(lengths, x, small_params, cosine, sine, in_mat)
    block_out, grad_y_first, grad_mixed, sums, grad_out, grad_upw, grad_down = mlp_both(
        lengths, x, cot, mixed, small_params, out_mat, up_mat, down_mat
    )

    def weight_grad(left, right):
        return dot(left.reshape(-1, left.shape[-1]), right.reshape(-1, right.shape[-1]), TN).astype(jnp.bfloat16)

    grad_proj = attention_backward(lengths, qkv, mixed, grad_mixed, totals, cosine, sine)
    grad_in = weight_grad(enter1, grad_proj)
    grad_in = grad_in.reshape(D, PAIRS, 3, 2, HEAD_DIM).transpose(0, 1, 3, 2, 4)

    def by_owner(mat):
        return jnp.moveaxis(mat.reshape(dp_size, depth, tensor_size, -1), 2, 1)

    stacked = jnp.concatenate([by_owner(grad_in), by_owner(grad_out), by_owner(grad_upw), by_owner(grad_down)], axis=-1)
    owned = lax.psum_scatter(
        stacked.reshape(dp_size * tensor_size, depth, -1), ("dp", "tensor"), scatter_dimension=0, tiled=False
    ).astype(jnp.float32)

    grad_enter1 = dot(grad_proj.reshape(-1, 3 * D), in_mat, NT).reshape(count, LEN, D)
    normal1, inverse1 = norm_parts(x.astype(jnp.float32))
    input_grad = (grad_y_first + norm_back(grad_enter1 * small_params[0], normal1, inverse1)).astype(jnp.bfloat16)
    late = jnp.sum(sums, axis=1)
    small_terms = jnp.stack(
        [jnp.sum(grad_enter1 * normal1, (0, 1)), jnp.sum(grad_enter1, (0, 1)), late[0], late[1], late[2], late[3]]
    )

    grads = (
        owned[:, :edge0].reshape(in_proj.shape),
        owned[:, edge0:edge1].T.reshape(out_proj.shape),
        owned[:, edge1:edge2],
        owned[:, edge2:].T,
    )
    weights_in = (in_proj, out_proj, up_proj, down_proj)
    firsts = (in_first, out_first, up_first, down_first)
    seconds = (in_second, out_second, up_second, down_second)
    own_squares = jnp.stack([jnp.sum(weight * weight) for weight in weights_in])
    small_grad, weight_squares = lax.psum((small_terms, own_squares), ("dp", "tensor"))
    new_firsts = []
    new_seconds = []
    updates = []
    for weight, gradient, first, second in zip(weights_in, grads, firsts, seconds):
        first = beta_first * first + (1.0 - beta_first) * gradient
        second = beta_second * second + (1.0 - beta_second) * gradient * gradient
        update = (
            first / (1.0 - beta_first**STEP) / (jnp.sqrt(second / (1.0 - beta_second**STEP)) + adam_eps)
            + decay_rate * weight
        )
        new_firsts.append(first)
        new_seconds.append(second)
        updates.append(update)
    update_squares = lax.psum(jnp.stack([jnp.sum(update * update) for update in updates]), ("dp", "tensor"))
    trust_ratio = jnp.sqrt(weight_squares) * lax.rsqrt(update_squares + 1e-12)
    new_weights = [weights_in[index] - learn_rate * trust_ratio[index] * updates[index] for index in range(4)]
    small_first_new = beta_first * small_first + (1.0 - beta_first) * small_grad
    small_second_new = beta_second * small_second + (1.0 - beta_second) * small_grad * small_grad
    small_update = (
        small_first_new / (1.0 - beta_first**STEP) / (jnp.sqrt(small_second_new / (1.0 - beta_second**STEP)) + adam_eps)
        + decay_rate * small_params
    )
    small_weight_sq = jnp.sum(small_params * small_params, axis=1, keepdims=True)
    small_update_sq = jnp.sum(small_update * small_update, axis=1, keepdims=True)
    small_new = small_params - learn_rate * jnp.sqrt(small_weight_sq) * lax.rsqrt(small_update_sq + 1e-12) * small_update
    norms = jnp.stack(
        [
            jnp.concatenate([jnp.sqrt(weight_squares), jnp.sqrt(small_weight_sq).reshape(-1)]),
            jnp.concatenate([jnp.sqrt(update_squares), jnp.sqrt(small_update_sq).reshape(-1)]),
        ]
    )
    outputs = [block_out.reshape(frames.shape), input_grad.reshape(frames.shape)]
    for new, first, second in zip(new_weights, new_firsts, new_seconds):
        outputs += [new, first, second, new.astype(jnp.bfloat16)]
    return tuple(outputs + [small_grad, small_new, small_first_new, small_second_new, norms])


def solution(mesh):
    rows = P(None, ("dp", "tensor"), None)
    in_spec = P("dp", "tensor", None)
    out_spec = P("tensor", None, "dp")
    up_spec = P("dp", "tensor")
    down_spec = P("tensor", "dp")
    shape = dict(mesh.shape)
    small_slice = shape["dp"] == HERE_DP and shape["tensor"] == HERE_TENSOR
    return jax.shard_map(
        on_device if small_slice else on_any_mesh,
        mesh=mesh,
        in_specs=(
            rows, rows, P(None, "dp", None), in_spec, out_spec, up_spec, down_spec, P(),
            in_spec, in_spec, out_spec, out_spec, up_spec, up_spec, down_spec, down_spec, P(), P(),
        ),
        out_specs=(rows, rows) + (in_spec,) * 4 + (out_spec,) * 4 + (up_spec,) * 4 + (down_spec,) * 4 + (P(),) * 5,
        check_vma=False,
    )
```

```python
import functools
import math

import jax
import jax.numpy as jnp
import numpy as np
from jax import lax
from jax.experimental import pallas as pl
from jax.experimental.pallas import tpu as pltpu
from jax.sharding import PartitionSpec as P

D = 512
HEADS = 8
HEAD_DIM = 64
FF = 2048
PAIRS = HEADS // 2
WINDOW = 250
LEN = 1024
CLIPS = 4
MICRO = 2
STEP = 3

BQ = 256
BH = 128
BLOCKS = LEN // BH
KEYS = 3 * BH
MLP_ROWS = 256
VMEM_LIMIT = 62 * 1024 * 1024

beta_first = 0.5
beta_second = 0.5
adam_eps = 1e-06
decay_rate = 0.01
learn_rate = 0.3

NT = (((1,), (1,)), ((), ()))
NN = (((1,), (0,)), ((), ()))
TN = (((0,), (0,)), ((), ()))


def dot(a, b, dims=NN):
    return lax.dot_general(a, b, dims, preferred_element_type=jnp.float32)


def norm_parts(rows):
    mean = jnp.mean(rows, -1, keepdims=True)
    centred = rows - mean
    inverse = lax.rsqrt(jnp.mean(centred * centred, -1, keepdims=True) + 1e-05)
    return centred * inverse, inverse


def norm_back(scaled, normal, inverse):
    return inverse * (
        scaled
        - jnp.mean(scaled, -1, keepdims=True)
        - normal * jnp.mean(scaled * normal, -1, keepdims=True)
    )


def lane_ids(shape):
    return lax.broadcasted_iota(jnp.int32, shape, len(shape) - 1)


def swap_pairs(rows):
    even = (lane_ids(rows.shape) & 1) == 0
    return jnp.where(even, pltpu.roll(rows, 127, 1), pltpu.roll(rows, 1, 1))


def run_starts(lengths_ref, bucket, position):
    end0 = lengths_ref[bucket, 0]
    end1 = end0 + lengths_ref[bucket, 1]
    end2 = end1 + lengths_ref[bucket, 2]
    start = jnp.where(position >= end0, end0, 0)
    start = jnp.where(position >= end1, end1, start)
    return jnp.where(position >= end2, end2, start), position < end2


def block_bias(lengths_ref, bucket, first_row, first_key, keys):
    position = first_row + lax.broadcasted_iota(jnp.int32, (BQ, 1), 0)
    start, _ = run_starts(lengths_ref, bucket, position)
    lowest = jnp.maximum(start, position - (WINDOW - 1))
    key = first_key + lax.broadcasted_iota(jnp.int32, (BQ, keys), 1)
    return jnp.where((key >= lowest) & (key <= position), 0.0, -1e30)


def head_lanes(tile, head):
    return jnp.where((lane_ids(tile.shape) // HEAD_DIM) == head, tile, jnp.zeros_like(tile))


MESH = pl.DeviceIdType.MESH
HERE_DP = 8
HERE_TENSOR = 4
IN_W, OUT_W, FF_W = 384, 128, 512
SHARD_W = IN_W + OUT_W + 2 * FF_W
CORE, ALONG_Y, ALONG_X = "core", "y", "x"

GATHERED = (
    (0, 0, 64, IN_W, 0, "xy"),
    (1, 0, 64, OUT_W, IN_W, "yx"),
    (2, 0, 32, FF_W, IN_W + OUT_W, "xy"),
    (3, 0, 32, FF_W, IN_W + OUT_W + FF_W, "yx"),
    (2, 32, 32, FF_W, IN_W + OUT_W, "xy"),
    (3, 32, 32, FF_W, IN_W + OUT_W + FF_W, "yx"),
)
IN, OUT, UP_A, DOWN_A, UP_B, DOWN_B = range(6)
SUMMED = (
    (1, 0, 64, OUT_W, "yx"),
    (2, 0, 64, FF_W, "yx"),
    (3, 0, 64, FF_W, "xy"),
    (0, 0, 32, IN_W, "xy"),
    (0, 32, 32, IN_W, "yx"),
)


class Place:
    def __init__(self):
        dp = lax.axis_index("dp")
        tensor = lax.axis_index("tensor")
        self.z, self.x = dp // 2, dp % 2
        self.y, self.c = tensor // 2, tensor % 2

    def device(self, dz=0, x=None, y=None, c=None):
        x = self.x if x is None else x
        y = self.y if y is None else y
        c = self.c if c is None else c
        return {"dp": (self.z + dz) % 4 * 2 + x, "tensor": y * 2 + c}

    def peers(self):
        return {
            CORE: self.device(c=1 - self.c),
            ALONG_Y: self.device(y=1 - self.y),
            ALONG_X: self.device(x=1 - self.x),
            1: self.device(dz=1),
            2: self.device(dz=2),
            3: self.device(dz=3),
        }


def tile_cols(slot, width):
    return pl.ds(pl.multiple_of(slot * width, 128), width)


def remote(source, target, send, recv, device):
    return pltpu.make_async_remote_copy(
        src_ref=source, dst_ref=target, send_sem=send, recv_sem=recv, device_id=device, device_id_type=MESH
    )


def meet(place):
    barrier = pltpu.get_barrier_semaphore()
    peers = place.peers()
    for device in peers.values():
        pl.semaphore_signal(barrier, inc=1, device_id=device, device_id_type=MESH)
    pl.semaphore_wait(barrier, len(peers))


def start_all(copies):
    for copy in copies:
        copy.start()


def arrive_all(copies):
    for copy in copies:
        copy.wait_recv()


def sent_all(copies):
    for copy in copies:
        copy.wait_send()


def gather_copies(index, stage, place, shard, weights, send, recv):
    weight, row, count, width, offset, order = GATHERED[index]
    full = weights[weight]
    rows = pl.ds(row, count)
    peers = place.peers()

    def copy(source, target, slot, peer):
        return remote(source, target, send.at[index, slot], recv.at[index, slot], peers[peer])

    def cols(slot):
        return slice(slot * width, slot * width + width)

    if stage == 0:
        return [
            copy(shard.at[rows, offset : offset + width], full.at[place.z, place.x, rows, cols(0)], step - 1, step)
            for step in (1, 2, 3)
        ]
    if stage == 1:
        part = full.at[:, place.x, rows, cols(0)]
        if order == "xy":
            return [copy(part, part, 3, ALONG_X)]
        return [copy(part, full.at[:, place.x, rows, cols(2)], 3, ALONG_Y)]
    if stage == 2:
        if order == "xy":
            return [copy(full.at[:, :, rows, cols(0)], full.at[:, :, rows, cols(2)], 4, ALONG_Y)]
        parts = [full.at[:, place.x, rows, cols(slot)] for slot in (0, 2)]
        return [copy(part, part, 4 + index, ALONG_X) for index, part in enumerate(parts)]
    slot = stage * 2 - 6
    return [copy(full.at[:, :, rows, cols(slot)], full.at[:, :, rows, cols(slot + 1)], stage + 3, CORE)]


def project_rows(rows, enter, cosine, sine, weight, qkv_ref, base):
    part = dot(enter, weight)
    for which in range(2):
        piece = part[:, which * 128 : which * 128 + 128]
        turned = piece * cosine + swap_pairs(piece) * sine
        if which == 0:
            turned = turned * (HEAD_DIM**-0.5)
        qkv_ref[0, rows, base + which * 128 : base + which * 128 + 128] = turned.astype(jnp.bfloat16)
    qkv_ref[0, rows, base + 256 : base + 384] = part[:, 256:].astype(jnp.bfloat16)


def attend_forward(lengths_ref, bucket, first_row, first_key, keys, qkv_ref, mixed_ref, total_ref):
    rows = pl.ds(first_row, BQ)
    key_rows = pl.ds(first_key, keys)
    bias = block_bias(lengths_ref, bucket, first_row, first_key, keys)
    for pair in range(PAIRS):
        base = pair * 384
        queries = qkv_ref[0, rows, base : base + 128]
        keys_rot = qkv_ref[0, key_rows, base + 128 : base + 256]
        values = qkv_ref[0, key_rows, base + 256 : base + 384]
        outs = []
        totals = []
        for head in range(2):
            scores = dot(head_lanes(queries, head), keys_rot, NT) + bias
            top = jnp.max(scores, -1, keepdims=True)
            powers = jnp.exp(scores - top)
            total = jnp.sum(powers, -1, keepdims=True)
            outs.append(dot(powers.astype(jnp.bfloat16), values) / total)
            totals.append(jnp.broadcast_to(top + jnp.log(total), (BQ, 128)))
        low = lane_ids((BQ, 128)) < HEAD_DIM
        mixed_ref[0, rows, pair * 128 : pair * 128 + 128] = jnp.where(low, outs[0], outs[1]).astype(jnp.bfloat16)
        total_ref[0, rows, pair * 128 : pair * 128 + 128] = jnp.where(low, totals[0], totals[1])


def turn_tables_here(lengths_ref, steps_ref, cos_ref, sin_ref):
    lanes = lane_ids((8, 128))
    frequency = jnp.exp(((lanes & (HEAD_DIM - 1)) // 2).astype(jnp.float32) * (-2.0 * math.log(10000.0) / HEAD_DIM))
    sign = jnp.where((lane_ids((1, 128)) & 1) == 0, -1.0, 1.0)
    fine_cos, fine_sin = steps_ref[2:3], steps_ref[3:4]
    for bucket in range(MICRO):
        end0 = lengths_ref[bucket, 0]
        end1 = end0 + lengths_ref[bucket, 1]
        end2 = end1 + lengths_ref[bucket, 2]
        row = lax.broadcasted_iota(jnp.int32, (8, 128), 0)
        start = jnp.where(row == 0, 0, jnp.where(row == 1, end0, jnp.where(row == 2, end1, end2)))
        angle = start.astype(jnp.float32) * frequency
        run_cos, run_sin = jnp.cos(angle), jnp.sin(angle)

        def chunk_tables(chunk, carry):
            coarse = pl.ds(pl.multiple_of(chunk * 8, 8), 8)
            coarse_cos, coarse_sin = steps_ref[0, coarse, :][:, None, :], steps_ref[1, coarse, :][:, None, :]
            at_cos = (coarse_cos * fine_cos - coarse_sin * fine_sin).reshape(BQ, 128)
            at_sin = (coarse_sin * fine_cos + coarse_cos * fine_sin).reshape(BQ, 128)
            position = chunk * BQ + lax.broadcasted_iota(jnp.int32, (BQ, 128), 0)
            first_cos, first_sin = run_cos[0:1], run_sin[0:1]
            for run, end in enumerate((end0, end1, end2)):
                first_cos = jnp.where(position >= end, run_cos[run + 1 : run + 2], first_cos)
                first_sin = jnp.where(position >= end, run_sin[run + 1 : run + 2], first_sin)
            rows = chunk_rows(chunk)
            cos_ref[bucket, rows, :] = at_cos * first_cos + at_sin * first_sin
            sin_ref[bucket, rows, :] = (at_sin * first_cos - at_cos * first_sin) * sign
            return carry

        lax.fori_loop(0, LEN // BQ, chunk_tables, 0)


def position_steps():
    lane = np.arange(128) % HEAD_DIM // 2
    frequency = np.exp(lane.astype(np.float32) * np.float32(-2.0 * math.log(10000.0) / HEAD_DIM)).astype(np.float64)
    step = np.arange(32)[:, None]
    coarse, fine = step * 32 * frequency, step * frequency
    return jnp.asarray(np.stack([np.cos(coarse), np.sin(coarse), np.cos(fine), np.sin(fine)]).astype(np.float32))


def enter_rows(x_ref, small_ref, rows, bucket=0):
    normal, _ = norm_parts(x_ref[bucket, rows, :].astype(jnp.float32))
    return (normal * small_ref[0:1, :] + small_ref[1:2, :]).astype(jnp.bfloat16)


def chunk_rows(chunk):
    return pl.ds(pl.multiple_of(chunk * BQ, BQ), BQ)


def forward_kernel(lengths_ref, x_ref, small_ref, cos_ref, sin_ref, in_ref, qkv_ref, mixed_ref, total_ref, enter_ref):
    bucket = pl.program_id(0)

    def project(chunk, carry):
        rows = chunk_rows(chunk)
        enter_ref[0, rows, :] = enter_rows(x_ref, small_ref, rows)
        for pair in range(PAIRS):
            weight = in_ref[:, pair * 384 : pair * 384 + 384]
            project_rows(rows, enter_ref[0, rows, :], cos_ref[0, rows, :], sin_ref[0, rows, :], weight, qkv_ref, pair * 384)
        return carry

    lax.fori_loop(0, LEN // BQ, project, 0)
    attend_forward(lengths_ref, bucket, 0, 0, BQ, qkv_ref, mixed_ref, total_ref)

    def later(step, carry):
        first_row = pl.multiple_of(step * BQ, BQ)
        attend_forward(lengths_ref, bucket, first_row, pl.multiple_of(first_row - BQ, BQ), 2 * BQ, qkv_ref, mixed_ref, total_ref)
        return carry

    lax.fori_loop(1, LEN // BQ, later, 0)


class RunLengths:
    def __init__(self, ref):
        self.ref, self.own = ref, lax.axis_index("tensor")

    def __getitem__(self, where):
        bucket, run = where
        return self.ref[bucket, self.own, run]


def band_biases(lengths, bias_ref):
    def fill(index, carry):
        bucket, block = index // BLOCKS, index % BLOCKS
        position = block * BH + lax.broadcasted_iota(jnp.int32, (BH, 1), 0)
        start, _ = run_starts(lengths, bucket, position)
        lowest = jnp.maximum(start, position - (WINDOW - 1))
        key = jnp.maximum(block - 2, 0) * BH + lax.broadcasted_iota(jnp.int32, (BH, KEYS), 1)
        bias_ref[bucket, block] = jnp.where((key >= lowest) & (key <= position), 0.0, -1e30)
        return carry

    lax.fori_loop(0, MICRO * BLOCKS, fill, 0)


def block_span(block):
    first = max(block - 2, 0)
    return slice(block * BH, block * BH + BH), slice(first * BH, block * BH + BH), (block + 1 - first) * BH


def both_heads(tile):
    return jnp.concatenate([head_lanes(tile, 0), head_lanes(tile, 1)], 0)


def each_head(rows):
    return jnp.where(lane_ids((BH, 128)) < HEAD_DIM, rows[:BH], rows[BH:])


def attend_pair(bias_ref, bucket, block, qkv_ref, mixed_ref, total_ref):
    rows, key_rows, keys = block_span(block)
    bias = bias_ref[bucket, block, :, :keys]
    scores = dot(both_heads(qkv_ref[0, rows, :128]), qkv_ref[0, key_rows, 128:256], NT)
    scores = scores + jnp.concatenate([bias, bias], 0)
    top = jnp.max(scores, -1, keepdims=True)
    powers = jnp.exp(scores - top)
    total = jnp.sum(powers, -1, keepdims=True)
    out = dot(powers.astype(jnp.bfloat16), qkv_ref[0, key_rows, 256:384]) / total
    mixed_ref[0, rows, :] = each_head(out).astype(jnp.bfloat16)
    total_ref[0, rows, :] = each_head(jnp.broadcast_to(top + jnp.log(total), (2 * BH, 128)))


def gather_kernel(
    lengths_ref, x_ref, small_ref, steps_ref, in_ref, out_ref, up_ref, down_ref,
    qkv_ref, mixed_ref, total_ref, cos_ref, sin_ref, *refs,
):
    kept, full, refs = refs[:4], refs[4:8], refs[8:]
    shard_ref, enter_ref, bias_ref, send, recv, own_sem, keep_sem = refs
    bucket = pl.program_id(1)
    step = pl.program_id(0) * MICRO + bucket
    place = Place()

    def copies(stage, which):
        found = []
        for index in which:
            found += gather_copies(index, stage, place, shard_ref, full, send, recv)
        return found

    def start(stage, *which):
        start_all(copies(stage, which))

    def arrive(stage, *which):
        arrive_all(copies(stage, which))

    def own_tiles():
        tiles = []
        for weight, width, offset in ((0, IN_W, 0), (1, OUT_W, IN_W), (2, FF_W, IN_W + OUT_W), (3, FF_W, IN_W + OUT_W + FF_W)):
            target = full[weight].at[place.z, place.x, :, 0:width]
            tiles.append(pltpu.make_async_copy(shard_ref.at[:, offset : offset + width], target, own_sem.at[weight]))
        return tiles

    def keep(index):
        weight, row, count = GATHERED[index][:3]
        rows = pl.ds(row, count)
        return pltpu.make_async_copy(full[weight].at[:, :, rows, :], kept[weight].at[:, :, rows, :], keep_sem.at[index])

    def finish(*which):
        arrive(3, *which)
        arrive(4, *which)
        for index in which:
            keep(index).start()

    def begin():
        lengths = RunLengths(lengths_ref)
        heads = [in_ref[:, head, :] for head in range(2)]
        pieces = [heads[head][:, part * HEAD_DIM : part * HEAD_DIM + HEAD_DIM] for part in range(3) for head in range(2)]
        shard_ref[:, :IN_W] = jnp.concatenate(pieces, 1).astype(jnp.bfloat16)
        shard_ref[:, IN_W : IN_W + OUT_W] = jnp.concatenate([out_ref[0].T, out_ref[1].T], 1).astype(jnp.bfloat16)
        shard_ref[:, IN_W + OUT_W : IN_W + OUT_W + FF_W] = up_ref[...].astype(jnp.bfloat16)
        shard_ref[:, IN_W + OUT_W + FF_W :] = down_ref[...].astype(jnp.bfloat16)
        meet(place)
        start(0, IN)
        start(0, OUT, UP_A, DOWN_A, UP_B, DOWN_B)
        start_all(own_tiles())
        turn_tables_here(lengths, steps_ref, cos_ref, sin_ref)

        def normalise(index, carry):
            rows = chunk_rows(index % (LEN // BQ))
            enter_ref[index // (LEN // BQ), rows, :] = enter_rows(x_ref, small_ref, rows, index // (LEN // BQ))
            return carry

        lax.fori_loop(0, MICRO * LEN // BQ, normalise, 0)
        for tile in own_tiles():
            tile.wait()
        arrive(0, IN)
        start(1, IN)
        arrive(0, OUT)
        start(1, OUT)
        band_biases(lengths, bias_ref)
        arrive(1, IN)

    def at_0_1():
        arrive(0, UP_A, DOWN_A)
        start(1, DOWN_A, UP_A)
        start(2, IN)
        start(3, IN)
        arrive(1, OUT)
        start(2, OUT)

    def at_2_0():
        arrive(3, IN)

    def at_2_1():
        arrive(0, UP_B, DOWN_B)
        start(1, DOWN_B, UP_B)

    def at_2_2():
        arrive(1, DOWN_A, UP_A)
        start(2, DOWN_A, UP_A)
        start(3, UP_A)

    def at_4_0():
        arrive(2, IN)
        start(4, IN)

    def at_5_2():
        arrive(1, DOWN_B, UP_B)
        start(2, DOWN_B, UP_B)
        start(3, UP_B)

    def at_6_0():
        arrive(4, IN)
        keep(IN).start()

    def at_6_1():
        arrive(2, OUT, DOWN_A)
        start(3, OUT, DOWN_A)
        start(4, OUT, DOWN_A)

    def at_7_1():
        arrive(2, UP_A)
        start(4, UP_A)

    def at_7_3():
        finish(OUT, DOWN_A)

    events = {
        (0, 0): begin, (0, 1): at_0_1, (2, 0): at_2_0, (2, 1): at_2_1, (2, 2): at_2_2, (4, 0): at_4_0,
        (5, 2): at_5_2, (6, 0): at_6_0, (6, 1): at_6_1, (7, 1): at_7_1, (7, 3): at_7_3,
    }

    def progress(point):
        for (moment, where), event in events.items():
            if where == point:
                pl.when(step == moment)(event)

    progress(0)
    weight = full[0][:, :, :, tile_cols(pl.program_id(0), IN_W)].reshape(D, IN_W)

    def project(chunk, carry):
        rows = chunk_rows(chunk)
        project_rows(rows, enter_ref[bucket, rows, :], cos_ref[bucket, rows, :], sin_ref[bucket, rows, :], weight, qkv_ref, 0)
        return carry

    lax.fori_loop(0, LEN // BQ, project, 0)
    for point, blocks in enumerate(((0, 1, 2), (3, 4, 5), (6, 7))):
        progress(point + 1)
        for block in blocks:
            attend_pair(bias_ref, bucket, block, qkv_ref, mixed_ref, total_ref)

    @pl.when(step == PAIRS * MICRO - 1)
    def _():
        arrive(2, DOWN_B)
        start(3, DOWN_B)
        start(4, DOWN_B)
        arrive(2, UP_B)
        start(4, UP_B)
        finish(UP_A)
        finish(DOWN_B, UP_B)
        for index in range(len(GATHERED)):
            keep(index).wait()
        for stage in range(5):
            sent_all(copies(stage, range(len(GATHERED))))


def mlp_kernel(
    lengths_ref, x_ref, cot_ref, mixed_ref, small_ref, out_ref, up_ref, down_ref,
    block_ref, gy1_ref, gmixed_ref, sums_ref, gout_ref, gup_out_ref, gdown_ref,
    act_ref, gup_ref, keep_ref, enter_t, gmlp_t, gbranch_t,
):
    lengths = RunLengths(lengths_ref) if len(lengths_ref.shape) == 3 else lengths_ref
    bucket = pl.program_id(0)
    chunk = pl.program_id(1)
    buckets = pl.num_programs(0)
    chunks = pl.num_programs(1)

    @pl.when((bucket == 0) & (chunk == 0))
    def _():
        sums_ref[...] = jnp.zeros_like(sums_ref)

    index = bucket * chunks + chunk
    rows = pl.ds(pl.multiple_of(index * MLP_ROWS, MLP_ROWS), MLP_ROWS)
    small = [small_ref[row : row + 1, :] for row in range(6)]
    x = x_ref[0].astype(jnp.float32)
    mixed = mixed_ref[0]
    keep_ref[rows, :] = mixed
    branch = dot(mixed, out_ref[...], NT)
    y_first = x + small[4] * branch
    normal, inverse = norm_parts(y_first)
    enter = (normal * small[2] + small[3]).astype(jnp.bfloat16)
    enter_t[:, rows] = enter.T
    position = chunk * MLP_ROWS + lax.broadcasted_iota(jnp.int32, (MLP_ROWS, 1), 0)
    _, valid = run_starts(lengths, bucket, position)
    grad_y = jnp.where(valid, cot_ref[0].astype(jnp.float32), 0.0)
    grad_mlp = (small[5] * grad_y).astype(jnp.bfloat16)
    gmlp_t[:, rows] = grad_mlp.T
    mlp = jnp.zeros((MLP_ROWS, D), jnp.float32)
    grad_enter = jnp.zeros((MLP_ROWS, D), jnp.float32)
    for part in range(FF // 512):
        cols = slice(part * 512, part * 512 + 512)
        upval = dot(enter, up_ref[:, cols])
        grad_act = dot(grad_mlp, down_ref[:, cols])
        cumulative = 0.5 + 0.5 * lax.erf(upval * (1.0 / math.sqrt(2.0)))
        act = (upval * cumulative).astype(jnp.bfloat16)
        act_ref[rows, cols] = act
        density = jnp.exp(-0.5 * upval * upval) * (1.0 / math.sqrt(2.0 * math.pi))
        grad_up = (grad_act * (cumulative + upval * density)).astype(jnp.bfloat16)
        gup_ref[rows, cols] = grad_up
        mlp = mlp + dot(act, down_ref[:, cols], NT)
        grad_enter = grad_enter + dot(grad_up, up_ref[:, cols], NT)
    block_ref[0] = (y_first + small[5] * mlp).astype(jnp.bfloat16)
    grad_y_first = grad_y + norm_back(grad_enter * small[2], normal, inverse)
    gy1_ref[0] = grad_y_first
    grad_branch = (small[4] * grad_y_first).astype(jnp.bfloat16)
    gbranch_t[:, rows] = grad_branch.T
    gmixed_ref[0] = dot(grad_branch, out_ref[...]).astype(jnp.bfloat16)

    def fold(terms):
        return jnp.sum(terms.reshape(MLP_ROWS // 8, 8, D), 0)

    sums_ref[0] += fold(grad_enter * normal)
    sums_ref[1] += fold(grad_enter)
    sums_ref[2] += fold(grad_y_first * branch)
    sums_ref[3] += fold(grad_y * mlp)

    @pl.when(index == buckets * chunks - 1)
    def _():
        gout_ref[...] = dot(gbranch_t[...], keep_ref[...]).astype(jnp.bfloat16)

        def weight_grads(part, carry):
            cols = pl.ds(pl.multiple_of(part * 256, 256), 256)
            gup_out_ref[:, cols] = dot(enter_t[...], gup_ref[:, cols]).astype(jnp.bfloat16)
            gdown_ref[:, cols] = dot(gmlp_t[...], act_ref[:, cols]).astype(jnp.bfloat16)
            return carry

        lax.fori_loop(0, FF // 256, weight_grads, 0)


def attend_backward(
    lengths_ref, bucket, slot, first_row, first_key, keys, qkv_ref, mixed_ref, gmixed_ref, total_ref, cos_ref, sin_ref, gproj_ref, dk_ref, dv_ref
):
    rows = pl.ds(first_row, BQ)
    key_rows = pl.ds(first_key, keys)
    bias = block_bias(lengths_ref, bucket, first_row, first_key, keys)
    low = lane_ids((BQ, 128)) < HEAD_DIM
    for pair in range(PAIRS):
        base = pair * 384
        queries = qkv_ref[0, rows, base : base + 128]
        keys_rot = qkv_ref[0, key_rows, base + 128 : base + 256]
        values = qkv_ref[0, key_rows, base + 256 : base + 384]
        grad = gmixed_ref[0, rows, pair * 128 : pair * 128 + 128]
        totals = total_ref[0, rows, pair * 128 : pair * 128 + 128]
        product = grad.astype(jnp.float32) * mixed_ref[0, rows, pair * 128 : pair * 128 + 128].astype(jnp.float32)
        grad_q = jnp.zeros((BQ, 128), jnp.float32)
        grad_k = jnp.zeros((keys, 128), jnp.float32)
        grad_v = jnp.zeros((keys, 128), jnp.float32)
        for head in range(2):
            query = head_lanes(queries, head)
            grad_head = head_lanes(grad, head)
            inner = jnp.sum(jnp.where(low == (head == 0), product, 0.0), -1, keepdims=True)
            total = totals[:, head * HEAD_DIM : head * HEAD_DIM + 1]
            attn = jnp.exp(dot(query, keys_rot, NT) + bias - total)
            grad_attn = dot(grad_head, values, NT)
            grad_scores = (attn * (grad_attn - inner)).astype(jnp.bfloat16)
            grad_v = grad_v + dot(attn.astype(jnp.bfloat16), grad_head, TN)
            grad_k = grad_k + dot(grad_scores, query, TN)
            grad_q = grad_q + dot(grad_scores, head_lanes(keys_rot, head))
        cosine = cos_ref[0, rows, :]
        sine = sin_ref[0, rows, :]
        grad_q = grad_q * (HEAD_DIM**-0.5)
        gproj_ref[slot, rows, base : base + 128] = (grad_q * cosine - swap_pairs(grad_q) * sine).astype(jnp.bfloat16)
        lanes = slice(pair * 128, pair * 128 + 128)
        if keys > BQ:
            before = pl.ds(first_key, BQ)
            dk_ref[before, lanes] += grad_k[:BQ]
            dv_ref[before, lanes] += grad_v[:BQ]
            dk_ref[rows, lanes] = grad_k[BQ:]
            dv_ref[rows, lanes] = grad_v[BQ:]
        else:
            dk_ref[rows, lanes] = grad_k
            dv_ref[rows, lanes] = grad_v


def finish_keys(slot, cos_ref, sin_ref, gproj_ref, dk_ref, dv_ref):
    def finish(chunk, carry):
        rows = chunk_rows(chunk)
        cosine = cos_ref[0, rows, :]
        sine = sin_ref[0, rows, :]
        for pair in range(PAIRS):
            grad_k = dk_ref[rows, pair * 128 : pair * 128 + 128]
            turned = grad_k * cosine - swap_pairs(grad_k) * sine
            gproj_ref[slot, rows, pair * 384 + 128 : pair * 384 + 256] = turned.astype(jnp.bfloat16)
            gproj_ref[slot, rows, pair * 384 + 256 : pair * 384 + 384] = dv_ref[rows, pair * 128 : pair * 128 + 128].astype(jnp.bfloat16)
        return carry

    lax.fori_loop(0, LEN // BQ, finish, 0)


def backward_kernel(lengths_ref, qkv_ref, mixed_ref, gmixed_ref, total_ref, cos_ref, sin_ref, gproj_ref, dk_ref, dv_ref):
    bucket = pl.program_id(0)
    shared = (qkv_ref, mixed_ref, gmixed_ref, total_ref, cos_ref, sin_ref, gproj_ref, dk_ref, dv_ref)
    attend_backward(lengths_ref, bucket, 0, 0, 0, BQ, *shared)

    def later(step, carry):
        first_row = pl.multiple_of(step * BQ, BQ)
        attend_backward(lengths_ref, bucket, 0, first_row, pl.multiple_of(first_row - BQ, BQ), 2 * BQ, *shared)
        return carry

    lax.fori_loop(1, LEN // BQ, later, 0)
    finish_keys(0, cos_ref, sin_ref, gproj_ref, dk_ref, dv_ref)


def moments(weight, gradient, first, second):
    first = beta_first * first + (1.0 - beta_first) * gradient
    second = beta_second * second + (1.0 - beta_second) * gradient * gradient
    update = (
        first / (1.0 - beta_first**STEP) / (jnp.sqrt(second / (1.0 - beta_second**STEP)) + adam_eps)
        + decay_rate * weight
    )
    return first, second, update


def planes(which):
    if which == 0:
        return [(slice(None), head, slice(None)) for head in range(2)]
    if which == 1:
        return [(head, slice(None), slice(None)) for head in range(2)]
    return [(slice(None), slice(None))]


def total_of(values_in):
    return jnp.sum(jnp.sum(values_in, 1, keepdims=True), 0, keepdims=True)


def sums_of_squares(tables):
    lanes = lane_ids((1, 512))
    row = jnp.zeros((1, 512), jnp.float32)
    for which, squares in enumerate(tables):
        amount = sum((total_of(plane) for plane in squares[1:]), total_of(squares[0]))
        row = row + jnp.where(lanes == which, amount, 0.0)
    return row


class Everywhere:
    def __init__(self, place, held, got, last, send, recv):
        self.place, self.held, self.got, self.last = place, held, got, last
        self.send, self.recv = send, recv

    def copies(self, stage):
        peers = self.place.peers()
        if stage < 3:
            peer = (CORE, ALONG_Y, ALONG_X)[stage]
            return [remote(self.held.at[stage], self.got.at[stage], self.send.at[stage], self.recv.at[stage], peers[peer])]
        return [
            remote(self.held.at[3], self.last.at[self.place.z], self.send.at[2 + step], self.recv.at[2 + step], peers[step])
            for step in (1, 2, 3)
        ]

    def start(self, stage):
        start_all(self.copies(stage))

    def step(self, stage):
        arrive_all(self.copies(stage))
        if stage == 3:
            return
        total = self.held[stage] + self.got[stage]
        self.held[stage + 1] = total
        if stage == 2:
            self.last[self.place.z] = total
        self.start(stage + 1)

    def total(self):
        return (self.last[0] + self.last[1]) + (self.last[2] + self.last[3])

    def sent(self):
        for stage in range(4):
            sent_all(self.copies(stage))


class Summing:
    def __init__(self, index, place, away, held, got, middle, near, last, send, recv):
        self.weight, self.row, self.count, self.width, self.order = SUMMED[index]
        self.index, self.place = index, place
        self.away, self.held, self.got = away, held, got
        self.middle, self.near, self.last = middle, near, last
        self.send, self.recv = send, recv
        self.rows = pl.ds(self.row, self.count)

    def copies(self, stage):
        place = self.place
        peers = place.peers()

        def copy(source, target, slot, peer):
            return remote(source, target, self.send.at[self.index, slot], self.recv.at[self.index, slot], peers[peer])

        held, rows = self.held, self.rows
        if stage == 0:
            return [copy(self.away(y, rows), self.got.at[y, :, :, rows, :], y, CORE) for y in range(2)]
        if stage == 1:
            if self.order == "yx":
                return [copy(held.at[1, :, :, rows, :], self.middle, 2, ALONG_Y)]
            return [copy(held.at[:, :, 1 - place.x, rows, :], self.middle, 2, ALONG_X)]
        if stage == 2:
            if self.order == "yx":
                return [copy(held.at[0, :, 1 - place.x, rows, :], self.near, 3, ALONG_X)]
            return [copy(held.at[1, :, place.x, rows, :], self.near, 3, ALONG_Y)]
        return [
            copy(held.at[0, (place.z + step) % 4, place.x, rows, :], self.last.at[step - 1], 3 + step, step)
            for step in (1, 2, 3)
        ]

    def start(self, stage):
        start_all(self.copies(stage))

    def add(self, where, more):
        held = self.held
        held[where] = (held[where].astype(jnp.float32) + more.astype(jnp.float32)).astype(jnp.bfloat16)

    def arrive(self, stage):
        arrive_all(self.copies(stage))
        place, rows = self.place, self.rows

        def block(z, carry):
            if stage == 0:
                for y in range(2):
                    for x in range(2):
                        self.add((y, z, x, rows, slice(None)), self.got[y, z, x, rows, :])
            elif stage == 1:
                for other in range(2):
                    if self.order == "yx":
                        self.add((0, z, other, rows, slice(None)), self.middle[z, other])
                    else:
                        self.add((other, z, place.x, rows, slice(None)), self.middle[other, z])
            else:
                self.add((0, z, place.x, rows, slice(None)), self.near[z])
            return carry

        lax.fori_loop(0, 4, block, 0)

    def result(self):
        arrive_all(self.copies(3))
        place = self.place
        own = self.held[0, place.z, place.x, self.rows, :].astype(jnp.float32)
        for step in range(3):
            own = own + self.last[step].astype(jnp.float32)
        return own

    def sent(self):
        for stage in range(4):
            sent_all(self.copies(stage))


def middle_shape(index):
    _, _, count, width, order = SUMMED[index]
    return (4, 2, count, width) if order == "yx" else (2, 4, count, width)


def tail_kernel(
    lengths_ref, qkv_ref, mixed_ref, gmixed_ref, total_ref, cos_ref, sin_ref, x_ref, small_ref, gy1_ref, sums_ref, in_ref,
    gout_hbm, gup_hbm, gdown_hbm, *refs,
):
    state, refs = refs[:12], refs[12:]
    grad_refs, (xgrad_ref, all_ref, norm_ref), refs = refs[:4], refs[4:7], refs[7:]
    gproj_ref, dk_ref, dv_ref, enter_t, away_in, small_acc, refs = *refs[:6], refs[6:]
    held, got, refs = refs[:4], refs[4:8], refs[8:]
    middle, near, last, refs = refs[:5], refs[5:10], refs[10:15], refs[15:]
    small_held, small_got, small_last, norm_held, norm_got, norm_last, refs = *refs[:6], refs[6:]
    send, recv, small_send, small_recv, norm_send, norm_recv, load_sem = refs
    lengths = RunLengths(lengths_ref)
    bucket = pl.program_id(0)
    place = Place()
    sources = (None, gout_hbm, gup_hbm, gdown_hbm)

    def away(weight, width):
        if weight == 0:
            return lambda y, rows: away_in.at[y, :, :, rows, :]
        return lambda y, rows: sources[weight].at[:, :, rows, tile_cols(y * 2 + 1, width)]

    def summing(which):
        return [
            Summing(
                index, place, away(SUMMED[index][0], SUMMED[index][3]), held[SUMMED[index][0]], got[SUMMED[index][0]],
                middle[index], near[index], last[index], send, recv,
            )
            for index in which
        ]

    early, late = summing((0, 1, 2)), summing((3, 4))
    small_sum = Everywhere(place, small_held, small_got, small_last, small_send, small_recv)
    norm_sum = Everywhere(place, norm_held, norm_got, norm_last, norm_send, norm_recv)

    def loads():
        found = []
        for weight, width in ((1, OUT_W), (2, FF_W), (3, FF_W)):
            for y in range(2):
                source = sources[weight].at[:, :, :, tile_cols(y * 2, width)]
                found.append(pltpu.make_async_copy(source, held[weight].at[y], load_sem.at[weight - 1, y]))
        return found

    @pl.when(bucket == 0)
    def _():
        meet(place)
        for item in early:
            item.start(0)
        start_all(loads())
        for index in range(MICRO):

            def normalise(chunk, carry):
                rows = chunk_rows(chunk)
                cols = pl.ds(pl.multiple_of(index * LEN + chunk * BQ, BQ), BQ)
                enter_t[:, cols] = enter_rows(x_ref, small_ref, rows, index).T
                return carry

            lax.fori_loop(0, LEN // BQ, normalise, 0)

    shared = (qkv_ref, mixed_ref, gmixed_ref, total_ref, cos_ref, sin_ref, gproj_ref, dk_ref, dv_ref)
    attend_backward(lengths, bucket, bucket, 0, 0, BQ, *shared)

    def later(step, carry):
        @pl.when((bucket == 0) & (step == 2))
        def _():
            for load in loads():
                load.wait()
            for item in early:
                item.arrive(0)
            for item in early:
                item.start(1)

        @pl.when((bucket == 1) & (step == 1))
        def _():
            for item in early:
                item.arrive(1)
            for item in early:
                item.start(2)

        @pl.when((bucket == 1) & (step == 3))
        def _():
            for item in early:
                item.arrive(2)
            for item in early:
                item.start(3)

        first_row = pl.multiple_of(step * BQ, BQ)
        attend_backward(lengths, bucket, bucket, first_row, pl.multiple_of(first_row - BQ, BQ), 2 * BQ, *shared)
        return carry

    lax.fori_loop(1, LEN // BQ, later, 0)
    finish_keys(bucket, cos_ref, sin_ref, gproj_ref, dk_ref, dv_ref)

    @pl.when(bucket == 1)
    def _():
        def grad_tile(tensor):
            right = gproj_ref[:, :, tile_cols(tensor, IN_W)].reshape(MICRO * LEN, IN_W)
            return dot(enter_t[...], right).astype(jnp.bfloat16).reshape(4, 2, 64, IN_W)

        def tiles(step, carry):
            @pl.when(step < 2)
            def _():
                away_in[step] = grad_tile(step * 2 + 1)

            @pl.when(step == 1)
            def _():
                for item in late:
                    item.start(0)

            @pl.when(step >= 2)
            def _():
                held[0][step - 2] = grad_tile((step - 2) * 2)

            return carry

        lax.fori_loop(0, 4, tiles, 0)
        small_acc[...] = jnp.zeros_like(small_acc)
        in_full = in_ref[...]

        def data_grad(step, carry):
            for stage, moment in ((0, 1), (1, 4), (2, 7)):

                @pl.when(step == moment)
                def _():
                    for item in late:
                        item.arrive(stage)
                    for item in late:
                        item.start(stage + 1)

            index = step // (LEN // BQ)
            rows = chunk_rows(step % (LEN // BQ))
            grad_enter = dot(gproj_ref[index, rows, :], in_full, NT)
            normal, inverse = norm_parts(x_ref[index, rows, :].astype(jnp.float32))
            back = norm_back(grad_enter * small_ref[0:1, :], normal, inverse)
            xgrad_ref[index, rows, :] = (gy1_ref[index, rows, :] + back).astype(jnp.bfloat16)
            small_acc[0] += jnp.sum((grad_enter * normal).reshape(BQ // 8, 8, D), 0)
            small_acc[1] += jnp.sum(grad_enter.reshape(BQ // 8, 8, D), 0)
            return carry

        lax.fori_loop(0, MICRO * LEN // BQ, data_grad, 0)

        rows = [jnp.sum(small_acc[row], 0, keepdims=True) for row in range(2)]
        rows += [jnp.sum(sums_ref[row], 0, keepdims=True) for row in range(4)]
        weights_sq = []
        for which in range(4):
            weights_sq.append([state[3 * which][plane] * state[3 * which][plane] for plane in planes(which)])
        rows.append(sums_of_squares(weights_sq))
        rows.append(jnp.zeros((1, D), jnp.float32))
        small_held[0] = jnp.concatenate(rows, 0)
        small_sum.start(0)

        grads = [None, early[0].result().T, early[1].result(), early[2].result()]
        grad_refs[1][0] = grads[1][:HEAD_DIM]
        grad_refs[1][1] = grads[1][HEAD_DIM:]
        grad_refs[2][...] = grads[2]
        grad_refs[3][...] = grads[3]
        small_sum.step(0)
        parts = [item.result() for item in late]
        part = jnp.concatenate(parts, 0)
        for head in range(2):
            pieces = [part[:, which * 128 + head * HEAD_DIM : which * 128 + head * HEAD_DIM + HEAD_DIM] for which in range(3)]
            grad_refs[0][:, head, :] = jnp.concatenate(pieces, 1)
        updates_sq = []
        for which in range(4):
            squares = []
            for plane in planes(which):
                weight, first, second = (state[3 * which + kind][plane] for kind in range(3))
                update = moments(weight, grad_refs[which][plane], first, second)[2]
                squares.append(update * update)
            updates_sq.append(squares)
        norm_held[0] = jnp.broadcast_to(sums_of_squares(updates_sq)[:, :128], (8, 128))
        norm_sum.start(0)
        small_sum.step(1)
        norm_sum.step(0)
        small_sum.step(2)
        norm_sum.step(1)
        small_sum.step(3)
        norm_sum.step(2)
        norm_sum.step(3)
        all_ref[...] = small_sum.total()
        norm_ref[...] = norm_sum.total()
        for item in early + late:
            item.sent()
        small_sum.sent()
        norm_sum.sent()


def lamb_kernel(*refs):
    state, grads, refs = refs[:12], refs[12:16], refs[16:]
    small_ref, small_first_ref, small_second_ref, all_ref, norm_ref, refs = *refs[:5], refs[5:]
    outs, (grad_ref, new_ref, first_ref, second_ref, norms_ref) = refs[:16], refs[16:]
    weight_norm = jnp.sqrt(all_ref[6:7, 0:128])
    update_sq = norm_ref[0:1, :]
    ratio = learn_rate * weight_norm * lax.rsqrt(update_sq + 1e-12)
    for which in range(4):
        scale = ratio[:, which : which + 1]
        for plane in planes(which):
            weight, first, second = (state[3 * which + kind][plane] for kind in range(3))
            first, second, update = moments(weight, grads[which][plane], first, second)
            new = weight - scale * update
            outs[4 * which][plane] = new
            outs[4 * which + 1][plane] = first
            outs[4 * which + 2][plane] = second
            outs[4 * which + 3][plane] = new.astype(jnp.bfloat16)
    small = small_ref[...]
    small_grad = all_ref[0:6, :]
    grad_ref[...] = small_grad
    first, second, update = moments(small, small_grad, small_first_ref[...], small_second_ref[...])
    small_sq = jnp.sum(small * small, 1, keepdims=True)
    change_sq = jnp.sum(update * update, 1, keepdims=True)
    new_ref[...] = small - learn_rate * jnp.sqrt(small_sq) * lax.rsqrt(change_sq + 1e-12) * update
    first_ref[...] = first
    second_ref[...] = second
    lanes = lane_ids((1, 128))
    top = jnp.where(lanes < 4, weight_norm, 0.0)
    bottom = jnp.where(lanes < 4, jnp.sqrt(update_sq), 0.0)
    for row in range(6):
        top = top + jnp.where(lanes == 4 + row, jnp.sqrt(small_sq[row : row + 1]), 0.0)
        bottom = bottom + jnp.where(lanes == 4 + row, jnp.sqrt(change_sq[row : row + 1]), 0.0)
    norms_ref[0:1, :] = top[:, :10]
    norms_ref[1:2, :] = bottom[:, :10]


def whole(shape):
    return pl.BlockSpec(shape, lambda *ids: (0,) * len(shape), pipeline_mode=pl.Buffered(1))


def per_bucket(*shape):
    return pl.BlockSpec((1,) + shape, lambda b: (b, 0, 0))


def bf16(*shape):
    return jax.ShapeDtypeStruct(shape, jnp.bfloat16)


def f32(*shape):
    return jax.ShapeDtypeStruct(shape, jnp.float32)


def vmem16(*shape):
    return pltpu.VMEM(shape, jnp.bfloat16)


def vmem32(*shape):
    return pltpu.VMEM(shape, jnp.float32)


SCALARS = pl.BlockSpec(memory_space=pltpu.SMEM)
ANYWHERE = pl.BlockSpec(memory_space=pl.ANY)


def params(count, collective=None):
    more = {} if collective is None else dict(collective_id=collective, has_side_effects=True)
    return pltpu.CompilerParams(dimension_semantics=("arbitrary",) * count, vmem_limit_bytes=VMEM_LIMIT, **more)


def turn_tables(lengths):
    ends = jnp.cumsum(lengths, axis=1)
    position = jnp.arange(LEN, dtype=jnp.int32)
    passed = position[None, :, None] >= ends[:, None, : CLIPS - 1]
    start = jnp.max(jnp.where(passed, ends[:, None, : CLIPS - 1], 0), axis=2)
    offset = (position[None, :] - start).astype(jnp.float32)
    frequency = jnp.exp(jnp.arange(HEAD_DIM // 2, dtype=jnp.float32) * (-2.0 * math.log(10000.0) / HEAD_DIM))
    angles = offset[:, :, None] * frequency
    cosine = jnp.repeat(jnp.cos(angles), 2, axis=-1)
    sine = jnp.sin(angles)
    sine = jnp.stack([-sine, sine], axis=-1).reshape(cosine.shape)
    return jnp.concatenate([cosine, cosine], -1), jnp.concatenate([sine, sine], -1)


def attention_forward(lengths, x, small, cosine, sine, in_mat):
    count = x.shape[0]
    return pl.pallas_call(
        forward_kernel,
        grid=(count,),
        in_specs=[SCALARS, per_bucket(LEN, D), whole((6, D)), per_bucket(LEN, 128), per_bucket(LEN, 128), whole((D, 3 * D))],
        out_specs=[per_bucket(LEN, 3 * D), per_bucket(LEN, D), per_bucket(LEN, D), per_bucket(LEN, D)],
        out_shape=[bf16(count, LEN, 3 * D), bf16(count, LEN, D), f32(count, LEN, D), bf16(count, LEN, D)],
        compiler_params=params(1),
        name="attention_forward",
    )(lengths, x, small, cosine, sine, in_mat)


def gather_forward(lengths, x, small, weights):
    shapes = [(4, 2, 64, 4 * width) for width in (IN_W, OUT_W, FF_W, FF_W)]

    def per_pair(width):
        return pl.BlockSpec((1, LEN, width), lambda pair, bucket: (bucket, 0, pair))

    return pl.pallas_call(
        gather_kernel,
        grid=(PAIRS, MICRO),
        in_specs=[SCALARS, whole((MICRO, LEN, D)), whole((6, D)), whole((4, 32, 128))] + [whole(item.shape) for item in weights],
        out_specs=[per_pair(IN_W), per_pair(128), per_pair(128)] + [whole((MICRO, LEN, 128))] * 2 + [ANYWHERE] * 4,
        out_shape=[bf16(MICRO, LEN, 3 * D), bf16(MICRO, LEN, D), f32(MICRO, LEN, D)]
        + [f32(MICRO, LEN, 128)] * 2
        + [bf16(*shape) for shape in shapes],
        scratch_shapes=[vmem16(*shape) for shape in shapes]
        + [
            vmem16(64, SHARD_W),
            vmem16(MICRO, LEN, D),
            vmem32(MICRO, BLOCKS, BH, KEYS),
            pltpu.SemaphoreType.DMA((6, 8)),
            pltpu.SemaphoreType.DMA((6, 8)),
            pltpu.SemaphoreType.DMA((4,)),
            pltpu.SemaphoreType.DMA((6,)),
        ],
        compiler_params=params(2, 1),
        name="gather_forward",
    )(lengths, x, small, position_steps(), *weights)


def mlp_both(lengths, x, cot, mixed, small, out_mat, up_mat, down_mat):
    count = x.shape[0]
    rows = count * LEN

    def chunked(width):
        return pl.BlockSpec((1, MLP_ROWS, width), lambda b, i: (b, i, 0))

    return pl.pallas_call(
        mlp_kernel,
        grid=(count, LEN // MLP_ROWS),
        in_specs=[SCALARS, chunked(D), chunked(D), chunked(D), whole((6, D)), whole((D, D)), whole((D, FF)), whole((D, FF))],
        out_specs=[chunked(D), chunked(D), chunked(D), whole((4, 8, D)), whole((D, D)), whole((D, FF)), whole((D, FF))],
        out_shape=[
            bf16(count, LEN, D), f32(count, LEN, D), bf16(count, LEN, D), f32(4, 8, D), bf16(D, D), bf16(D, FF), bf16(D, FF),
        ],
        scratch_shapes=[
            vmem16(rows, FF), vmem16(rows, FF), vmem16(rows, D), vmem16(D, rows), vmem16(D, rows), vmem16(D, rows),
        ],
        compiler_params=params(2),
        name="mlp_both",
    )(lengths, x, cot, mixed, small, out_mat, up_mat, down_mat)


def attention_backward(lengths, qkv, mixed, gmixed, totals, cosine, sine):
    count = qkv.shape[0]
    return pl.pallas_call(
        backward_kernel,
        grid=(count,),
        in_specs=[SCALARS, per_bucket(LEN, 3 * D), per_bucket(LEN, D), per_bucket(LEN, D), per_bucket(LEN, D), per_bucket(LEN, 128), per_bucket(LEN, 128)],
        out_specs=per_bucket(LEN, 3 * D),
        out_shape=bf16(count, LEN, 3 * D),
        scratch_shapes=[vmem32(LEN, D), vmem32(LEN, D)],
        compiler_params=params(1),
        name="attention_backward",
    )(lengths, qkv, mixed, gmixed, totals, cosine, sine)


def backward_tail(lengths, qkv, mixed, gmixed, totals, cosine, sine, x, small, gy1, sums, in_mat, gout, gup, gdown, state):
    widths = (IN_W, OUT_W, FF_W, FF_W)
    dma = pltpu.SemaphoreType.DMA
    grad_shapes = [f32(*state[3 * which].shape) for which in range(4)]
    return pl.pallas_call(
        tail_kernel,
        grid=(MICRO,),
        in_specs=[
            SCALARS, per_bucket(LEN, 3 * D), per_bucket(LEN, D), per_bucket(LEN, D), per_bucket(LEN, D),
            per_bucket(LEN, 128), per_bucket(LEN, 128), whole((MICRO, LEN, D)), whole((6, D)), whole((MICRO, LEN, D)),
            whole((4, 8, D)), whole((D, 3 * D)), ANYWHERE, ANYWHERE, ANYWHERE,
        ]
        + [whole(item.shape) for item in state],
        out_specs=[whole(item.shape) for item in grad_shapes] + [whole((MICRO, LEN, D)), whole((8, D)), whole((8, 128))],
        out_shape=grad_shapes + [bf16(MICRO, LEN, D), f32(8, D), f32(8, 128)],
        scratch_shapes=[
            vmem16(MICRO, LEN, 3 * D), vmem32(LEN, D), vmem32(LEN, D), vmem16(D, MICRO * LEN), vmem16(2, 4, 2, 64, IN_W), vmem32(2, 8, D),
        ]
        + [vmem16(2, 4, 2, 64, width) for width in widths]
        + [vmem16(2, 4, 2, 64, width) for width in widths]
        + [vmem16(*middle_shape(index)) for index in range(5)]
        + [vmem16(4, SUMMED[index][2], SUMMED[index][3]) for index in range(5)]
        + [vmem16(3, SUMMED[index][2], SUMMED[index][3]) for index in range(5)]
        + [vmem32(4, 8, D), vmem32(3, 8, D), vmem32(4, 8, D), vmem32(4, 8, 128), vmem32(3, 8, 128), vmem32(4, 8, 128)]
        + [dma((5, 7)), dma((5, 7)), dma((6,)), dma((6,)), dma((6,)), dma((6,)), dma((3, 2))],
        compiler_params=params(1, 2),
        name="backward_tail",
    )(lengths, qkv, mixed, gmixed, totals, cosine, sine, x, small, gy1, sums, in_mat, gout, gup, gdown, *state)


def lamb_all(state, grads, small, small_first, small_second, everything, norm_squares):
    outs = []
    for which in range(4):
        shape = state[3 * which].shape
        outs += [f32(*shape)] * 3 + [bf16(*shape)]
    outs += [f32(6, D)] * 4 + [f32(2, 10)]
    return pl.pallas_call(
        lamb_kernel,
        out_shape=outs,
        compiler_params=pltpu.CompilerParams(vmem_limit_bytes=VMEM_LIMIT),
        name="lamb_all",
    )(*state, *grads, small, small_first, small_second, everything, norm_squares)


def tile_shard(in_proj, out_proj, up_proj, down_proj):
    depth, heads_here, _ = in_proj.shape
    out_cols = out_proj.reshape(heads_here * HEAD_DIM, depth).T
    parts = [in_proj.reshape(depth, -1), out_cols, up_proj, down_proj.T]
    return jnp.concatenate(parts, axis=1).astype(jnp.bfloat16)


def on_device(
    frames, cotangent, clip_lengths, in_proj, out_proj, up_proj, down_proj, small_params,
    in_first, in_second, out_first, out_second, up_first, up_second, down_first, down_second,
    small_first, small_second,
):
    lengths = clip_lengths
    qkv, mixed, totals, cosine, sine, in_full, out_full, up_full, down_full = gather_forward(
        lengths, frames, small_params, (in_proj, out_proj, up_proj, down_proj.T)
    )
    block_out, gy1, gmixed, sums, gout, gup, gdown = mlp_both(
        lengths, frames, cotangent, mixed, small_params, out_full.reshape(D, D), up_full.reshape(D, FF), down_full.reshape(D, FF)
    )
    state = (
        in_proj, in_first, in_second, out_proj, out_first, out_second, up_proj, up_first, up_second, down_proj.T, down_first.T, down_second.T,
    )
    *grads, input_grad, everything, norm_squares = backward_tail(
        lengths, qkv, mixed, gmixed, totals, cosine, sine, frames, small_params, gy1, sums, in_full.reshape(D, 3 * D),
        gout.reshape(4, 2, 64, D), gup.reshape(4, 2, 64, FF), gdown.reshape(4, 2, 64, FF), state,
    )
    outs = list(lamb_all(state, grads, small_params, small_first, small_second, everything, norm_squares))
    outs[12:16] = [item.T for item in outs[12:16]]
    return (block_out, input_grad, *outs)


def on_any_mesh(
    frames, cotangent, clip_lengths, in_proj, out_proj, up_proj, down_proj, small_params,
    in_first, in_second, out_first, out_second, up_first, up_second, down_first, down_second,
    small_first, small_second,
):
    rows_here = frames.shape[1]
    own_buckets = rows_here // LEN
    first_bucket = lax.axis_index("tensor") * own_buckets
    lengths = lax.dynamic_slice_in_dim(clip_lengths, first_bucket, own_buckets, 1).reshape(-1, CLIPS)
    count = MICRO * own_buckets
    x = frames.reshape(count, LEN, D)
    cot = cotangent.reshape(count, LEN, D)
    tensor_size = lax.axis_size("tensor")
    dp_size = lax.axis_size("dp")
    depth = in_proj.shape[0]
    heads_here = in_proj.shape[1]
    ff_here = up_proj.shape[1]

    shard = tile_shard(in_proj, out_proj, up_proj, down_proj)
    gathered = lax.all_gather(shard, ("dp", "tensor"), axis=0)
    gathered = gathered.reshape(dp_size, tensor_size, depth, shard.shape[1])
    gathered = jnp.moveaxis(gathered, 1, 2).reshape(D, tensor_size, shard.shape[1])
    edge0 = heads_here * 192
    edge1 = edge0 + heads_here * HEAD_DIM
    edge2 = edge1 + ff_here
    in_mat = gathered[:, :, :edge0].reshape(D, PAIRS, 2, 3, HEAD_DIM).transpose(0, 1, 3, 2, 4).reshape(D, 3 * D)
    out_mat = gathered[:, :, edge0:edge1].reshape(D, D)
    up_mat = gathered[:, :, edge1:edge2].reshape(D, FF)
    down_mat = gathered[:, :, edge2:].reshape(D, FF)

    cosine, sine = turn_tables(lengths)
    qkv, mixed, totals, enter1 = attention_forward(lengths, x, small_params, cosine, sine, in_mat)
    block_out, grad_y_first, grad_mixed, sums, grad_out, grad_upw, grad_down = mlp_both(
        lengths, x, cot, mixed, small_params, out_mat, up_mat, down_mat
    )

    def weight_grad(left, right):
        return dot(left.reshape(-1, left.shape[-1]), right.reshape(-1, right.shape[-1]), TN).astype(jnp.bfloat16)

    grad_proj = attention_backward(lengths, qkv, mixed, grad_mixed, totals, cosine, sine)
    grad_in = weight_grad(enter1, grad_proj)
    grad_in = grad_in.reshape(D, PAIRS, 3, 2, HEAD_DIM).transpose(0, 1, 3, 2, 4)

    def by_owner(mat):
        return jnp.moveaxis(mat.reshape(dp_size, depth, tensor_size, -1), 2, 1)

    stacked = jnp.concatenate([by_owner(grad_in), by_owner(grad_out), by_owner(grad_upw), by_owner(grad_down)], axis=-1)
    owned = lax.psum_scatter(
        stacked.reshape(dp_size * tensor_size, depth, -1), ("dp", "tensor"), scatter_dimension=0, tiled=False
    ).astype(jnp.float32)

    grad_enter1 = dot(grad_proj.reshape(-1, 3 * D), in_mat, NT).reshape(count, LEN, D)
    normal1, inverse1 = norm_parts(x.astype(jnp.float32))
    input_grad = (grad_y_first + norm_back(grad_enter1 * small_params[0], normal1, inverse1)).astype(jnp.bfloat16)
    late = jnp.sum(sums, axis=1)
    small_terms = jnp.stack(
        [jnp.sum(grad_enter1 * normal1, (0, 1)), jnp.sum(grad_enter1, (0, 1)), late[0], late[1], late[2], late[3]]
    )

    grads = (
        owned[:, :edge0].reshape(in_proj.shape),
        owned[:, edge0:edge1].T.reshape(out_proj.shape),
        owned[:, edge1:edge2],
        owned[:, edge2:].T,
    )
    weights_in = (in_proj, out_proj, up_proj, down_proj)
    firsts = (in_first, out_first, up_first, down_first)
    seconds = (in_second, out_second, up_second, down_second)
    own_squares = jnp.stack([jnp.sum(weight * weight) for weight in weights_in])
    small_grad, weight_squares = lax.psum((small_terms, own_squares), ("dp", "tensor"))
    new_firsts = []
    new_seconds = []
    updates = []
    for weight, gradient, first, second in zip(weights_in, grads, firsts, seconds):
        first = beta_first * first + (1.0 - beta_first) * gradient
        second = beta_second * second + (1.0 - beta_second) * gradient * gradient
        update = (
            first / (1.0 - beta_first**STEP) / (jnp.sqrt(second / (1.0 - beta_second**STEP)) + adam_eps)
            + decay_rate * weight
        )
        new_firsts.append(first)
        new_seconds.append(second)
        updates.append(update)
    update_squares = lax.psum(jnp.stack([jnp.sum(update * update) for update in updates]), ("dp", "tensor"))
    trust_ratio = jnp.sqrt(weight_squares) * lax.rsqrt(update_squares + 1e-12)
    new_weights = [weights_in[index] - learn_rate * trust_ratio[index] * updates[index] for index in range(4)]
    small_first_new = beta_first * small_first + (1.0 - beta_first) * small_grad
    small_second_new = beta_second * small_second + (1.0 - beta_second) * small_grad * small_grad
    small_update = (
        small_first_new / (1.0 - beta_first**STEP) / (jnp.sqrt(small_second_new / (1.0 - beta_second**STEP)) + adam_eps)
        + decay_rate * small_params
    )
    small_weight_sq = jnp.sum(small_params * small_params, axis=1, keepdims=True)
    small_update_sq = jnp.sum(small_update * small_update, axis=1, keepdims=True)
    small_new = small_params - learn_rate * jnp.sqrt(small_weight_sq) * lax.rsqrt(small_update_sq + 1e-12) * small_update
    norms = jnp.stack(
        [
            jnp.concatenate([jnp.sqrt(weight_squares), jnp.sqrt(small_weight_sq).reshape(-1)]),
            jnp.concatenate([jnp.sqrt(update_squares), jnp.sqrt(small_update_sq).reshape(-1)]),
        ]
    )
    outputs = [block_out.reshape(frames.shape), input_grad.reshape(frames.shape)]
    for new, first, second in zip(new_weights, new_firsts, new_seconds):
        outputs += [new, first, second, new.astype(jnp.bfloat16)]
    return tuple(outputs + [small_grad, small_new, small_first_new, small_second_new, norms])


def solution(mesh):
    rows = P(None, ("dp", "tensor"), None)
    in_spec = P("dp", "tensor", None)
    out_spec = P("tensor", None, "dp")
    up_spec = P("dp", "tensor")
    down_spec = P("tensor", "dp")
    shape = dict(mesh.shape)
    small_slice = shape["dp"] == HERE_DP and shape["tensor"] == HERE_TENSOR
    return jax.shard_map(
        on_device if small_slice else on_any_mesh,
        mesh=mesh,
        in_specs=(
            rows, rows, P(None, "dp", None), in_spec, out_spec, up_spec, down_spec, P(),
            in_spec, in_spec, out_spec, out_spec, up_spec, up_spec, down_spec, down_spec, P(), P(),
        ),
        out_specs=(rows, rows) + (in_spec,) * 4 + (out_spec,) * 4 + (up_spec,) * 4 + (down_spec,) * 4 + (P(),) * 5,
        check_vma=False,
    )
```

```python
import functools
import math

import jax
import jax.numpy as jnp
import numpy as np
from jax import lax
from jax.experimental import pallas as pl
from jax.experimental.pallas import tpu as pltpu
from jax.sharding import PartitionSpec as P

D = 512
HEADS = 8
HEAD_DIM = 64
FF = 2048
PAIRS = HEADS // 2
WINDOW = 250
LEN = 1024
CLIPS = 4
MICRO = 2
STEP = 3

BQ = 256
BH = 128
BLOCKS = LEN // BH
KEYS = 3 * BH
MLP_ROWS = 512
LAST_ROWS = 512
VMEM_LIMIT = 62 * 1024 * 1024

beta_first = 0.5
beta_second = 0.5
adam_eps = 1e-06
decay_rate = 0.01
learn_rate = 0.3

NT = (((1,), (1,)), ((), ()))
NN = (((1,), (0,)), ((), ()))
TN = (((0,), (0,)), ((), ()))


def dot(a, b, dims=NN):
    return lax.dot_general(a, b, dims, preferred_element_type=jnp.float32)


def norm_parts(rows):
    mean = jnp.mean(rows, -1, keepdims=True)
    centred = rows - mean
    inverse = lax.rsqrt(jnp.mean(centred * centred, -1, keepdims=True) + 1e-05)
    return centred * inverse, inverse


def norm_back(scaled, normal, inverse):
    return inverse * (
        scaled
        - jnp.mean(scaled, -1, keepdims=True)
        - normal * jnp.mean(scaled * normal, -1, keepdims=True)
    )


def lane_ids(shape):
    return lax.broadcasted_iota(jnp.int32, shape, len(shape) - 1)


def swap_pairs(rows):
    even = (lane_ids(rows.shape) & 1) == 0
    return jnp.where(even, pltpu.roll(rows, 127, 1), pltpu.roll(rows, 1, 1))


def run_starts(lengths_ref, bucket, position):
    end0 = lengths_ref[bucket, 0]
    end1 = end0 + lengths_ref[bucket, 1]
    end2 = end1 + lengths_ref[bucket, 2]
    start = jnp.where(position >= end0, end0, 0)
    start = jnp.where(position >= end1, end1, start)
    return jnp.where(position >= end2, end2, start), position < end2


def block_bias(lengths_ref, bucket, first_row, first_key, keys):
    position = first_row + lax.broadcasted_iota(jnp.int32, (BQ, 1), 0)
    start, _ = run_starts(lengths_ref, bucket, position)
    lowest = jnp.maximum(start, position - (WINDOW - 1))
    key = first_key + lax.broadcasted_iota(jnp.int32, (BQ, keys), 1)
    return jnp.where((key >= lowest) & (key <= position), 0.0, -1e30)


def head_lanes(tile, head):
    return jnp.where((lane_ids(tile.shape) // HEAD_DIM) == head, tile, jnp.zeros_like(tile))


MESH = pl.DeviceIdType.MESH
HERE_DP = 8
HERE_TENSOR = 4
IN_W, OUT_W, FF_W = 384, 128, 512
SHARD_W = IN_W + OUT_W + 2 * FF_W
CORE, ALONG_Y, ALONG_X = "core", "y", "x"

GATHERED = (
    (0, 0, 64, IN_W, 0, "xy"),
    (1, 0, 64, OUT_W, IN_W, "yx"),
    (2, 0, 32, FF_W, IN_W + OUT_W, "xy"),
    (3, 0, 32, FF_W, IN_W + OUT_W + FF_W, "yx"),
    (2, 32, 32, FF_W, IN_W + OUT_W, "xy"),
    (3, 32, 32, FF_W, IN_W + OUT_W + FF_W, "yx"),
)
IN, OUT, UP_A, DOWN_A, UP_B, DOWN_B = range(6)
SUMMED = (
    (1, 0, 64, OUT_W, "yx"),
    (2, 0, 32, FF_W, "yx"),
    (3, 0, 32, FF_W, "xy"),
    (2, 32, 32, FF_W, "yx"),
    (3, 32, 32, FF_W, "xy"),
    (0, 0, 32, IN_W, "yx"),
    (0, 32, 32, IN_W, "yx"),
)


class Place:
    def __init__(self):
        dp = lax.axis_index("dp")
        tensor = lax.axis_index("tensor")
        self.z, self.x = dp // 2, dp % 2
        self.y, self.c = tensor // 2, tensor % 2

    def device(self, dz=0, x=None, y=None, c=None):
        x = self.x if x is None else x
        y = self.y if y is None else y
        c = self.c if c is None else c
        return {"dp": (self.z + dz) % 4 * 2 + x, "tensor": y * 2 + c}

    def peers(self):
        return {
            CORE: self.device(c=1 - self.c),
            ALONG_Y: self.device(y=1 - self.y),
            ALONG_X: self.device(x=1 - self.x),
            1: self.device(dz=1),
            2: self.device(dz=2),
            3: self.device(dz=3),
        }


def tile_cols(slot, width):
    return pl.ds(pl.multiple_of(slot * width, 128), width)


def remote(source, target, send, recv, device):
    return pltpu.make_async_remote_copy(
        src_ref=source, dst_ref=target, send_sem=send, recv_sem=recv, device_id=device, device_id_type=MESH
    )


def meet(place):
    barrier = pltpu.get_barrier_semaphore()
    peers = place.peers()
    for device in peers.values():
        pl.semaphore_signal(barrier, inc=1, device_id=device, device_id_type=MESH)
    pl.semaphore_wait(barrier, len(peers))


def start_all(copies):
    for copy in copies:
        copy.start()


def arrive_all(copies):
    for copy in copies:
        copy.wait_recv()


def sent_all(copies):
    for copy in copies:
        copy.wait_send()


def gather_copies(index, stage, place, shard, weights, send, recv):
    weight, row, count, width, offset, order = GATHERED[index]
    full = weights[weight]
    rows = pl.ds(row, count)
    peers = place.peers()

    def copy(source, target, slot, peer):
        return remote(source, target, send.at[index, slot], recv.at[index, slot], peers[peer])

    def cols(slot):
        return slice(slot * width, slot * width + width)

    if stage == 0:
        return [
            copy(shard.at[rows, offset : offset + width], full.at[place.z, place.x, rows, cols(0)], step - 1, step)
            for step in (1, 2, 3)
        ]
    if stage == 1:
        part = full.at[:, place.x, rows, cols(0)]
        if order == "xy":
            return [copy(part, part, 3, ALONG_X)]
        return [copy(part, full.at[:, place.x, rows, cols(2)], 3, ALONG_Y)]
    if stage == 2:
        if order == "xy":
            return [copy(full.at[:, :, rows, cols(0)], full.at[:, :, rows, cols(2)], 4, ALONG_Y)]
        parts = [full.at[:, place.x, rows, cols(slot)] for slot in (0, 2)]
        return [copy(part, part, 4 + index, ALONG_X) for index, part in enumerate(parts)]
    slot = stage * 2 - 6
    return [copy(full.at[:, :, rows, cols(slot)], full.at[:, :, rows, cols(slot + 1)], stage + 3, CORE)]


def project_rows(rows, enter, cosine, sine, weight, qkv_ref, base):
    part = dot(enter, weight)
    for which in range(2):
        piece = part[:, which * 128 : which * 128 + 128]
        turned = piece * cosine + swap_pairs(piece) * sine
        if which == 0:
            turned = turned * (HEAD_DIM**-0.5)
        qkv_ref[0, rows, base + which * 128 : base + which * 128 + 128] = turned.astype(jnp.bfloat16)
    qkv_ref[0, rows, base + 256 : base + 384] = part[:, 256:].astype(jnp.bfloat16)


def attend_forward(lengths_ref, bucket, first_row, first_key, keys, qkv_ref, mixed_ref, total_ref):
    rows = pl.ds(first_row, BQ)
    key_rows = pl.ds(first_key, keys)
    bias = block_bias(lengths_ref, bucket, first_row, first_key, keys)
    for pair in range(PAIRS):
        base = pair * 384
        queries = qkv_ref[0, rows, base : base + 128]
        keys_rot = qkv_ref[0, key_rows, base + 128 : base + 256]
        values = qkv_ref[0, key_rows, base + 256 : base + 384]
        outs = []
        totals = []
        for head in range(2):
            scores = dot(head_lanes(queries, head), keys_rot, NT) + bias
            top = jnp.max(scores, -1, keepdims=True)
            powers = jnp.exp(scores - top)
            total = jnp.sum(powers, -1, keepdims=True)
            outs.append(dot(powers.astype(jnp.bfloat16), values) / total)
            totals.append(jnp.broadcast_to(top + jnp.log(total), (BQ, 128)))
        low = lane_ids((BQ, 128)) < HEAD_DIM
        mixed_ref[0, rows, pair * 128 : pair * 128 + 128] = jnp.where(low, outs[0], outs[1]).astype(jnp.bfloat16)
        total_ref[0, rows, pair * 128 : pair * 128 + 128] = jnp.where(low, totals[0], totals[1])


def turn_tables_here(lengths_ref, steps_ref, cos_ref, sin_ref):
    lanes = lane_ids((8, 128))
    frequency = jnp.exp(((lanes & (HEAD_DIM - 1)) // 2).astype(jnp.float32) * (-2.0 * math.log(10000.0) / HEAD_DIM))
    sign = jnp.where((lane_ids((1, 128)) & 1) == 0, -1.0, 1.0)
    fine_cos, fine_sin = steps_ref[2:3], steps_ref[3:4]
    for bucket in range(MICRO):
        end0 = lengths_ref[bucket, 0]
        end1 = end0 + lengths_ref[bucket, 1]
        end2 = end1 + lengths_ref[bucket, 2]
        row = lax.broadcasted_iota(jnp.int32, (8, 128), 0)
        start = jnp.where(row == 0, 0, jnp.where(row == 1, end0, jnp.where(row == 2, end1, end2)))
        angle = start.astype(jnp.float32) * frequency
        run_cos, run_sin = jnp.cos(angle), jnp.sin(angle)

        def chunk_tables(chunk, carry):
            coarse = pl.ds(pl.multiple_of(chunk * 8, 8), 8)
            coarse_cos, coarse_sin = steps_ref[0, coarse, :][:, None, :], steps_ref[1, coarse, :][:, None, :]
            at_cos = (coarse_cos * fine_cos - coarse_sin * fine_sin).reshape(BQ, 128)
            at_sin = (coarse_sin * fine_cos + coarse_cos * fine_sin).reshape(BQ, 128)
            position = chunk * BQ + lax.broadcasted_iota(jnp.int32, (BQ, 128), 0)
            first_cos, first_sin = run_cos[0:1], run_sin[0:1]
            for run, end in enumerate((end0, end1, end2)):
                first_cos = jnp.where(position >= end, run_cos[run + 1 : run + 2], first_cos)
                first_sin = jnp.where(position >= end, run_sin[run + 1 : run + 2], first_sin)
            rows = chunk_rows(chunk)
            cos_ref[bucket, rows, :] = at_cos * first_cos + at_sin * first_sin
            sin_ref[bucket, rows, :] = (at_sin * first_cos - at_cos * first_sin) * sign
            return carry

        lax.fori_loop(0, LEN // BQ, chunk_tables, 0)


def position_steps():
    lane = np.arange(128) % HEAD_DIM // 2
    frequency = np.exp(lane.astype(np.float32) * np.float32(-2.0 * math.log(10000.0) / HEAD_DIM)).astype(np.float64)
    step = np.arange(32)[:, None]
    coarse, fine = step * 32 * frequency, step * frequency
    return jnp.asarray(np.stack([np.cos(coarse), np.sin(coarse), np.cos(fine), np.sin(fine)]).astype(np.float32))


def enter_rows(x_ref, small_ref, rows, bucket=0):
    normal, _ = norm_parts(x_ref[bucket, rows, :].astype(jnp.float32))
    return (normal * small_ref[0:1, :] + small_ref[1:2, :]).astype(jnp.bfloat16)


def chunk_rows(chunk):
    return pl.ds(pl.multiple_of(chunk * BQ, BQ), BQ)


def forward_kernel(lengths_ref, x_ref, small_ref, cos_ref, sin_ref, in_ref, qkv_ref, mixed_ref, total_ref, enter_ref):
    bucket = pl.program_id(0)

    def project(chunk, carry):
        rows = chunk_rows(chunk)
        enter_ref[0, rows, :] = enter_rows(x_ref, small_ref, rows)
        for pair in range(PAIRS):
            weight = in_ref[:, pair * 384 : pair * 384 + 384]
            project_rows(rows, enter_ref[0, rows, :], cos_ref[0, rows, :], sin_ref[0, rows, :], weight, qkv_ref, pair * 384)
        return carry

    lax.fori_loop(0, LEN // BQ, project, 0)
    attend_forward(lengths_ref, bucket, 0, 0, BQ, qkv_ref, mixed_ref, total_ref)

    def later(step, carry):
        first_row = pl.multiple_of(step * BQ, BQ)
        attend_forward(lengths_ref, bucket, first_row, pl.multiple_of(first_row - BQ, BQ), 2 * BQ, qkv_ref, mixed_ref, total_ref)
        return carry

    lax.fori_loop(1, LEN // BQ, later, 0)


class RunLengths:
    def __init__(self, ref):
        self.ref, self.own = ref, lax.axis_index("tensor")

    def __getitem__(self, where):
        bucket, run = where
        return self.ref[bucket, self.own, run]


def band_biases(lengths, bias_ref):
    def fill(index, carry):
        bucket, block = index // BLOCKS, index % BLOCKS
        position = block * BH + lax.broadcasted_iota(jnp.int32, (BH, 1), 0)
        start, _ = run_starts(lengths, bucket, position)
        lowest = jnp.maximum(start, position - (WINDOW - 1))
        key = jnp.maximum(block - 2, 0) * BH + lax.broadcasted_iota(jnp.int32, (BH, KEYS), 1)
        bias_ref[bucket, block] = jnp.where((key >= lowest) & (key <= position), 0.0, -1e30)
        return carry

    lax.fori_loop(0, MICRO * BLOCKS, fill, 0)


def block_span(block):
    first = max(block - 2, 0)
    return slice(block * BH, block * BH + BH), slice(first * BH, block * BH + BH), (block + 1 - first) * BH


def both_heads(tile):
    return jnp.concatenate([head_lanes(tile, 0), head_lanes(tile, 1)], 0)


def each_head(rows):
    return jnp.where(lane_ids((BH, 128)) < HEAD_DIM, rows[:BH], rows[BH:])


def attend_pair(bias_ref, bucket, block, qkv_ref, mixed_ref, total_ref):
    rows, key_rows, keys = block_span(block)
    bias = bias_ref[bucket, block, :, :keys]
    scores = dot(both_heads(qkv_ref[0, rows, :128]), qkv_ref[0, key_rows, 128:256], NT)
    scores = scores + jnp.concatenate([bias, bias], 0)
    top = jnp.max(scores, -1, keepdims=True)
    powers = jnp.exp(scores - top)
    total = jnp.sum(powers, -1, keepdims=True)
    out = dot(powers.astype(jnp.bfloat16), qkv_ref[0, key_rows, 256:384]) / total
    mixed_ref[0, rows, :] = each_head(out).astype(jnp.bfloat16)
    total_ref[0, rows, :] = each_head(jnp.broadcast_to(top + jnp.log(total), (2 * BH, 128)))


def gather_kernel(
    lengths_ref, x_ref, small_ref, steps_ref, in_ref, out_ref, up_ref, down_ref,
    qkv_ref, mixed_ref, total_ref, cos_ref, sin_ref, *refs,
):
    kept, full, refs = refs[:4], refs[4:8], refs[8:]
    shard_ref, enter_ref, bias_ref, send, recv, own_sem, keep_sem = refs
    bucket = pl.program_id(1)
    step = pl.program_id(0) * MICRO + bucket
    place = Place()

    def copies(stage, which):
        found = []
        for index in which:
            found += gather_copies(index, stage, place, shard_ref, full, send, recv)
        return found

    def start(stage, *which):
        start_all(copies(stage, which))

    def arrive(stage, *which):
        arrive_all(copies(stage, which))

    def own_tiles():
        tiles = []
        for weight, width, offset in ((0, IN_W, 0), (1, OUT_W, IN_W), (2, FF_W, IN_W + OUT_W), (3, FF_W, IN_W + OUT_W + FF_W)):
            target = full[weight].at[place.z, place.x, :, 0:width]
            tiles.append(pltpu.make_async_copy(shard_ref.at[:, offset : offset + width], target, own_sem.at[weight]))
        return tiles

    def keep(index):
        weight, row, count = GATHERED[index][:3]
        rows = pl.ds(row, count)
        return pltpu.make_async_copy(full[weight].at[:, :, rows, :], kept[weight].at[:, :, rows, :], keep_sem.at[index])

    def finish(*which):
        arrive(3, *which)
        arrive(4, *which)
        for index in which:
            keep(index).start()

    def begin():
        lengths = RunLengths(lengths_ref)
        heads = [in_ref[:, head, :] for head in range(2)]
        pieces = [heads[head][:, part * HEAD_DIM : part * HEAD_DIM + HEAD_DIM] for part in range(3) for head in range(2)]
        shard_ref[:, :IN_W] = jnp.concatenate(pieces, 1).astype(jnp.bfloat16)
        shard_ref[:, IN_W : IN_W + OUT_W] = jnp.concatenate([out_ref[0].T, out_ref[1].T], 1).astype(jnp.bfloat16)
        shard_ref[:, IN_W + OUT_W : IN_W + OUT_W + FF_W] = up_ref[...].astype(jnp.bfloat16)
        shard_ref[:, IN_W + OUT_W + FF_W :] = down_ref[...].astype(jnp.bfloat16)
        meet(place)
        start(0, IN)
        start(0, OUT, UP_A, DOWN_A, UP_B, DOWN_B)
        start_all(own_tiles())
        turn_tables_here(lengths, steps_ref, cos_ref, sin_ref)

        def normalise(index, carry):
            rows = chunk_rows(index % (LEN // BQ))
            enter_ref[index // (LEN // BQ), rows, :] = enter_rows(x_ref, small_ref, rows, index // (LEN // BQ))
            return carry

        lax.fori_loop(0, MICRO * LEN // BQ, normalise, 0)
        for tile in own_tiles():
            tile.wait()
        arrive(0, IN)
        start(1, IN)
        arrive(0, OUT)
        start(1, OUT)
        band_biases(lengths, bias_ref)
        arrive(1, IN)

    def at_0_1():
        arrive(0, UP_A, DOWN_A)
        start(1, DOWN_A, UP_A)
        start(2, IN)
        start(3, IN)
        arrive(1, OUT)
        start(2, OUT)

    def at_2_0():
        arrive(3, IN)

    def at_2_1():
        arrive(0, UP_B, DOWN_B)
        start(1, DOWN_B, UP_B)

    def at_2_2():
        arrive(1, DOWN_A, UP_A)
        start(2, DOWN_A, UP_A)
        start(3, UP_A)

    def at_4_0():
        arrive(2, IN)
        start(4, IN)

    def at_5_2():
        arrive(1, DOWN_B, UP_B)
        start(2, DOWN_B, UP_B)
        start(3, UP_B)

    def at_6_0():
        arrive(4, IN)
        keep(IN).start()

    def at_6_1():
        arrive(2, OUT, DOWN_A)
        start(3, OUT, DOWN_A)
        start(4, OUT, DOWN_A)

    def at_7_1():
        arrive(2, UP_A)
        start(4, UP_A)

    def at_7_3():
        finish(OUT, DOWN_A)

    events = {
        (0, 0): begin, (0, 1): at_0_1, (2, 0): at_2_0, (2, 1): at_2_1, (2, 2): at_2_2, (4, 0): at_4_0,
        (5, 2): at_5_2, (6, 0): at_6_0, (6, 1): at_6_1, (7, 1): at_7_1, (7, 3): at_7_3,
    }

    def progress(point):
        for (moment, where), event in events.items():
            if where == point:
                pl.when(step == moment)(event)

    progress(0)
    weight = full[0][:, :, :, tile_cols(pl.program_id(0), IN_W)].reshape(D, IN_W)

    project_rows(slice(None), enter_ref[bucket], cos_ref[bucket], sin_ref[bucket], weight, qkv_ref, 0)
    for point, blocks in enumerate(((0, 1, 2), (3, 4, 5), (6, 7))):
        progress(point + 1)
        for block in blocks:
            attend_pair(bias_ref, bucket, block, qkv_ref, mixed_ref, total_ref)

    @pl.when(step == PAIRS * MICRO - 1)
    def _():
        arrive(2, DOWN_B)
        start(3, DOWN_B)
        start(4, DOWN_B)
        arrive(2, UP_B)
        start(4, UP_B)
        finish(UP_A)
        finish(DOWN_B, UP_B)
        for index in range(len(GATHERED)):
            keep(index).wait()
        for stage in range(5):
            sent_all(copies(stage, range(len(GATHERED))))


def mlp_kernel(
    lengths_ref, x_ref, cot_ref, mixed_ref, small_ref, out_ref, up_ref, down_ref,
    block_ref, gy1_ref, gmixed_ref, sums_ref, gout_ref, gup_out_ref, gdown_ref,
    act_ref, gup_ref, keep_ref, enter_t, gmlp_t, gbranch_t,
):
    lengths = RunLengths(lengths_ref) if len(lengths_ref.shape) == 3 else lengths_ref
    bucket = pl.program_id(0)
    chunk = pl.program_id(1)
    buckets = pl.num_programs(0)
    chunks = pl.num_programs(1)

    @pl.when((bucket == 0) & (chunk == 0))
    def _():
        sums_ref[...] = jnp.zeros_like(sums_ref)

    index = bucket * chunks + chunk
    rows = pl.ds(pl.multiple_of(index * MLP_ROWS, MLP_ROWS), MLP_ROWS)
    small = [small_ref[row : row + 1, :] for row in range(6)]
    x = x_ref[0].astype(jnp.float32)
    mixed = mixed_ref[0]
    keep_ref[rows, :] = mixed
    branch = dot(mixed, out_ref[...], NT)
    y_first = x + small[4] * branch
    normal, inverse = norm_parts(y_first)
    enter = (normal * small[2] + small[3]).astype(jnp.bfloat16)
    enter_t[:, rows] = enter.T
    position = chunk * MLP_ROWS + lax.broadcasted_iota(jnp.int32, (MLP_ROWS, 1), 0)
    _, valid = run_starts(lengths, bucket, position)
    grad_y = jnp.where(valid, cot_ref[0].astype(jnp.float32), 0.0)
    grad_mlp = (small[5] * grad_y).astype(jnp.bfloat16)
    gmlp_t[:, rows] = grad_mlp.T
    mlp = jnp.zeros((MLP_ROWS, D), jnp.float32)
    grad_enter = jnp.zeros((MLP_ROWS, D), jnp.float32)
    for part in range(FF // 512):
        cols = slice(part * 512, part * 512 + 512)
        upval = dot(enter, up_ref[:, cols])
        grad_act = dot(grad_mlp, down_ref[:, cols])
        cumulative = 0.5 + 0.5 * lax.erf(upval * (1.0 / math.sqrt(2.0)))
        act = (upval * cumulative).astype(jnp.bfloat16)
        act_ref[rows, cols] = act
        density = jnp.exp(-0.5 * upval * upval) * (1.0 / math.sqrt(2.0 * math.pi))
        grad_up = (grad_act * (cumulative + upval * density)).astype(jnp.bfloat16)
        gup_ref[rows, cols] = grad_up
        mlp = mlp + dot(act, down_ref[:, cols], NT)
        grad_enter = grad_enter + dot(grad_up, up_ref[:, cols], NT)
    block_ref[0] = (y_first + small[5] * mlp).astype(jnp.bfloat16)
    grad_y_first = grad_y + norm_back(grad_enter * small[2], normal, inverse)
    gy1_ref[0] = grad_y_first
    grad_branch = (small[4] * grad_y_first).astype(jnp.bfloat16)
    gbranch_t[:, rows] = grad_branch.T
    gmixed_ref[0] = dot(grad_branch, out_ref[...]).astype(jnp.bfloat16)

    def fold(terms):
        return jnp.sum(terms.reshape(MLP_ROWS // 8, 8, D), 0)

    sums_ref[0] += fold(grad_enter * normal)
    sums_ref[1] += fold(grad_enter)
    sums_ref[2] += fold(grad_y_first * branch)
    sums_ref[3] += fold(grad_y * mlp)

    @pl.when(index == buckets * chunks - 1)
    def _():
        gout_ref[...] = dot(gbranch_t[...], keep_ref[...]).astype(jnp.bfloat16)

        def weight_grads(part, carry):
            cols = pl.ds(pl.multiple_of(part * 256, 256), 256)
            gup_out_ref[:, cols] = dot(enter_t[...], gup_ref[:, cols]).astype(jnp.bfloat16)
            gdown_ref[:, cols] = dot(gmlp_t[...], act_ref[:, cols]).astype(jnp.bfloat16)
            return carry

        lax.fori_loop(0, FF // 256, weight_grads, 0)


def attend_backward(
    lengths_ref, bucket, slot, first_row, first_key, keys, qkv_ref, mixed_ref, gmixed_ref, total_ref, cos_ref, sin_ref, gproj_ref, dk_ref, dv_ref
):
    rows = pl.ds(first_row, BQ)
    key_rows = pl.ds(first_key, keys)
    bias = block_bias(lengths_ref, bucket, first_row, first_key, keys)
    low = lane_ids((BQ, 128)) < HEAD_DIM
    for pair in range(PAIRS):
        base = pair * 384
        queries = qkv_ref[0, rows, base : base + 128]
        keys_rot = qkv_ref[0, key_rows, base + 128 : base + 256]
        values = qkv_ref[0, key_rows, base + 256 : base + 384]
        grad = gmixed_ref[0, rows, pair * 128 : pair * 128 + 128]
        totals = total_ref[0, rows, pair * 128 : pair * 128 + 128]
        product = grad.astype(jnp.float32) * mixed_ref[0, rows, pair * 128 : pair * 128 + 128].astype(jnp.float32)
        grad_q = jnp.zeros((BQ, 128), jnp.float32)
        grad_k = jnp.zeros((keys, 128), jnp.float32)
        grad_v = jnp.zeros((keys, 128), jnp.float32)
        for head in range(2):
            query = head_lanes(queries, head)
            grad_head = head_lanes(grad, head)
            inner = jnp.sum(jnp.where(low == (head == 0), product, 0.0), -1, keepdims=True)
            total = totals[:, head * HEAD_DIM : head * HEAD_DIM + 1]
            attn = jnp.exp(dot(query, keys_rot, NT) + bias - total)
            grad_attn = dot(grad_head, values, NT)
            grad_scores = (attn * (grad_attn - inner)).astype(jnp.bfloat16)
            grad_v = grad_v + dot(attn.astype(jnp.bfloat16), grad_head, TN)
            grad_k = grad_k + dot(grad_scores, query, TN)
            grad_q = grad_q + dot(grad_scores, head_lanes(keys_rot, head))
        cosine = cos_ref[0, rows, :]
        sine = sin_ref[0, rows, :]
        grad_q = grad_q * (HEAD_DIM**-0.5)
        gproj_ref[slot, rows, base : base + 128] = (grad_q * cosine - swap_pairs(grad_q) * sine).astype(jnp.bfloat16)
        lanes = slice(pair * 128, pair * 128 + 128)
        if keys > BQ:
            before = pl.ds(first_key, BQ)
            dk_ref[before, lanes] += grad_k[:BQ]
            dv_ref[before, lanes] += grad_v[:BQ]
            dk_ref[rows, lanes] = grad_k[BQ:]
            dv_ref[rows, lanes] = grad_v[BQ:]
        else:
            dk_ref[rows, lanes] = grad_k
            dv_ref[rows, lanes] = grad_v


def finish_keys(slot, cos_ref, sin_ref, gproj_ref, dk_ref, dv_ref):
    def finish(chunk, carry):
        rows = chunk_rows(chunk)
        cosine = cos_ref[0, rows, :]
        sine = sin_ref[0, rows, :]
        for pair in range(PAIRS):
            grad_k = dk_ref[rows, pair * 128 : pair * 128 + 128]
            turned = grad_k * cosine - swap_pairs(grad_k) * sine
            gproj_ref[slot, rows, pair * 384 + 128 : pair * 384 + 256] = turned.astype(jnp.bfloat16)
            gproj_ref[slot, rows, pair * 384 + 256 : pair * 384 + 384] = dv_ref[rows, pair * 128 : pair * 128 + 128].astype(jnp.bfloat16)
        return carry

    lax.fori_loop(0, LEN // BQ, finish, 0)


def backward_kernel(lengths_ref, qkv_ref, mixed_ref, gmixed_ref, total_ref, cos_ref, sin_ref, gproj_ref, dk_ref, dv_ref):
    bucket = pl.program_id(0)
    shared = (qkv_ref, mixed_ref, gmixed_ref, total_ref, cos_ref, sin_ref, gproj_ref, dk_ref, dv_ref)
    attend_backward(lengths_ref, bucket, 0, 0, 0, BQ, *shared)

    def later(step, carry):
        first_row = pl.multiple_of(step * BQ, BQ)
        attend_backward(lengths_ref, bucket, 0, first_row, pl.multiple_of(first_row - BQ, BQ), 2 * BQ, *shared)
        return carry

    lax.fori_loop(1, LEN // BQ, later, 0)
    finish_keys(0, cos_ref, sin_ref, gproj_ref, dk_ref, dv_ref)


def moments(weight, gradient, first, second):
    first = beta_first * first + (1.0 - beta_first) * gradient
    second = beta_second * second + (1.0 - beta_second) * gradient * gradient
    update = (
        first / (1.0 - beta_first**STEP) / (jnp.sqrt(second / (1.0 - beta_second**STEP)) + adam_eps)
        + decay_rate * weight
    )
    return first, second, update


def planes(which):
    if which == 0:
        return [(slice(None), head, slice(None)) for head in range(2)]
    if which == 1:
        return [(head, slice(None), slice(None)) for head in range(2)]
    return [(slice(None), slice(None))]


def total_of(values_in):
    return jnp.sum(jnp.sum(values_in, 1, keepdims=True), 0, keepdims=True)


def sums_of_squares(tables):
    lanes = lane_ids((1, 512))
    row = jnp.zeros((1, 512), jnp.float32)
    for which, squares in enumerate(tables):
        amount = sum((total_of(plane) for plane in squares[1:]), total_of(squares[0]))
        row = row + jnp.where(lanes == which, amount, 0.0)
    return row


class Everywhere:
    def __init__(self, place, held, got, last, send, recv):
        self.place, self.held, self.got, self.last = place, held, got, last
        self.send, self.recv = send, recv

    def copies(self, stage):
        peers = self.place.peers()
        if stage < 3:
            peer = (CORE, ALONG_Y, ALONG_X)[stage]
            return [remote(self.held.at[stage], self.got.at[stage], self.send.at[stage], self.recv.at[stage], peers[peer])]
        return [
            remote(self.held.at[3], self.last.at[self.place.z], self.send.at[2 + step], self.recv.at[2 + step], peers[step])
            for step in (1, 2, 3)
        ]

    def start(self, stage):
        start_all(self.copies(stage))

    def step(self, stage):
        arrive_all(self.copies(stage))
        if stage == 3:
            return
        total = self.held[stage] + self.got[stage]
        self.held[stage + 1] = total
        if stage == 2:
            self.last[self.place.z] = total
        self.start(stage + 1)

    def total(self):
        return (self.last[0] + self.last[1]) + (self.last[2] + self.last[3])

    def sent(self):
        for stage in range(4):
            sent_all(self.copies(stage))


class Summing:
    def __init__(self, index, place, away, held, got, middle, near, last, send, recv):
        self.weight, self.row, self.count, self.width, self.order = SUMMED[index]
        self.index, self.place = index, place
        self.away, self.held, self.got = away, held, got
        self.middle, self.near, self.last = middle, near, last
        self.send, self.recv = send, recv
        self.rows = pl.ds(self.row, self.count)

    def copies(self, stage, which=(0, 1)):
        place = self.place
        peers = place.peers()

        def copy(source, target, slot, peer):
            return remote(source, target, self.send.at[self.index, slot], self.recv.at[self.index, slot], peers[peer])

        held, rows = self.held, self.rows
        if stage == 0:
            return [copy(self.away(y, rows), self.got.at[y, :, :, rows, :], y, CORE) for y in which]
        if stage == 1:
            if self.order == "yx":
                return [copy(held.at[1, :, :, rows, :], self.middle, 2, ALONG_Y)]
            return [copy(held.at[:, :, 1 - place.x, rows, :], self.middle, 2, ALONG_X)]
        if stage == 2:
            if self.order == "yx":
                return [copy(held.at[0, :, 1 - place.x, rows, :], self.near, 3, ALONG_X)]
            return [copy(held.at[1, :, place.x, rows, :], self.near, 3, ALONG_Y)]
        return [
            copy(held.at[0, (place.z + step) % 4, place.x, rows, :], self.last.at[step - 1], 3 + step, step)
            for step in (1, 2, 3)
        ]

    def start(self, stage, which=(0, 1)):
        start_all(self.copies(stage, which))

    def add(self, where, more):
        held = self.held
        held[where] = (held[where].astype(jnp.float32) + more.astype(jnp.float32)).astype(jnp.bfloat16)

    def arrive(self, stage, which=(0, 1)):
        arrive_all(self.copies(stage, which))
        place, rows = self.place, self.rows

        def block(z, carry):
            if stage == 0:
                for y in which:
                    for x in range(2):
                        self.add((y, z, x, rows, slice(None)), self.got[y, z, x, rows, :])
            elif stage == 1:
                for other in range(2):
                    if self.order == "yx":
                        self.add((0, z, other, rows, slice(None)), self.middle[z, other])
                    else:
                        self.add((other, z, place.x, rows, slice(None)), self.middle[other, z])
            else:
                self.add((0, z, place.x, rows, slice(None)), self.near[z])
            return carry

        lax.fori_loop(0, 4, block, 0)

    def result(self):
        arrive_all(self.copies(3))
        place = self.place
        own = self.held[0, place.z, place.x, self.rows, :].astype(jnp.float32)
        for step in range(3):
            own = own + self.last[step].astype(jnp.float32)
        return own

    def sent(self):
        for stage in range(4):
            sent_all(self.copies(stage))


def middle_shape(index):
    _, _, count, width, order = SUMMED[index]
    return (4, 2, count, width) if order == "yx" else (2, 4, count, width)


def back_pair(bias_ref, bucket, slot, block, qkv_ref, mixed_ref, gmixed_ref, total_ref, cos_ref, sin_ref, gproj_ref, dk_ref, dv_ref):
    rows, key_rows, keys = block_span(block)
    bias = bias_ref[bucket, block, :, :keys]
    keys_rot = qkv_ref[0, key_rows, 128:256]
    query = both_heads(qkv_ref[0, rows, :128])
    grad = gmixed_ref[0, rows, :]
    product = grad.astype(jnp.float32) * mixed_ref[0, rows, :].astype(jnp.float32)
    inner = jnp.sum(both_heads(product), -1, keepdims=True)
    grad = both_heads(grad)
    totals = total_ref[0, rows, :]
    total = jnp.concatenate([totals[:, 0:1], totals[:, HEAD_DIM : HEAD_DIM + 1]], 0)
    attn = jnp.exp(dot(query, keys_rot, NT) + jnp.concatenate([bias, bias], 0) - total)
    grad_attn = dot(grad, qkv_ref[0, key_rows, 256:384], NT)
    grad_scores = (attn * (grad_attn - inner)).astype(jnp.bfloat16)
    grad_v = dot(attn.astype(jnp.bfloat16), grad, TN)
    grad_k = dot(grad_scores, query, TN)
    grad_q = each_head(dot(grad_scores, keys_rot)) * (HEAD_DIM**-0.5)
    turned = grad_q * cos_ref[0, rows, :] - swap_pairs(grad_q) * sin_ref[0, rows, :]
    gproj_ref[bucket, rows, pair_cols(slot, 0)] = turned.astype(jnp.bfloat16)
    old = keys - BH
    if old:
        before = slice(key_rows.start, key_rows.start + old)
        dk_ref[before, :] += grad_k[:old]
        dv_ref[before, :] += grad_v[:old]
    dk_ref[rows, :] = grad_k[old:]
    dv_ref[rows, :] = grad_v[old:]


def pair_cols(slot, which):
    return pl.ds(pl.multiple_of(slot * IN_W + which * 128, 128), 128)


def finish_pair(bucket, slot, cos_ref, sin_ref, gproj_ref, dk_ref, dv_ref):
    def finish(chunk, carry):
        rows = chunk_rows(chunk)
        grad_k = dk_ref[rows, :]
        turned = grad_k * cos_ref[0, rows, :] - swap_pairs(grad_k) * sin_ref[0, rows, :]
        gproj_ref[bucket, rows, pair_cols(slot, 1)] = turned.astype(jnp.bfloat16)
        gproj_ref[bucket, rows, pair_cols(slot, 2)] = dv_ref[rows, :].astype(jnp.bfloat16)
        return carry

    lax.fori_loop(0, LEN // BQ, finish, 0)


def tail_kernel(
    lengths_ref, qkv_ref, mixed_ref, gmixed_ref, total_ref, cos_ref, sin_ref, x_ref, small_ref, sums_ref,
    gy1_hbm, in_hbm, gout_hbm, gup_hbm, gdown_hbm, *refs,
):
    count = len(SUMMED)
    state, refs = refs[:12], refs[12:]
    grad_refs, (xgrad_ref, all_ref, norm_ref), refs = refs[:4], refs[4:7], refs[7:]
    gproj_ref, dk_ref, dv_ref, enter_t, bias_ref, gy1_ref, in_ref, away_in, small_acc, refs = *refs[:9], refs[9:]
    held, got, refs = refs[:4], refs[4:8], refs[8:]
    middle, near, last, refs = refs[:count], refs[count : 2 * count], refs[2 * count : 3 * count], refs[3 * count :]
    small_held, small_got, small_last, norm_held, norm_got, norm_last, refs = *refs[:6], refs[6:]
    send, recv, small_send, small_recv, norm_send, norm_recv, load_sem, late_sem = refs
    bucket = pl.program_id(1)
    slot = PAIRS - 1 - pl.program_id(0)
    step = pl.program_id(0) * MICRO + bucket
    place = Place()
    sources = (None, gout_hbm, gup_hbm, gdown_hbm)

    def away(weight, width):
        if weight == 0:
            return lambda y, rows: away_in.at[y, :, :, rows, :]
        return lambda y, rows: sources[weight].at[:, :, rows, tile_cols(y * 2 + 1, width)]

    items = [
        Summing(
            index, place, away(item[0], item[3]), held[item[0]], got[item[0]], middle[index], near[index], last[index], send, recv
        )
        for index, item in enumerate(SUMMED)
    ]
    out_sum, up_a, down_a, up_b, down_b = items[:5]
    early, late = items[:5], items[5:]
    small_sum = Everywhere(place, small_held, small_got, small_last, small_send, small_recv)
    norm_sum = Everywhere(place, norm_held, norm_got, norm_last, norm_send, norm_recv)

    def loads():
        found = []
        for weight, width in ((1, OUT_W), (2, FF_W), (3, FF_W)):
            for y in range(2):
                source = sources[weight].at[:, :, :, tile_cols(y * 2, width)]
                found.append(pltpu.make_async_copy(source, held[weight].at[y], load_sem.at[weight - 1, y]))
        return found

    def late_loads():
        return [pltpu.make_async_copy(gy1_hbm, gy1_ref, late_sem.at[0]), pltpu.make_async_copy(in_hbm, in_ref, late_sem.at[1])]

    def advance(stage, *which):
        for item in which:
            item.arrive(stage)
            item.start(stage + 1)

    def begin():
        lengths = RunLengths(lengths_ref)
        meet(place)
        for item in early:
            item.start(0)
        start_all(loads())
        start_all(late_loads())
        band_biases(lengths, bias_ref)

        def normalise(index, carry):
            half, chunk = index // (LEN // BQ), index % (LEN // BQ)
            cols = pl.ds(pl.multiple_of(index * BQ, BQ), BQ)
            enter_t[:, cols] = enter_rows(x_ref, small_ref, chunk_rows(chunk), half).T
            return carry

        lax.fori_loop(0, MICRO * LEN // BQ, normalise, 0)

    def at_0_1():
        for load in loads():
            load.wait()
        advance(0, out_sum, up_a, down_a)

    events = {
        (0, 0): begin,
        (0, 1): at_0_1,
        (0, 2): lambda: advance(0, up_b, down_b),
        (2, 1): lambda: advance(1, out_sum),
        (2, 2): lambda: advance(1, down_a),
        (3, 1): lambda: advance(1, up_a),
        (4, 0): lambda: advance(1, down_b),
        (4, 1): lambda: advance(2, out_sum),
        (5, 0): lambda: advance(1, up_b),
        (5, 1): lambda: advance(2, up_a),
        (6, 0): lambda: advance(2, up_b, down_a),
    }

    def progress(point):
        for (moment, where), event in events.items():
            if where == point:
                pl.when(step == moment)(event)

    shared = (qkv_ref, mixed_ref, gmixed_ref, total_ref, cos_ref, sin_ref, gproj_ref, dk_ref, dv_ref)
    for point, blocks in enumerate(((0, 1, 2), (3, 4, 5), (6, 7))):
        progress(point)
        for block in blocks:
            back_pair(bias_ref, bucket, slot, block, *shared)
    finish_pair(bucket, slot, cos_ref, sin_ref, gproj_ref, dk_ref, dv_ref)

    def grad_tile():
        right = gproj_ref[:, :, tile_cols(slot, IN_W)].reshape(MICRO * LEN, IN_W)
        return dot(enter_t[...], right).astype(jnp.bfloat16).reshape(4, 2, 64, IN_W)

    @pl.when((bucket == 1) & (slot % 2 == 1))
    def _():
        away_in[slot // 2] = grad_tile()

    @pl.when((bucket == 1) & (slot % 2 == 0))
    def _():
        held[0][slot // 2] = grad_tile()

    for which in range(2):

        @pl.when((bucket == 1) & (slot == which * 2 + 1))
        def _():
            for item in late:
                item.start(0, (which,))

    @pl.when((bucket == 1) & (slot == 2))
    def _():
        for item in late:
            item.arrive(0, (1,))
            item.start(1)

    @pl.when((bucket == 1) & (slot == 0))
    def _():
        for item in late:
            item.arrive(0, (0,))
            item.arrive(1)
            item.start(2)
        small_acc[...] = jnp.zeros_like(small_acc)
        for load in late_loads():
            load.wait()

        def data_grad(step, carry):
            for stage, item, moment in ((2, down_b, 1), (2, late[0], 2), (2, late[1], 3)):
                pl.when(step == moment)(lambda: advance(stage, item))
            index = step // (LEN // LAST_ROWS)
            rows = pl.ds(pl.multiple_of(step % (LEN // LAST_ROWS) * LAST_ROWS, LAST_ROWS), LAST_ROWS)
            grad_enter = dot(gproj_ref[index, rows, :], in_ref[...], NT)
            normal, inverse = norm_parts(x_ref[index, rows, :].astype(jnp.float32))
            back = norm_back(grad_enter * small_ref[0:1, :], normal, inverse)
            xgrad_ref[index, rows, :] = (gy1_ref[index, rows, :] + back).astype(jnp.bfloat16)
            small_acc[0] += jnp.sum((grad_enter * normal).reshape(LAST_ROWS // 8, 8, D), 0)
            small_acc[1] += jnp.sum(grad_enter.reshape(LAST_ROWS // 8, 8, D), 0)
            return carry

        lax.fori_loop(0, MICRO * LEN // LAST_ROWS, data_grad, 0)

        rows = [jnp.sum(small_acc[row], 0, keepdims=True) for row in range(2)]
        rows += [jnp.sum(sums_ref[row], 0, keepdims=True) for row in range(4)]
        weights_sq = []
        for which in range(4):
            weights_sq.append([state[3 * which][plane] * state[3 * which][plane] for plane in planes(which)])
        rows.append(sums_of_squares(weights_sq))
        rows.append(jnp.zeros((1, D), jnp.float32))
        small_held[0] = jnp.concatenate(rows, 0)
        small_sum.start(0)

        grads = [
            None,
            out_sum.result().T,
            jnp.concatenate([up_a.result(), up_b.result()], 0),
            jnp.concatenate([down_a.result(), down_b.result()], 0),
        ]
        grad_refs[1][0] = grads[1][:HEAD_DIM]
        grad_refs[1][1] = grads[1][HEAD_DIM:]
        grad_refs[2][...] = grads[2]
        grad_refs[3][...] = grads[3]
        small_sum.step(0)
        parts = [item.result() for item in late]
        part = jnp.concatenate(parts, 0)
        for head in range(2):
            pieces = [part[:, which * 128 + head * HEAD_DIM : which * 128 + head * HEAD_DIM + HEAD_DIM] for which in range(3)]
            grad_refs[0][:, head, :] = jnp.concatenate(pieces, 1)
        updates_sq = []
        for which in range(4):
            squares = []
            for plane in planes(which):
                weight, first, second = (state[3 * which + kind][plane] for kind in range(3))
                update = moments(weight, grad_refs[which][plane], first, second)[2]
                squares.append(update * update)
            updates_sq.append(squares)
        norm_held[0] = jnp.broadcast_to(sums_of_squares(updates_sq)[:, :128], (8, 128))
        norm_sum.start(0)
        small_sum.step(1)
        norm_sum.step(0)
        small_sum.step(2)
        norm_sum.step(1)
        small_sum.step(3)
        norm_sum.step(2)
        norm_sum.step(3)
        all_ref[...] = small_sum.total()
        norm_ref[...] = norm_sum.total()
        for item in early + late:
            item.sent()
        small_sum.sent()
        norm_sum.sent()


def lamb_kernel(*refs):
    state, grads, refs = refs[:12], refs[12:16], refs[16:]
    small_ref, small_first_ref, small_second_ref, all_ref, norm_ref, xgrad_ref, refs = *refs[:6], refs[6:]
    outs, (grad_ref, new_ref, first_ref, second_ref, norms_ref, xgrad_out_ref) = refs[:16], refs[16:]
    xgrad_out_ref[...] = xgrad_ref[...]
    weight_norm = jnp.sqrt(all_ref[6:7, 0:128])
    update_sq = norm_ref[0:1, :]
    ratio = learn_rate * weight_norm * lax.rsqrt(update_sq + 1e-12)
    for which in range(4):
        scale = ratio[:, which : which + 1]
        for plane in planes(which):
            weight, first, second = (state[3 * which + kind][plane] for kind in range(3))
            first, second, update = moments(weight, grads[which][plane], first, second)
            new = weight - scale * update
            outs[4 * which][plane] = new
            outs[4 * which + 1][plane] = first
            outs[4 * which + 2][plane] = second
            outs[4 * which + 3][plane] = new.astype(jnp.bfloat16)
    small = small_ref[...]
    small_grad = all_ref[0:6, :]
    grad_ref[...] = small_grad
    first, second, update = moments(small, small_grad, small_first_ref[...], small_second_ref[...])
    small_sq = jnp.sum(small * small, 1, keepdims=True)
    change_sq = jnp.sum(update * update, 1, keepdims=True)
    new_ref[...] = small - learn_rate * jnp.sqrt(small_sq) * lax.rsqrt(change_sq + 1e-12) * update
    first_ref[...] = first
    second_ref[...] = second
    lanes = lane_ids((1, 128))
    top = jnp.where(lanes < 4, weight_norm, 0.0)
    bottom = jnp.where(lanes < 4, jnp.sqrt(update_sq), 0.0)
    for row in range(6):
        top = top + jnp.where(lanes == 4 + row, jnp.sqrt(small_sq[row : row + 1]), 0.0)
        bottom = bottom + jnp.where(lanes == 4 + row, jnp.sqrt(change_sq[row : row + 1]), 0.0)
    norms_ref[0:1, :] = top[:, :10]
    norms_ref[1:2, :] = bottom[:, :10]


def whole(shape):
    return pl.BlockSpec(shape, lambda *ids: (0,) * len(shape), pipeline_mode=pl.Buffered(1))


def per_bucket(*shape):
    return pl.BlockSpec((1,) + shape, lambda b: (b, 0, 0))


def bf16(*shape):
    return jax.ShapeDtypeStruct(shape, jnp.bfloat16)


def f32(*shape):
    return jax.ShapeDtypeStruct(shape, jnp.float32)


def vmem16(*shape):
    return pltpu.VMEM(shape, jnp.bfloat16)


def vmem32(*shape):
    return pltpu.VMEM(shape, jnp.float32)


SCALARS = pl.BlockSpec(memory_space=pltpu.SMEM)
ANYWHERE = pl.BlockSpec(memory_space=pl.ANY)


def params(count, collective=None):
    more = {} if collective is None else dict(collective_id=collective, has_side_effects=True)
    return pltpu.CompilerParams(dimension_semantics=("arbitrary",) * count, vmem_limit_bytes=VMEM_LIMIT, **more)


def turn_tables(lengths):
    ends = jnp.cumsum(lengths, axis=1)
    position = jnp.arange(LEN, dtype=jnp.int32)
    passed = position[None, :, None] >= ends[:, None, : CLIPS - 1]
    start = jnp.max(jnp.where(passed, ends[:, None, : CLIPS - 1], 0), axis=2)
    offset = (position[None, :] - start).astype(jnp.float32)
    frequency = jnp.exp(jnp.arange(HEAD_DIM // 2, dtype=jnp.float32) * (-2.0 * math.log(10000.0) / HEAD_DIM))
    angles = offset[:, :, None] * frequency
    cosine = jnp.repeat(jnp.cos(angles), 2, axis=-1)
    sine = jnp.sin(angles)
    sine = jnp.stack([-sine, sine], axis=-1).reshape(cosine.shape)
    return jnp.concatenate([cosine, cosine], -1), jnp.concatenate([sine, sine], -1)


def attention_forward(lengths, x, small, cosine, sine, in_mat):
    count = x.shape[0]
    return pl.pallas_call(
        forward_kernel,
        grid=(count,),
        in_specs=[SCALARS, per_bucket(LEN, D), whole((6, D)), per_bucket(LEN, 128), per_bucket(LEN, 128), whole((D, 3 * D))],
        out_specs=[per_bucket(LEN, 3 * D), per_bucket(LEN, D), per_bucket(LEN, D), per_bucket(LEN, D)],
        out_shape=[bf16(count, LEN, 3 * D), bf16(count, LEN, D), f32(count, LEN, D), bf16(count, LEN, D)],
        compiler_params=params(1),
        name="attention_forward",
    )(lengths, x, small, cosine, sine, in_mat)


def gather_forward(lengths, x, small, weights):
    shapes = [(4, 2, 64, 4 * width) for width in (IN_W, OUT_W, FF_W, FF_W)]

    def per_pair(width):
        return pl.BlockSpec((1, LEN, width), lambda pair, bucket: (bucket, 0, pair))

    return pl.pallas_call(
        gather_kernel,
        grid=(PAIRS, MICRO),
        in_specs=[SCALARS, whole((MICRO, LEN, D)), whole((6, D)), whole((4, 32, 128))] + [whole(item.shape) for item in weights],
        out_specs=[per_pair(IN_W), per_pair(128), per_pair(128)] + [whole((MICRO, LEN, 128))] * 2 + [ANYWHERE] * 4,
        out_shape=[bf16(MICRO, LEN, 3 * D), bf16(MICRO, LEN, D), f32(MICRO, LEN, D)]
        + [f32(MICRO, LEN, 128)] * 2
        + [bf16(*shape) for shape in shapes],
        scratch_shapes=[vmem16(*shape) for shape in shapes]
        + [
            vmem16(64, SHARD_W),
            vmem16(MICRO, LEN, D),
            vmem32(MICRO, BLOCKS, BH, KEYS),
            pltpu.SemaphoreType.DMA((6, 8)),
            pltpu.SemaphoreType.DMA((6, 8)),
            pltpu.SemaphoreType.DMA((4,)),
            pltpu.SemaphoreType.DMA((6,)),
        ],
        compiler_params=params(2, 1),
        name="gather_forward",
    )(lengths, x, small, position_steps(), *weights)


def mlp_both(lengths, x, cot, mixed, small, out_mat, up_mat, down_mat):
    count = x.shape[0]
    rows = count * LEN

    def chunked(width):
        return pl.BlockSpec((1, MLP_ROWS, width), lambda b, i: (b, i, 0))

    return pl.pallas_call(
        mlp_kernel,
        grid=(count, LEN // MLP_ROWS),
        in_specs=[SCALARS, chunked(D), chunked(D), chunked(D), whole((6, D)), whole((D, D)), whole((D, FF)), whole((D, FF))],
        out_specs=[chunked(D), chunked(D), chunked(D), whole((4, 8, D)), whole((D, D)), whole((D, FF)), whole((D, FF))],
        out_shape=[
            bf16(count, LEN, D), f32(count, LEN, D), bf16(count, LEN, D), f32(4, 8, D), bf16(D, D), bf16(D, FF), bf16(D, FF),
        ],
        scratch_shapes=[
            vmem16(rows, FF), vmem16(rows, FF), vmem16(rows, D), vmem16(D, rows), vmem16(D, rows), vmem16(D, rows),
        ],
        compiler_params=params(2),
        name="mlp_both",
    )(lengths, x, cot, mixed, small, out_mat, up_mat, down_mat)


def attention_backward(lengths, qkv, mixed, gmixed, totals, cosine, sine):
    count = qkv.shape[0]
    return pl.pallas_call(
        backward_kernel,
        grid=(count,),
        in_specs=[SCALARS, per_bucket(LEN, 3 * D), per_bucket(LEN, D), per_bucket(LEN, D), per_bucket(LEN, D), per_bucket(LEN, 128), per_bucket(LEN, 128)],
        out_specs=per_bucket(LEN, 3 * D),
        out_shape=bf16(count, LEN, 3 * D),
        scratch_shapes=[vmem32(LEN, D), vmem32(LEN, D)],
        compiler_params=params(1),
        name="attention_backward",
    )(lengths, qkv, mixed, gmixed, totals, cosine, sine)


def backward_tail(lengths, qkv, mixed, gmixed, totals, cosine, sine, x, small, gy1, sums, in_mat, gout, gup, gdown, state):
    widths = (IN_W, OUT_W, FF_W, FF_W)
    dma = pltpu.SemaphoreType.DMA
    count = len(SUMMED)
    grad_shapes = [f32(*state[3 * which].shape) for which in range(4)]

    def per_pair(width):
        return pl.BlockSpec((1, LEN, width), lambda pair, bucket: (bucket, 0, PAIRS - 1 - pair))

    tables = pl.BlockSpec((1, LEN, 128), lambda pair, bucket: (bucket, 0, 0))
    return pl.pallas_call(
        tail_kernel,
        grid=(PAIRS, MICRO),
        in_specs=[SCALARS, per_pair(IN_W), per_pair(128), per_pair(128), per_pair(128), tables, tables]
        + [whole((MICRO, LEN, D)), whole((6, D)), whole((4, 8, D))]
        + [ANYWHERE] * 5
        + [whole(item.shape) for item in state],
        out_specs=[whole(item.shape) for item in grad_shapes] + [whole((MICRO, LEN, D)), whole((8, D)), whole((8, 128))],
        out_shape=grad_shapes + [bf16(MICRO, LEN, D), f32(8, D), f32(8, 128)],
        scratch_shapes=[
            vmem16(MICRO, LEN, 3 * D), vmem32(LEN, 128), vmem32(LEN, 128), vmem16(D, MICRO * LEN), vmem32(MICRO, BLOCKS, BH, KEYS),
            vmem32(MICRO, LEN, D), vmem16(D, 3 * D), vmem16(2, 4, 2, 64, IN_W), vmem32(2, 8, D),
        ]
        + [vmem16(2, 4, 2, 64, width) for width in widths]
        + [vmem16(2, 4, 2, 64, width) for width in widths]
        + [vmem16(*middle_shape(index)) for index in range(count)]
        + [vmem16(4, SUMMED[index][2], SUMMED[index][3]) for index in range(count)]
        + [vmem16(3, SUMMED[index][2], SUMMED[index][3]) for index in range(count)]
        + [vmem32(4, 8, D), vmem32(3, 8, D), vmem32(4, 8, D), vmem32(4, 8, 128), vmem32(3, 8, 128), vmem32(4, 8, 128)]
        + [dma((count, 7)), dma((count, 7)), dma((6,)), dma((6,)), dma((6,)), dma((6,)), dma((3, 2)), dma((2,))],
        compiler_params=params(2, 2),
        name="backward_tail",
    )(lengths, qkv, mixed, gmixed, totals, cosine, sine, x, small, sums, gy1, in_mat, gout, gup, gdown, *state)


def lamb_all(state, grads, small, small_first, small_second, everything, norm_squares, input_grad):
    outs = []
    for which in range(4):
        shape = state[3 * which].shape
        outs += [f32(*shape)] * 3 + [bf16(*shape)]
    outs += [f32(6, D)] * 4 + [f32(2, 10), bf16(MICRO, LEN, D)]
    return pl.pallas_call(
        lamb_kernel,
        out_shape=outs,
        compiler_params=pltpu.CompilerParams(vmem_limit_bytes=VMEM_LIMIT),
        name="lamb_all",
    )(*state, *grads, small, small_first, small_second, everything, norm_squares, input_grad)


def tile_shard(in_proj, out_proj, up_proj, down_proj):
    depth, heads_here, _ = in_proj.shape
    out_cols = out_proj.reshape(heads_here * HEAD_DIM, depth).T
    parts = [in_proj.reshape(depth, -1), out_cols, up_proj, down_proj.T]
    return jnp.concatenate(parts, axis=1).astype(jnp.bfloat16)


def on_device(
    frames, cotangent, clip_lengths, in_proj, out_proj, up_proj, down_proj, small_params,
    in_first, in_second, out_first, out_second, up_first, up_second, down_first, down_second,
    small_first, small_second,
):
    lengths = clip_lengths
    qkv, mixed, totals, cosine, sine, in_full, out_full, up_full, down_full = gather_forward(
        lengths, frames, small_params, (in_proj, out_proj, up_proj, down_proj.T)
    )
    block_out, gy1, gmixed, sums, gout, gup, gdown = mlp_both(
        lengths, frames, cotangent, mixed, small_params, out_full.reshape(D, D), up_full.reshape(D, FF), down_full.reshape(D, FF)
    )
    state = (
        in_proj, in_first, in_second, out_proj, out_first, out_second, up_proj, up_first, up_second, down_proj.T, down_first.T, down_second.T,
    )
    *grads, input_grad, everything, norm_squares = backward_tail(
        lengths, qkv, mixed, gmixed, totals, cosine, sine, frames, small_params, gy1, sums, in_full.reshape(D, 3 * D),
        gout.reshape(4, 2, 64, D), gup.reshape(4, 2, 64, FF), gdown.reshape(4, 2, 64, FF), state,
    )
    *outs, input_grad = lamb_all(state, grads, small_params, small_first, small_second, everything, norm_squares, input_grad)
    outs[12:16] = [item.T for item in outs[12:16]]
    return (block_out, input_grad, *outs)


def on_any_mesh(
    frames, cotangent, clip_lengths, in_proj, out_proj, up_proj, down_proj, small_params,
    in_first, in_second, out_first, out_second, up_first, up_second, down_first, down_second,
    small_first, small_second,
):
    rows_here = frames.shape[1]
    own_buckets = rows_here // LEN
    first_bucket = lax.axis_index("tensor") * own_buckets
    lengths = lax.dynamic_slice_in_dim(clip_lengths, first_bucket, own_buckets, 1).reshape(-1, CLIPS)
    count = MICRO * own_buckets
    x = frames.reshape(count, LEN, D)
    cot = cotangent.reshape(count, LEN, D)
    tensor_size = lax.axis_size("tensor")
    dp_size = lax.axis_size("dp")
    depth = in_proj.shape[0]
    heads_here = in_proj.shape[1]
    ff_here = up_proj.shape[1]

    shard = tile_shard(in_proj, out_proj, up_proj, down_proj)
    gathered = lax.all_gather(shard, ("dp", "tensor"), axis=0)
    gathered = gathered.reshape(dp_size, tensor_size, depth, shard.shape[1])
    gathered = jnp.moveaxis(gathered, 1, 2).reshape(D, tensor_size, shard.shape[1])
    edge0 = heads_here * 192
    edge1 = edge0 + heads_here * HEAD_DIM
    edge2 = edge1 + ff_here
    in_mat = gathered[:, :, :edge0].reshape(D, PAIRS, 2, 3, HEAD_DIM).transpose(0, 1, 3, 2, 4).reshape(D, 3 * D)
    out_mat = gathered[:, :, edge0:edge1].reshape(D, D)
    up_mat = gathered[:, :, edge1:edge2].reshape(D, FF)
    down_mat = gathered[:, :, edge2:].reshape(D, FF)

    cosine, sine = turn_tables(lengths)
    qkv, mixed, totals, enter1 = attention_forward(lengths, x, small_params, cosine, sine, in_mat)
    block_out, grad_y_first, grad_mixed, sums, grad_out, grad_upw, grad_down = mlp_both(
        lengths, x, cot, mixed, small_params, out_mat, up_mat, down_mat
    )

    def weight_grad(left, right):
        return dot(left.reshape(-1, left.shape[-1]), right.reshape(-1, right.shape[-1]), TN).astype(jnp.bfloat16)

    grad_proj = attention_backward(lengths, qkv, mixed, grad_mixed, totals, cosine, sine)
    grad_in = weight_grad(enter1, grad_proj)
    grad_in = grad_in.reshape(D, PAIRS, 3, 2, HEAD_DIM).transpose(0, 1, 3, 2, 4)

    def by_owner(mat):
        return jnp.moveaxis(mat.reshape(dp_size, depth, tensor_size, -1), 2, 1)

    stacked = jnp.concatenate([by_owner(grad_in), by_owner(grad_out), by_owner(grad_upw), by_owner(grad_down)], axis=-1)
    owned = lax.psum_scatter(
        stacked.reshape(dp_size * tensor_size, depth, -1), ("dp", "tensor"), scatter_dimension=0, tiled=False
    ).astype(jnp.float32)

    grad_enter1 = dot(grad_proj.reshape(-1, 3 * D), in_mat, NT).reshape(count, LEN, D)
    normal1, inverse1 = norm_parts(x.astype(jnp.float32))
    input_grad = (grad_y_first + norm_back(grad_enter1 * small_params[0], normal1, inverse1)).astype(jnp.bfloat16)
    late = jnp.sum(sums, axis=1)
    small_terms = jnp.stack(
        [jnp.sum(grad_enter1 * normal1, (0, 1)), jnp.sum(grad_enter1, (0, 1)), late[0], late[1], late[2], late[3]]
    )

    grads = (
        owned[:, :edge0].reshape(in_proj.shape),
        owned[:, edge0:edge1].T.reshape(out_proj.shape),
        owned[:, edge1:edge2],
        owned[:, edge2:].T,
    )
    weights_in = (in_proj, out_proj, up_proj, down_proj)
    firsts = (in_first, out_first, up_first, down_first)
    seconds = (in_second, out_second, up_second, down_second)
    own_squares = jnp.stack([jnp.sum(weight * weight) for weight in weights_in])
    small_grad, weight_squares = lax.psum((small_terms, own_squares), ("dp", "tensor"))
    new_firsts = []
    new_seconds = []
    updates = []
    for weight, gradient, first, second in zip(weights_in, grads, firsts, seconds):
        first = beta_first * first + (1.0 - beta_first) * gradient
        second = beta_second * second + (1.0 - beta_second) * gradient * gradient
        update = (
            first / (1.0 - beta_first**STEP) / (jnp.sqrt(second / (1.0 - beta_second**STEP)) + adam_eps)
            + decay_rate * weight
        )
        new_firsts.append(first)
        new_seconds.append(second)
        updates.append(update)
    update_squares = lax.psum(jnp.stack([jnp.sum(update * update) for update in updates]), ("dp", "tensor"))
    trust_ratio = jnp.sqrt(weight_squares) * lax.rsqrt(update_squares + 1e-12)
    new_weights = [weights_in[index] - learn_rate * trust_ratio[index] * updates[index] for index in range(4)]
    small_first_new = beta_first * small_first + (1.0 - beta_first) * small_grad
    small_second_new = beta_second * small_second + (1.0 - beta_second) * small_grad * small_grad
    small_update = (
        small_first_new / (1.0 - beta_first**STEP) / (jnp.sqrt(small_second_new / (1.0 - beta_second**STEP)) + adam_eps)
        + decay_rate * small_params
    )
    small_weight_sq = jnp.sum(small_params * small_params, axis=1, keepdims=True)
    small_update_sq = jnp.sum(small_update * small_update, axis=1, keepdims=True)
    small_new = small_params - learn_rate * jnp.sqrt(small_weight_sq) * lax.rsqrt(small_update_sq + 1e-12) * small_update
    norms = jnp.stack(
        [
            jnp.concatenate([jnp.sqrt(weight_squares), jnp.sqrt(small_weight_sq).reshape(-1)]),
            jnp.concatenate([jnp.sqrt(update_squares), jnp.sqrt(small_update_sq).reshape(-1)]),
        ]
    )
    outputs = [block_out.reshape(frames.shape), input_grad.reshape(frames.shape)]
    for new, first, second in zip(new_weights, new_firsts, new_seconds):
        outputs += [new, first, second, new.astype(jnp.bfloat16)]
    return tuple(outputs + [small_grad, small_new, small_first_new, small_second_new, norms])


def solution(mesh):
    rows = P(None, ("dp", "tensor"), None)
    in_spec = P("dp", "tensor", None)
    out_spec = P("tensor", None, "dp")
    up_spec = P("dp", "tensor")
    down_spec = P("tensor", "dp")
    shape = dict(mesh.shape)
    small_slice = shape["dp"] == HERE_DP and shape["tensor"] == HERE_TENSOR
    return jax.shard_map(
        on_device if small_slice else on_any_mesh,
        mesh=mesh,
        in_specs=(
            rows, rows, P(None, "dp", None), in_spec, out_spec, up_spec, down_spec, P(),
            in_spec, in_spec, out_spec, out_spec, up_spec, up_spec, down_spec, down_spec, P(), P(),
        ),
        out_specs=(rows, rows) + (in_spec,) * 4 + (out_spec,) * 4 + (up_spec,) * 4 + (down_spec,) * 4 + (P(),) * 5,
        check_vma=False,
    )
```

```python
import functools
import math

import jax
import jax.numpy as jnp
import numpy as np
from jax import lax
from jax.experimental import pallas as pl
from jax.experimental.pallas import tpu as pltpu
from jax.sharding import PartitionSpec as P

D = 512
HEADS = 8
HEAD_DIM = 64
FF = 2048
PAIRS = HEADS // 2
WINDOW = 250
LEN = 1024
CLIPS = 4
MICRO = 2
STEP = 3

BQ = 256
BH = 128
BLOCKS = LEN // BH
KEYS = 3 * BH
MLP_ROWS = 512
LAST_ROWS = 512
VMEM_LIMIT = 62 * 1024 * 1024

beta_first = 0.5
beta_second = 0.5
adam_eps = 1e-06
decay_rate = 0.01
learn_rate = 0.3

NT = (((1,), (1,)), ((), ()))
NN = (((1,), (0,)), ((), ()))
TN = (((0,), (0,)), ((), ()))


def dot(a, b, dims=NN):
    return lax.dot_general(a, b, dims, preferred_element_type=jnp.float32)


def norm_parts(rows):
    mean = jnp.mean(rows, -1, keepdims=True)
    centred = rows - mean
    inverse = lax.rsqrt(jnp.mean(centred * centred, -1, keepdims=True) + 1e-05)
    return centred * inverse, inverse


def norm_back(scaled, normal, inverse):
    return inverse * (
        scaled
        - jnp.mean(scaled, -1, keepdims=True)
        - normal * jnp.mean(scaled * normal, -1, keepdims=True)
    )


def lane_ids(shape):
    return lax.broadcasted_iota(jnp.int32, shape, len(shape) - 1)


def swap_pairs(rows):
    even = (lane_ids(rows.shape) & 1) == 0
    return jnp.where(even, pltpu.roll(rows, 127, 1), pltpu.roll(rows, 1, 1))


def run_starts(lengths_ref, bucket, position):
    end0 = lengths_ref[bucket, 0]
    end1 = end0 + lengths_ref[bucket, 1]
    end2 = end1 + lengths_ref[bucket, 2]
    start = jnp.where(position >= end0, end0, 0)
    start = jnp.where(position >= end1, end1, start)
    return jnp.where(position >= end2, end2, start), position < end2


def block_bias(lengths_ref, bucket, first_row, first_key, keys):
    position = first_row + lax.broadcasted_iota(jnp.int32, (BQ, 1), 0)
    start, _ = run_starts(lengths_ref, bucket, position)
    lowest = jnp.maximum(start, position - (WINDOW - 1))
    key = first_key + lax.broadcasted_iota(jnp.int32, (BQ, keys), 1)
    return jnp.where((key >= lowest) & (key <= position), 0.0, -1e30)


def head_lanes(tile, head):
    return jnp.where((lane_ids(tile.shape) // HEAD_DIM) == head, tile, jnp.zeros_like(tile))


MESH = pl.DeviceIdType.MESH
HERE_DP = 8
HERE_TENSOR = 4
IN_W, OUT_W, FF_W = 384, 128, 512
SHARD_W = IN_W + OUT_W + 2 * FF_W
CORE, ALONG_Y, ALONG_X = "core", "y", "x"

GATHERED = (
    (0, 0, 64, IN_W, 0, "xy"),
    (1, 0, 64, OUT_W, IN_W, "yx"),
    (2, 0, 32, FF_W, IN_W + OUT_W, "xy"),
    (3, 0, 32, FF_W, IN_W + OUT_W + FF_W, "yx"),
    (2, 32, 32, FF_W, IN_W + OUT_W, "xy"),
    (3, 32, 32, FF_W, IN_W + OUT_W + FF_W, "yx"),
)
IN, OUT, UP_A, DOWN_A, UP_B, DOWN_B = range(6)
SUMMED = (
    (1, 0, 64, OUT_W, "yx"),
    (2, 0, 32, FF_W, "yx"),
    (3, 0, 32, FF_W, "xy"),
    (2, 32, 32, FF_W, "yx"),
    (3, 32, 32, FF_W, "xy"),
    (0, 0, 32, IN_W, "yx"),
    (0, 32, 32, IN_W, "yx"),
)


class Place:
    def __init__(self):
        dp = lax.axis_index("dp")
        tensor = lax.axis_index("tensor")
        self.z, self.x = dp // 2, dp % 2
        self.y, self.c = tensor // 2, tensor % 2

    def device(self, dz=0, x=None, y=None, c=None):
        x = self.x if x is None else x
        y = self.y if y is None else y
        c = self.c if c is None else c
        return {"dp": (self.z + dz) % 4 * 2 + x, "tensor": y * 2 + c}

    def peers(self):
        return {
            CORE: self.device(c=1 - self.c),
            ALONG_Y: self.device(y=1 - self.y),
            ALONG_X: self.device(x=1 - self.x),
            1: self.device(dz=1),
            2: self.device(dz=2),
            3: self.device(dz=3),
        }


def tile_cols(slot, width):
    return pl.ds(pl.multiple_of(slot * width, 128), width)


def remote(source, target, send, recv, device):
    return pltpu.make_async_remote_copy(
        src_ref=source, dst_ref=target, send_sem=send, recv_sem=recv, device_id=device, device_id_type=MESH
    )


def meet(place):
    barrier = pltpu.get_barrier_semaphore()
    peers = place.peers()
    for device in peers.values():
        pl.semaphore_signal(barrier, inc=1, device_id=device, device_id_type=MESH)
    pl.semaphore_wait(barrier, len(peers))


def start_all(copies):
    for copy in copies:
        copy.start()


def arrive_all(copies):
    for copy in copies:
        copy.wait_recv()


def sent_all(copies):
    for copy in copies:
        copy.wait_send()


def gather_copies(index, stage, place, shard, weights, send, recv):
    weight, row, count, width, offset, order = GATHERED[index]
    full = weights[weight]
    rows = pl.ds(row, count)
    peers = place.peers()

    def copy(source, target, slot, peer):
        return remote(source, target, send.at[index, slot], recv.at[index, slot], peers[peer])

    def cols(slot):
        return slice(slot * width, slot * width + width)

    if stage == 0:
        return [
            copy(shard.at[rows, offset : offset + width], full.at[place.z, place.x, rows, cols(0)], step - 1, step)
            for step in (1, 2, 3)
        ]
    if stage == 1:
        part = full.at[:, place.x, rows, cols(0)]
        if order == "xy":
            return [copy(part, part, 3, ALONG_X)]
        return [copy(part, full.at[:, place.x, rows, cols(2)], 3, ALONG_Y)]
    if stage == 2:
        if order == "xy":
            return [copy(full.at[:, :, rows, cols(0)], full.at[:, :, rows, cols(2)], 4, ALONG_Y)]
        parts = [full.at[:, place.x, rows, cols(slot)] for slot in (0, 2)]
        return [copy(part, part, 4 + index, ALONG_X) for index, part in enumerate(parts)]
    slot = stage * 2 - 6
    return [copy(full.at[:, :, rows, cols(slot)], full.at[:, :, rows, cols(slot + 1)], stage + 3, CORE)]


def project_rows(rows, enter, cosine, sine, weight, qkv_ref, base):
    part = dot(enter, weight)
    for which in range(2):
        piece = part[:, which * 128 : which * 128 + 128]
        turned = piece * cosine + swap_pairs(piece) * sine
        if which == 0:
            turned = turned * (HEAD_DIM**-0.5)
        qkv_ref[0, rows, base + which * 128 : base + which * 128 + 128] = turned.astype(jnp.bfloat16)
    qkv_ref[0, rows, base + 256 : base + 384] = part[:, 256:].astype(jnp.bfloat16)


def attend_forward(lengths_ref, bucket, first_row, first_key, keys, qkv_ref, mixed_ref, total_ref):
    rows = pl.ds(first_row, BQ)
    key_rows = pl.ds(first_key, keys)
    bias = block_bias(lengths_ref, bucket, first_row, first_key, keys)
    for pair in range(PAIRS):
        base = pair * 384
        queries = qkv_ref[0, rows, base : base + 128]
        keys_rot = qkv_ref[0, key_rows, base + 128 : base + 256]
        values = qkv_ref[0, key_rows, base + 256 : base + 384]
        outs = []
        totals = []
        for head in range(2):
            scores = dot(head_lanes(queries, head), keys_rot, NT) + bias
            top = jnp.max(scores, -1, keepdims=True)
            powers = jnp.exp(scores - top)
            total = jnp.sum(powers, -1, keepdims=True)
            outs.append(dot(powers.astype(jnp.bfloat16), values) / total)
            totals.append(jnp.broadcast_to(top + jnp.log(total), (BQ, 128)))
        low = lane_ids((BQ, 128)) < HEAD_DIM
        mixed_ref[0, rows, pair * 128 : pair * 128 + 128] = jnp.where(low, outs[0], outs[1]).astype(jnp.bfloat16)
        total_ref[0, rows, pair * 128 : pair * 128 + 128] = jnp.where(low, totals[0], totals[1])


def turn_tables_here(lengths_ref, steps_ref, cos_ref, sin_ref):
    lanes = lane_ids((8, 128))
    frequency = jnp.exp(((lanes & (HEAD_DIM - 1)) // 2).astype(jnp.float32) * (-2.0 * math.log(10000.0) / HEAD_DIM))
    sign = jnp.where((lane_ids((1, 128)) & 1) == 0, -1.0, 1.0)
    fine_cos, fine_sin = steps_ref[2:3], steps_ref[3:4]
    for bucket in range(MICRO):
        end0 = lengths_ref[bucket, 0]
        end1 = end0 + lengths_ref[bucket, 1]
        end2 = end1 + lengths_ref[bucket, 2]
        row = lax.broadcasted_iota(jnp.int32, (8, 128), 0)
        start = jnp.where(row == 0, 0, jnp.where(row == 1, end0, jnp.where(row == 2, end1, end2)))
        angle = start.astype(jnp.float32) * frequency
        run_cos, run_sin = jnp.cos(angle), jnp.sin(angle)

        def chunk_tables(chunk, carry):
            coarse = pl.ds(pl.multiple_of(chunk * 8, 8), 8)
            coarse_cos, coarse_sin = steps_ref[0, coarse, :][:, None, :], steps_ref[1, coarse, :][:, None, :]
            at_cos = (coarse_cos * fine_cos - coarse_sin * fine_sin).reshape(BQ, 128)
            at_sin = (coarse_sin * fine_cos + coarse_cos * fine_sin).reshape(BQ, 128)
            position = chunk * BQ + lax.broadcasted_iota(jnp.int32, (BQ, 128), 0)
            first_cos, first_sin = run_cos[0:1], run_sin[0:1]
            for run, end in enumerate((end0, end1, end2)):
                first_cos = jnp.where(position >= end, run_cos[run + 1 : run + 2], first_cos)
                first_sin = jnp.where(position >= end, run_sin[run + 1 : run + 2], first_sin)
            rows = chunk_rows(chunk)
            cos_ref[bucket, rows, :] = at_cos * first_cos + at_sin * first_sin
            sin_ref[bucket, rows, :] = (at_sin * first_cos - at_cos * first_sin) * sign
            return carry

        lax.fori_loop(0, LEN // BQ, chunk_tables, 0)


def position_steps():
    lane = np.arange(128) % HEAD_DIM // 2
    frequency = np.exp(lane.astype(np.float32) * np.float32(-2.0 * math.log(10000.0) / HEAD_DIM)).astype(np.float64)
    step = np.arange(32)[:, None]
    coarse, fine = step * 32 * frequency, step * frequency
    return jnp.asarray(np.stack([np.cos(coarse), np.sin(coarse), np.cos(fine), np.sin(fine)]).astype(np.float32))


def enter_rows(x_ref, small_ref, rows, bucket=0):
    normal, _ = norm_parts(x_ref[bucket, rows, :].astype(jnp.float32))
    return (normal * small_ref[0:1, :] + small_ref[1:2, :]).astype(jnp.bfloat16)


def chunk_rows(chunk):
    return pl.ds(pl.multiple_of(chunk * BQ, BQ), BQ)


def forward_kernel(lengths_ref, x_ref, small_ref, cos_ref, sin_ref, in_ref, qkv_ref, mixed_ref, total_ref, enter_ref):
    bucket = pl.program_id(0)

    def project(chunk, carry):
        rows = chunk_rows(chunk)
        enter_ref[0, rows, :] = enter_rows(x_ref, small_ref, rows)
        for pair in range(PAIRS):
            weight = in_ref[:, pair * 384 : pair * 384 + 384]
            project_rows(rows, enter_ref[0, rows, :], cos_ref[0, rows, :], sin_ref[0, rows, :], weight, qkv_ref, pair * 384)
        return carry

    lax.fori_loop(0, LEN // BQ, project, 0)
    attend_forward(lengths_ref, bucket, 0, 0, BQ, qkv_ref, mixed_ref, total_ref)

    def later(step, carry):
        first_row = pl.multiple_of(step * BQ, BQ)
        attend_forward(lengths_ref, bucket, first_row, pl.multiple_of(first_row - BQ, BQ), 2 * BQ, qkv_ref, mixed_ref, total_ref)
        return carry

    lax.fori_loop(1, LEN // BQ, later, 0)


class RunLengths:
    def __init__(self, ref):
        self.ref, self.own = ref, lax.axis_index("tensor")

    def __getitem__(self, where):
        bucket, run = where
        return self.ref[bucket, self.own, run]


def band_biases(lengths, bias_ref):
    def fill(index, carry):
        bucket, block = index // BLOCKS, index % BLOCKS
        position = block * BH + lax.broadcasted_iota(jnp.int32, (BH, 1), 0)
        start, _ = run_starts(lengths, bucket, position)
        lowest = jnp.maximum(start, position - (WINDOW - 1))
        key = jnp.maximum(block - 2, 0) * BH + lax.broadcasted_iota(jnp.int32, (BH, KEYS), 1)
        bias_ref[bucket, block] = jnp.where((key >= lowest) & (key <= position), 0.0, -1e30)
        return carry

    lax.fori_loop(0, MICRO * BLOCKS, fill, 0)


def block_span(block):
    first = max(block - 2, 0)
    return slice(block * BH, block * BH + BH), slice(first * BH, block * BH + BH), (block + 1 - first) * BH


def both_heads(tile):
    return jnp.concatenate([head_lanes(tile, 0), head_lanes(tile, 1)], 0)


def each_head(rows):
    return jnp.where(lane_ids((BH, 128)) < HEAD_DIM, rows[:BH], rows[BH:])


def attend_pair(bias_ref, bucket, block, qkv_ref, mixed_ref, total_ref):
    rows, key_rows, keys = block_span(block)
    bias = bias_ref[bucket, block, :, :keys]
    scores = dot(both_heads(qkv_ref[0, rows, :128]), qkv_ref[0, key_rows, 128:256], NT)
    scores = scores + jnp.concatenate([bias, bias], 0)
    top = jnp.max(scores, -1, keepdims=True)
    powers = jnp.exp(scores - top)
    total = jnp.sum(powers, -1, keepdims=True)
    out = dot(powers.astype(jnp.bfloat16), qkv_ref[0, key_rows, 256:384]) / total
    mixed_ref[0, rows, :] = each_head(out).astype(jnp.bfloat16)
    total_ref[0, rows, :] = each_head(jnp.broadcast_to(top + jnp.log(total), (2 * BH, 128)))


def gather_kernel(
    lengths_ref, x_ref, small_ref, steps_ref, in_ref, out_ref, up_ref, down_ref,
    qkv_ref, mixed_ref, total_ref, cos_ref, sin_ref, *refs,
):
    kept, full, refs = refs[:4], refs[4:8], refs[8:]
    shard_ref, enter_ref, bias_ref, send, recv, own_sem, keep_sem = refs
    bucket = pl.program_id(1)
    step = pl.program_id(0) * MICRO + bucket
    place = Place()

    def copies(stage, which):
        found = []
        for index in which:
            found += gather_copies(index, stage, place, shard_ref, full, send, recv)
        return found

    def start(stage, *which):
        start_all(copies(stage, which))

    def arrive(stage, *which):
        arrive_all(copies(stage, which))

    def own_tiles():
        tiles = []
        for weight, width, offset in ((0, IN_W, 0), (1, OUT_W, IN_W), (2, FF_W, IN_W + OUT_W), (3, FF_W, IN_W + OUT_W + FF_W)):
            target = full[weight].at[place.z, place.x, :, 0:width]
            tiles.append(pltpu.make_async_copy(shard_ref.at[:, offset : offset + width], target, own_sem.at[weight]))
        return tiles

    def keep(index):
        weight, row, count = GATHERED[index][:3]
        rows = pl.ds(row, count)
        return pltpu.make_async_copy(full[weight].at[:, :, rows, :], kept[weight].at[:, :, rows, :], keep_sem.at[index])

    def finish(*which):
        arrive(3, *which)
        arrive(4, *which)
        for index in which:
            keep(index).start()

    def begin():
        lengths = RunLengths(lengths_ref)
        heads = [in_ref[:, head, :] for head in range(2)]
        pieces = [heads[head][:, part * HEAD_DIM : part * HEAD_DIM + HEAD_DIM] for part in range(3) for head in range(2)]
        shard_ref[:, :IN_W] = jnp.concatenate(pieces, 1).astype(jnp.bfloat16)
        shard_ref[:, IN_W : IN_W + OUT_W] = jnp.concatenate([out_ref[0].T, out_ref[1].T], 1).astype(jnp.bfloat16)
        shard_ref[:, IN_W + OUT_W : IN_W + OUT_W + FF_W] = up_ref[...].astype(jnp.bfloat16)
        shard_ref[:, IN_W + OUT_W + FF_W :] = down_ref[...].astype(jnp.bfloat16)
        meet(place)
        start(0, IN)
        start(0, OUT, UP_A, DOWN_A, UP_B, DOWN_B)
        start_all(own_tiles())
        turn_tables_here(lengths, steps_ref, cos_ref, sin_ref)

        def normalise(index, carry):
            rows = chunk_rows(index % (LEN // BQ))
            enter_ref[index // (LEN // BQ), rows, :] = enter_rows(x_ref, small_ref, rows, index // (LEN // BQ))
            return carry

        lax.fori_loop(0, MICRO * LEN // BQ, normalise, 0)
        for tile in own_tiles():
            tile.wait()
        arrive(0, IN)
        start(1, IN)
        arrive(0, OUT)
        start(1, OUT)
        band_biases(lengths, bias_ref)
        arrive(1, IN)

    def send_pair():
        arrive(0, UP_A, DOWN_A)
        start(1, DOWN_A, UP_A)
        start(2, IN)
        start(3, IN)
        arrive(1, OUT)
        start(2, OUT)

    def take_core():
        arrive(3, IN)

    def start_rest():
        arrive(0, UP_B, DOWN_B)
        start(1, DOWN_B, UP_B)

    def turn_first():
        arrive(1, DOWN_A, UP_A)
        start(2, DOWN_A, UP_A)
        start(3, UP_A)

    def take_y():
        arrive(2, IN)
        start(4, IN)

    def turn_rest():
        arrive(1, DOWN_B, UP_B)
        start(2, DOWN_B, UP_B)
        start(3, UP_B)

    def take_last():
        arrive(4, IN)
        keep(IN).start()

    def core_first():
        arrive(2, OUT, DOWN_A)
        start(3, OUT, DOWN_A)
        start(4, OUT, DOWN_A)

    def core_up():
        arrive(2, UP_A)
        start(4, UP_A)

    def keep_first():
        finish(OUT, DOWN_A)

    events = {
        (0, 0): begin, (0, 1): send_pair, (1, 2): start_rest, (2, 0): take_core, (2, 1): turn_first, (4, 0): take_y,
        (4, 2): turn_rest, (5, 2): core_first, (6, 0): take_last, (6, 2): core_up, (7, 2): keep_first,
    }

    def progress(point):
        for (moment, where), event in events.items():
            if where == point:
                pl.when(step == moment)(event)

    progress(0)
    weight = full[0][:, :, :, tile_cols(pl.program_id(0), IN_W)].reshape(D, IN_W)

    project_rows(slice(None), enter_ref[bucket], cos_ref[bucket], sin_ref[bucket], weight, qkv_ref, 0)
    for point, blocks in enumerate(((0, 1, 2), (3, 4, 5), (6, 7))):
        progress(point + 1)
        for block in blocks:
            attend_pair(bias_ref, bucket, block, qkv_ref, mixed_ref, total_ref)

    @pl.when(step == PAIRS * MICRO - 1)
    def _():
        arrive(2, DOWN_B)
        start(3, DOWN_B)
        start(4, DOWN_B)
        arrive(2, UP_B)
        start(4, UP_B)
        finish(UP_A)
        finish(DOWN_B, UP_B)
        for index in range(len(GATHERED)):
            keep(index).wait()
        for stage in range(5):
            sent_all(copies(stage, range(len(GATHERED))))


def mlp_kernel(
    lengths_ref, x_ref, cot_ref, mixed_ref, small_ref, out_ref, up_ref, down_ref,
    block_ref, gy1_ref, gmixed_ref, sums_ref, gout_ref, gup_out_ref, gdown_ref,
    act_ref, gup_ref, keep_ref, enter_t, gmlp_t, gbranch_t,
):
    lengths = RunLengths(lengths_ref) if len(lengths_ref.shape) == 3 else lengths_ref
    bucket = pl.program_id(0)
    chunk = pl.program_id(1)
    buckets = pl.num_programs(0)
    chunks = pl.num_programs(1)

    @pl.when((bucket == 0) & (chunk == 0))
    def _():
        sums_ref[...] = jnp.zeros_like(sums_ref)

    index = bucket * chunks + chunk
    rows = pl.ds(pl.multiple_of(index * MLP_ROWS, MLP_ROWS), MLP_ROWS)
    small = [small_ref[row : row + 1, :] for row in range(6)]
    x = x_ref[0].astype(jnp.float32)
    mixed = mixed_ref[0]
    keep_ref[rows, :] = mixed
    branch = dot(mixed, out_ref[...], NT)
    y_first = x + small[4] * branch
    normal, inverse = norm_parts(y_first)
    enter = (normal * small[2] + small[3]).astype(jnp.bfloat16)
    enter_t[:, rows] = enter.T
    position = chunk * MLP_ROWS + lax.broadcasted_iota(jnp.int32, (MLP_ROWS, 1), 0)
    _, valid = run_starts(lengths, bucket, position)
    grad_y = jnp.where(valid, cot_ref[0].astype(jnp.float32), 0.0)
    grad_mlp = (small[5] * grad_y).astype(jnp.bfloat16)
    gmlp_t[:, rows] = grad_mlp.T
    mlp = jnp.zeros((MLP_ROWS, D), jnp.float32)
    grad_enter = jnp.zeros((MLP_ROWS, D), jnp.float32)
    for part in range(FF // 512):
        cols = slice(part * 512, part * 512 + 512)
        upval = dot(enter, up_ref[:, cols])
        grad_act = dot(grad_mlp, down_ref[:, cols])
        cumulative = 0.5 + 0.5 * lax.erf(upval * (1.0 / math.sqrt(2.0)))
        act = (upval * cumulative).astype(jnp.bfloat16)
        act_ref[rows, cols] = act
        density = jnp.exp(-0.5 * upval * upval) * (1.0 / math.sqrt(2.0 * math.pi))
        grad_up = (grad_act * (cumulative + upval * density)).astype(jnp.bfloat16)
        gup_ref[rows, cols] = grad_up
        mlp = mlp + dot(act, down_ref[:, cols], NT)
        grad_enter = grad_enter + dot(grad_up, up_ref[:, cols], NT)
    block_ref[0] = (y_first + small[5] * mlp).astype(jnp.bfloat16)
    grad_y_first = grad_y + norm_back(grad_enter * small[2], normal, inverse)
    gy1_ref[0] = grad_y_first
    grad_branch = (small[4] * grad_y_first).astype(jnp.bfloat16)
    gbranch_t[:, rows] = grad_branch.T
    gmixed_ref[0] = dot(grad_branch, out_ref[...]).astype(jnp.bfloat16)

    def fold(terms):
        return jnp.sum(terms.reshape(MLP_ROWS // 8, 8, D), 0)

    sums_ref[0] += fold(grad_enter * normal)
    sums_ref[1] += fold(grad_enter)
    sums_ref[2] += fold(grad_y_first * branch)
    sums_ref[3] += fold(grad_y * mlp)

    @pl.when(index == buckets * chunks - 1)
    def _():
        gout_ref[...] = dot(gbranch_t[...], keep_ref[...]).astype(jnp.bfloat16)

        def weight_grads(part, carry):
            cols = pl.ds(pl.multiple_of(part * 512, 512), 512)
            gup_out_ref[:, cols] = dot(enter_t[...], gup_ref[:, cols]).astype(jnp.bfloat16)
            gdown_ref[:, cols] = dot(gmlp_t[...], act_ref[:, cols]).astype(jnp.bfloat16)
            return carry

        lax.fori_loop(0, FF // 512, weight_grads, 0)


def attend_backward(
    lengths_ref, bucket, slot, first_row, first_key, keys, qkv_ref, mixed_ref, gmixed_ref, total_ref, cos_ref, sin_ref, gproj_ref, dk_ref, dv_ref
):
    rows = pl.ds(first_row, BQ)
    key_rows = pl.ds(first_key, keys)
    bias = block_bias(lengths_ref, bucket, first_row, first_key, keys)
    low = lane_ids((BQ, 128)) < HEAD_DIM
    for pair in range(PAIRS):
        base = pair * 384
        queries = qkv_ref[0, rows, base : base + 128]
        keys_rot = qkv_ref[0, key_rows, base + 128 : base + 256]
        values = qkv_ref[0, key_rows, base + 256 : base + 384]
        grad = gmixed_ref[0, rows, pair * 128 : pair * 128 + 128]
        totals = total_ref[0, rows, pair * 128 : pair * 128 + 128]
        product = grad.astype(jnp.float32) * mixed_ref[0, rows, pair * 128 : pair * 128 + 128].astype(jnp.float32)
        grad_q = jnp.zeros((BQ, 128), jnp.float32)
        grad_k = jnp.zeros((keys, 128), jnp.float32)
        grad_v = jnp.zeros((keys, 128), jnp.float32)
        for head in range(2):
            query = head_lanes(queries, head)
            grad_head = head_lanes(grad, head)
            inner = jnp.sum(jnp.where(low == (head == 0), product, 0.0), -1, keepdims=True)
            total = totals[:, head * HEAD_DIM : head * HEAD_DIM + 1]
            attn = jnp.exp(dot(query, keys_rot, NT) + bias - total)
            grad_attn = dot(grad_head, values, NT)
            grad_scores = (attn * (grad_attn - inner)).astype(jnp.bfloat16)
            grad_v = grad_v + dot(attn.astype(jnp.bfloat16), grad_head, TN)
            grad_k = grad_k + dot(grad_scores, query, TN)
            grad_q = grad_q + dot(grad_scores, head_lanes(keys_rot, head))
        cosine = cos_ref[0, rows, :]
        sine = sin_ref[0, rows, :]
        grad_q = grad_q * (HEAD_DIM**-0.5)
        gproj_ref[slot, rows, base : base + 128] = (grad_q * cosine - swap_pairs(grad_q) * sine).astype(jnp.bfloat16)
        lanes = slice(pair * 128, pair * 128 + 128)
        if keys > BQ:
            before = pl.ds(first_key, BQ)
            dk_ref[before, lanes] += grad_k[:BQ]
            dv_ref[before, lanes] += grad_v[:BQ]
            dk_ref[rows, lanes] = grad_k[BQ:]
            dv_ref[rows, lanes] = grad_v[BQ:]
        else:
            dk_ref[rows, lanes] = grad_k
            dv_ref[rows, lanes] = grad_v


def finish_keys(slot, cos_ref, sin_ref, gproj_ref, dk_ref, dv_ref):
    def finish(chunk, carry):
        rows = chunk_rows(chunk)
        cosine = cos_ref[0, rows, :]
        sine = sin_ref[0, rows, :]
        for pair in range(PAIRS):
            grad_k = dk_ref[rows, pair * 128 : pair * 128 + 128]
            turned = grad_k * cosine - swap_pairs(grad_k) * sine
            gproj_ref[slot, rows, pair * 384 + 128 : pair * 384 + 256] = turned.astype(jnp.bfloat16)
            gproj_ref[slot, rows, pair * 384 + 256 : pair * 384 + 384] = dv_ref[rows, pair * 128 : pair * 128 + 128].astype(jnp.bfloat16)
        return carry

    lax.fori_loop(0, LEN // BQ, finish, 0)


def backward_kernel(lengths_ref, qkv_ref, mixed_ref, gmixed_ref, total_ref, cos_ref, sin_ref, gproj_ref, dk_ref, dv_ref):
    bucket = pl.program_id(0)
    shared = (qkv_ref, mixed_ref, gmixed_ref, total_ref, cos_ref, sin_ref, gproj_ref, dk_ref, dv_ref)
    attend_backward(lengths_ref, bucket, 0, 0, 0, BQ, *shared)

    def later(step, carry):
        first_row = pl.multiple_of(step * BQ, BQ)
        attend_backward(lengths_ref, bucket, 0, first_row, pl.multiple_of(first_row - BQ, BQ), 2 * BQ, *shared)
        return carry

    lax.fori_loop(1, LEN // BQ, later, 0)
    finish_keys(0, cos_ref, sin_ref, gproj_ref, dk_ref, dv_ref)


def moments(weight, gradient, first, second):
    first = beta_first * first + (1.0 - beta_first) * gradient
    second = beta_second * second + (1.0 - beta_second) * gradient * gradient
    update = (
        first / (1.0 - beta_first**STEP) / (jnp.sqrt(second / (1.0 - beta_second**STEP)) + adam_eps)
        + decay_rate * weight
    )
    return first, second, update


def planes(which):
    if which == 0:
        return [(slice(None), head, slice(None)) for head in range(2)]
    if which == 1:
        return [(head, slice(None), slice(None)) for head in range(2)]
    return [(slice(None), slice(None))]


def total_of(values_in):
    return jnp.sum(jnp.sum(values_in, 1, keepdims=True), 0, keepdims=True)


def sums_of_squares(tables):
    lanes = lane_ids((1, 512))
    row = jnp.zeros((1, 512), jnp.float32)
    for which, squares in enumerate(tables):
        amount = sum((total_of(plane) for plane in squares[1:]), total_of(squares[0]))
        row = row + jnp.where(lanes == which, amount, 0.0)
    return row


class Everywhere:
    def __init__(self, place, held, got, last, send, recv):
        self.place, self.held, self.got, self.last = place, held, got, last
        self.send, self.recv = send, recv

    def copies(self, stage):
        peers = self.place.peers()
        if stage < 3:
            peer = (CORE, ALONG_Y, ALONG_X)[stage]
            return [remote(self.held.at[stage], self.got.at[stage], self.send.at[stage], self.recv.at[stage], peers[peer])]
        return [
            remote(self.held.at[3], self.last.at[self.place.z], self.send.at[2 + step], self.recv.at[2 + step], peers[step])
            for step in (1, 2, 3)
        ]

    def start(self, stage):
        start_all(self.copies(stage))

    def step(self, stage):
        arrive_all(self.copies(stage))
        if stage == 3:
            return
        total = self.held[stage] + self.got[stage]
        self.held[stage + 1] = total
        if stage == 2:
            self.last[self.place.z] = total
        self.start(stage + 1)

    def total(self):
        return (self.last[0] + self.last[1]) + (self.last[2] + self.last[3])

    def sent(self):
        for stage in range(4):
            sent_all(self.copies(stage))


class Summing:
    def __init__(self, index, place, away, held, got, middle, near, last, send, recv):
        self.weight, self.row, self.count, self.width, self.order = SUMMED[index]
        self.index, self.place = index, place
        self.away, self.held, self.got = away, held, got
        self.middle, self.near, self.last = middle, near, last
        self.send, self.recv = send, recv
        self.rows = pl.ds(self.row, self.count)

    def copies(self, stage, which=(0, 1)):
        place = self.place
        peers = place.peers()

        def copy(source, target, slot, peer):
            return remote(source, target, self.send.at[self.index, slot], self.recv.at[self.index, slot], peers[peer])

        held, rows = self.held, self.rows
        if stage == 0:
            return [copy(self.away(y, rows), self.got.at[y, :, :, rows, :], y, CORE) for y in which]
        if stage == 1:
            if self.order == "yx":
                return [copy(held.at[1, :, :, rows, :], self.middle, 2, ALONG_Y)]
            return [copy(held.at[:, :, 1 - place.x, rows, :], self.middle, 2, ALONG_X)]
        if stage == 2:
            if self.order == "yx":
                return [copy(held.at[0, :, 1 - place.x, rows, :], self.near, 3, ALONG_X)]
            return [copy(held.at[1, :, place.x, rows, :], self.near, 3, ALONG_Y)]
        return [
            copy(held.at[0, (place.z + step) % 4, place.x, rows, :], self.last.at[step - 1], 3 + step, step)
            for step in (1, 2, 3)
        ]

    def start(self, stage, which=(0, 1)):
        start_all(self.copies(stage, which))

    def add(self, where, more):
        held = self.held
        held[where] = (held[where].astype(jnp.float32) + more.astype(jnp.float32)).astype(jnp.bfloat16)

    def arrive(self, stage, which=(0, 1)):
        arrive_all(self.copies(stage, which))
        place, rows = self.place, self.rows

        def block(z, carry):
            if stage == 0:
                for y in which:
                    for x in range(2):
                        self.add((y, z, x, rows, slice(None)), self.got[y, z, x, rows, :])
            elif stage == 1:
                for other in range(2):
                    if self.order == "yx":
                        self.add((0, z, other, rows, slice(None)), self.middle[z, other])
                    else:
                        self.add((other, z, place.x, rows, slice(None)), self.middle[other, z])
            else:
                self.add((0, z, place.x, rows, slice(None)), self.near[z])
            return carry

        lax.fori_loop(0, 4, block, 0)

    def result(self):
        arrive_all(self.copies(3))
        place = self.place
        own = self.held[0, place.z, place.x, self.rows, :].astype(jnp.float32)
        for step in range(3):
            own = own + self.last[step].astype(jnp.float32)
        return own

    def sent(self):
        for stage in range(4):
            sent_all(self.copies(stage))


def middle_shape(index):
    _, _, count, width, order = SUMMED[index]
    return (4, 2, count, width) if order == "yx" else (2, 4, count, width)


def back_pair(bias_ref, bucket, slot, block, qkv_ref, mixed_ref, gmixed_ref, total_ref, cos_ref, sin_ref, gproj_ref, dk_ref, dv_ref):
    rows, key_rows, keys = block_span(block)
    bias = bias_ref[bucket, block, :, :keys]
    keys_rot = qkv_ref[0, key_rows, 128:256]
    query = both_heads(qkv_ref[0, rows, :128])
    grad = gmixed_ref[0, rows, :]
    product = grad.astype(jnp.float32) * mixed_ref[0, rows, :].astype(jnp.float32)
    inner = jnp.sum(both_heads(product), -1, keepdims=True)
    grad = both_heads(grad)
    totals = total_ref[0, rows, :]
    total = jnp.concatenate([totals[:, 0:1], totals[:, HEAD_DIM : HEAD_DIM + 1]], 0)
    attn = jnp.exp(dot(query, keys_rot, NT) + jnp.concatenate([bias, bias], 0) - total)
    grad_attn = dot(grad, qkv_ref[0, key_rows, 256:384], NT)
    grad_scores = (attn * (grad_attn - inner)).astype(jnp.bfloat16)
    grad_v = dot(attn.astype(jnp.bfloat16), grad, TN)
    grad_k = dot(grad_scores, query, TN)
    grad_q = each_head(dot(grad_scores, keys_rot)) * (HEAD_DIM**-0.5)
    turned = grad_q * cos_ref[0, rows, :] - swap_pairs(grad_q) * sin_ref[0, rows, :]
    gproj_ref[bucket, rows, pair_cols(slot, 0)] = turned.astype(jnp.bfloat16)
    old = keys - BH
    if old:
        before = slice(key_rows.start, key_rows.start + old)
        dk_ref[before, :] += grad_k[:old]
        dv_ref[before, :] += grad_v[:old]
    dk_ref[rows, :] = grad_k[old:]
    dv_ref[rows, :] = grad_v[old:]


def pair_cols(slot, which):
    return pl.ds(pl.multiple_of(slot * IN_W + which * 128, 128), 128)


def finish_pair(bucket, slot, cos_ref, sin_ref, gproj_ref, dk_ref, dv_ref):
    def finish(chunk, carry):
        rows = chunk_rows(chunk)
        grad_k = dk_ref[rows, :]
        turned = grad_k * cos_ref[0, rows, :] - swap_pairs(grad_k) * sin_ref[0, rows, :]
        gproj_ref[bucket, rows, pair_cols(slot, 1)] = turned.astype(jnp.bfloat16)
        gproj_ref[bucket, rows, pair_cols(slot, 2)] = dv_ref[rows, :].astype(jnp.bfloat16)
        return carry

    lax.fori_loop(0, LEN // BQ, finish, 0)


def tail_kernel(
    lengths_ref, qkv_ref, mixed_ref, gmixed_ref, total_ref, cos_ref, sin_ref, x_ref, small_ref, sums_ref,
    gy1_hbm, in_hbm, gout_hbm, gup_hbm, gdown_hbm, *refs,
):
    count = len(SUMMED)
    state, refs = refs[:12], refs[12:]
    grad_refs, (xgrad_ref, all_ref, norm_ref), refs = refs[:4], refs[4:7], refs[7:]
    gproj_ref, dk_ref, dv_ref, enter_t, bias_ref, gy1_ref, in_ref, away_in, small_acc, refs = *refs[:9], refs[9:]
    held, got, refs = refs[:4], refs[4:8], refs[8:]
    middle, near, last, refs = refs[:count], refs[count : 2 * count], refs[2 * count : 3 * count], refs[3 * count :]
    small_held, small_got, small_last, norm_held, norm_got, norm_last, refs = *refs[:6], refs[6:]
    send, recv, small_send, small_recv, norm_send, norm_recv, load_sem, late_sem = refs
    bucket = pl.program_id(1)
    slot = PAIRS - 1 - pl.program_id(0)
    step = pl.program_id(0) * MICRO + bucket
    place = Place()
    sources = (None, gout_hbm, gup_hbm, gdown_hbm)

    def away(weight, width):
        if weight == 0:
            return lambda y, rows: away_in.at[y, :, :, rows, :]
        return lambda y, rows: sources[weight].at[:, :, rows, tile_cols(y * 2 + 1, width)]

    items = [
        Summing(
            index, place, away(item[0], item[3]), held[item[0]], got[item[0]], middle[index], near[index], last[index], send, recv
        )
        for index, item in enumerate(SUMMED)
    ]
    out_sum, up_a, down_a, up_b, down_b = items[:5]
    early, late = items[:5], items[5:]
    small_sum = Everywhere(place, small_held, small_got, small_last, small_send, small_recv)
    norm_sum = Everywhere(place, norm_held, norm_got, norm_last, norm_send, norm_recv)

    def loads():
        found = []
        for weight, width in ((1, OUT_W), (2, FF_W), (3, FF_W)):
            for y in range(2):
                source = sources[weight].at[:, :, :, tile_cols(y * 2, width)]
                found.append(pltpu.make_async_copy(source, held[weight].at[y], load_sem.at[weight - 1, y]))
        return found

    def late_loads():
        return [pltpu.make_async_copy(gy1_hbm, gy1_ref, late_sem.at[0]), pltpu.make_async_copy(in_hbm, in_ref, late_sem.at[1])]

    def advance(stage, *which):
        for item in which:
            item.arrive(stage)
            item.start(stage + 1)

    def begin():
        lengths = RunLengths(lengths_ref)
        meet(place)
        for item in early:
            item.start(0)
        start_all(loads())
        start_all(late_loads())
        band_biases(lengths, bias_ref)

        def normalise(index, carry):
            half, chunk = index // (LEN // BQ), index % (LEN // BQ)
            cols = pl.ds(pl.multiple_of(index * BQ, BQ), BQ)
            enter_t[:, cols] = enter_rows(x_ref, small_ref, chunk_rows(chunk), half).T
            return carry

        lax.fori_loop(0, MICRO * LEN // BQ, normalise, 0)

    def at_0_1():
        for load in loads():
            load.wait()
        advance(0, out_sum, up_a, down_a)

    events = {
        (0, 0): begin,
        (0, 1): at_0_1,
        (0, 2): lambda: advance(0, up_b, down_b),
        (2, 1): lambda: advance(1, out_sum),
        (2, 2): lambda: advance(1, down_a),
        (3, 1): lambda: advance(1, up_a),
        (4, 0): lambda: advance(1, down_b),
        (4, 1): lambda: advance(2, out_sum),
        (5, 0): lambda: advance(1, up_b),
        (5, 1): lambda: advance(2, up_a),
        (6, 0): lambda: advance(2, up_b, down_a),
    }

    def progress(point):
        for (moment, where), event in events.items():
            if where == point:
                pl.when(step == moment)(event)

    shared = (qkv_ref, mixed_ref, gmixed_ref, total_ref, cos_ref, sin_ref, gproj_ref, dk_ref, dv_ref)
    for point, blocks in enumerate(((0, 1, 2), (3, 4, 5), (6, 7))):
        progress(point)
        for block in blocks:
            back_pair(bias_ref, bucket, slot, block, *shared)
    finish_pair(bucket, slot, cos_ref, sin_ref, gproj_ref, dk_ref, dv_ref)

    def grad_tile():
        right = gproj_ref[:, :, tile_cols(slot, IN_W)].reshape(MICRO * LEN, IN_W)
        return dot(enter_t[...], right).astype(jnp.bfloat16).reshape(4, 2, 64, IN_W)

    @pl.when((bucket == 1) & (slot % 2 == 1))
    def _():
        away_in[slot // 2] = grad_tile()

    @pl.when((bucket == 1) & (slot % 2 == 0))
    def _():
        held[0][slot // 2] = grad_tile()

    for which in range(2):

        @pl.when((bucket == 1) & (slot == which * 2 + 1))
        def _():
            for item in late:
                item.start(0, (which,))

    @pl.when((bucket == 1) & (slot == 2))
    def _():
        for item in late:
            item.arrive(0, (1,))
            item.start(1)

    @pl.when((bucket == 1) & (slot == 0))
    def _():
        for item in late:
            item.arrive(0, (0,))
            item.arrive(1)
            item.start(2)
        small_acc[...] = jnp.zeros_like(small_acc)
        for load in late_loads():
            load.wait()

        def data_grad(step, carry):
            for stage, item, moment in ((2, down_b, 1), (2, late[0], 2), (2, late[1], 3)):
                pl.when(step == moment)(lambda: advance(stage, item))
            index = step // (LEN // LAST_ROWS)
            rows = pl.ds(pl.multiple_of(step % (LEN // LAST_ROWS) * LAST_ROWS, LAST_ROWS), LAST_ROWS)
            grad_enter = dot(gproj_ref[index, rows, :], in_ref[...], NT)
            normal, inverse = norm_parts(x_ref[index, rows, :].astype(jnp.float32))
            back = norm_back(grad_enter * small_ref[0:1, :], normal, inverse)
            xgrad_ref[index, rows, :] = (gy1_ref[index, rows, :] + back).astype(jnp.bfloat16)
            small_acc[0] += jnp.sum((grad_enter * normal).reshape(LAST_ROWS // 8, 8, D), 0)
            small_acc[1] += jnp.sum(grad_enter.reshape(LAST_ROWS // 8, 8, D), 0)
            return carry

        lax.fori_loop(0, MICRO * LEN // LAST_ROWS, data_grad, 0)

        rows = [jnp.sum(small_acc[row], 0, keepdims=True) for row in range(2)]
        rows += [jnp.sum(sums_ref[row], 0, keepdims=True) for row in range(4)]
        weights_sq = []
        for which in range(4):
            weights_sq.append([state[3 * which][plane] * state[3 * which][plane] for plane in planes(which)])
        rows.append(sums_of_squares(weights_sq))
        rows.append(jnp.zeros((1, D), jnp.float32))
        small_held[0] = jnp.concatenate(rows, 0)
        small_sum.start(0)

        grads = [
            None,
            out_sum.result().T,
            jnp.concatenate([up_a.result(), up_b.result()], 0),
            jnp.concatenate([down_a.result(), down_b.result()], 0),
        ]
        grad_refs[1][0] = grads[1][:HEAD_DIM]
        grad_refs[1][1] = grads[1][HEAD_DIM:]
        grad_refs[2][...] = grads[2]
        grad_refs[3][...] = grads[3]
        small_sum.step(0)
        parts = [item.result() for item in late]
        part = jnp.concatenate(parts, 0)
        for head in range(2):
            pieces = [part[:, which * 128 + head * HEAD_DIM : which * 128 + head * HEAD_DIM + HEAD_DIM] for which in range(3)]
            grad_refs[0][:, head, :] = jnp.concatenate(pieces, 1)
        updates_sq = []
        for which in range(4):
            squares = []
            for plane in planes(which):
                weight, first, second = (state[3 * which + kind][plane] for kind in range(3))
                update = moments(weight, grad_refs[which][plane], first, second)[2]
                squares.append(update * update)
            updates_sq.append(squares)
        norm_held[0] = jnp.broadcast_to(sums_of_squares(updates_sq)[:, :128], (8, 128))
        norm_sum.start(0)
        small_sum.step(1)
        norm_sum.step(0)
        small_sum.step(2)
        norm_sum.step(1)
        small_sum.step(3)
        norm_sum.step(2)
        norm_sum.step(3)
        all_ref[...] = small_sum.total()
        norm_ref[...] = norm_sum.total()
        for item in early + late:
            item.sent()
        small_sum.sent()
        norm_sum.sent()


def lamb_kernel(*refs):
    state, grads, refs = refs[:12], refs[12:16], refs[16:]
    small_ref, small_first_ref, small_second_ref, all_ref, norm_ref, xgrad_ref, refs = *refs[:6], refs[6:]
    outs, (grad_ref, new_ref, first_ref, second_ref, norms_ref, xgrad_out_ref) = refs[:16], refs[16:]
    xgrad_out_ref[...] = xgrad_ref[...]
    weight_norm = jnp.sqrt(all_ref[6:7, 0:128])
    update_sq = norm_ref[0:1, :]
    ratio = learn_rate * weight_norm * lax.rsqrt(update_sq + 1e-12)
    for which in range(4):
        scale = ratio[:, which : which + 1]
        for plane in planes(which):
            weight, first, second = (state[3 * which + kind][plane] for kind in range(3))
            first, second, update = moments(weight, grads[which][plane], first, second)
            new = weight - scale * update
            outs[4 * which][plane] = new
            outs[4 * which + 1][plane] = first
            outs[4 * which + 2][plane] = second
            outs[4 * which + 3][plane] = new.astype(jnp.bfloat16)
    small = small_ref[...]
    small_grad = all_ref[0:6, :]
    grad_ref[...] = small_grad
    first, second, update = moments(small, small_grad, small_first_ref[...], small_second_ref[...])
    small_sq = jnp.sum(small * small, 1, keepdims=True)
    change_sq = jnp.sum(update * update, 1, keepdims=True)
    new_ref[...] = small - learn_rate * jnp.sqrt(small_sq) * lax.rsqrt(change_sq + 1e-12) * update
    first_ref[...] = first
    second_ref[...] = second
    lanes = lane_ids((1, 128))
    top = jnp.where(lanes < 4, weight_norm, 0.0)
    bottom = jnp.where(lanes < 4, jnp.sqrt(update_sq), 0.0)
    for row in range(6):
        top = top + jnp.where(lanes == 4 + row, jnp.sqrt(small_sq[row : row + 1]), 0.0)
        bottom = bottom + jnp.where(lanes == 4 + row, jnp.sqrt(change_sq[row : row + 1]), 0.0)
    norms_ref[0:1, :] = top[:, :10]
    norms_ref[1:2, :] = bottom[:, :10]


def whole(shape):
    return pl.BlockSpec(shape, lambda *ids: (0,) * len(shape), pipeline_mode=pl.Buffered(1))


def per_bucket(*shape):
    return pl.BlockSpec((1,) + shape, lambda b: (b, 0, 0))


def bf16(*shape):
    return jax.ShapeDtypeStruct(shape, jnp.bfloat16)


def f32(*shape):
    return jax.ShapeDtypeStruct(shape, jnp.float32)


def vmem16(*shape):
    return pltpu.VMEM(shape, jnp.bfloat16)


def vmem32(*shape):
    return pltpu.VMEM(shape, jnp.float32)


SCALARS = pl.BlockSpec(memory_space=pltpu.SMEM)
ANYWHERE = pl.BlockSpec(memory_space=pl.ANY)


def params(count, collective=None):
    more = {} if collective is None else dict(collective_id=collective, has_side_effects=True)
    return pltpu.CompilerParams(dimension_semantics=("arbitrary",) * count, vmem_limit_bytes=VMEM_LIMIT, **more)


def turn_tables(lengths):
    ends = jnp.cumsum(lengths, axis=1)
    position = jnp.arange(LEN, dtype=jnp.int32)
    passed = position[None, :, None] >= ends[:, None, : CLIPS - 1]
    start = jnp.max(jnp.where(passed, ends[:, None, : CLIPS - 1], 0), axis=2)
    offset = (position[None, :] - start).astype(jnp.float32)
    frequency = jnp.exp(jnp.arange(HEAD_DIM // 2, dtype=jnp.float32) * (-2.0 * math.log(10000.0) / HEAD_DIM))
    angles = offset[:, :, None] * frequency
    cosine = jnp.repeat(jnp.cos(angles), 2, axis=-1)
    sine = jnp.sin(angles)
    sine = jnp.stack([-sine, sine], axis=-1).reshape(cosine.shape)
    return jnp.concatenate([cosine, cosine], -1), jnp.concatenate([sine, sine], -1)


def attention_forward(lengths, x, small, cosine, sine, in_mat):
    count = x.shape[0]
    return pl.pallas_call(
        forward_kernel,
        grid=(count,),
        in_specs=[SCALARS, per_bucket(LEN, D), whole((6, D)), per_bucket(LEN, 128), per_bucket(LEN, 128), whole((D, 3 * D))],
        out_specs=[per_bucket(LEN, 3 * D), per_bucket(LEN, D), per_bucket(LEN, D), per_bucket(LEN, D)],
        out_shape=[bf16(count, LEN, 3 * D), bf16(count, LEN, D), f32(count, LEN, D), bf16(count, LEN, D)],
        compiler_params=params(1),
        name="attention_forward",
    )(lengths, x, small, cosine, sine, in_mat)


def gather_forward(lengths, x, small, weights):
    shapes = [(4, 2, 64, 4 * width) for width in (IN_W, OUT_W, FF_W, FF_W)]

    def per_pair(width):
        return pl.BlockSpec((1, LEN, width), lambda pair, bucket: (bucket, 0, pair))

    return pl.pallas_call(
        gather_kernel,
        grid=(PAIRS, MICRO),
        in_specs=[SCALARS, whole((MICRO, LEN, D)), whole((6, D)), whole((4, 32, 128))] + [whole(item.shape) for item in weights],
        out_specs=[per_pair(IN_W), per_pair(128), per_pair(128)] + [whole((MICRO, LEN, 128))] * 2 + [ANYWHERE] * 4,
        out_shape=[bf16(MICRO, LEN, 3 * D), bf16(MICRO, LEN, D), f32(MICRO, LEN, D)]
        + [f32(MICRO, LEN, 128)] * 2
        + [bf16(*shape) for shape in shapes],
        scratch_shapes=[vmem16(*shape) for shape in shapes]
        + [
            vmem16(64, SHARD_W),
            vmem16(MICRO, LEN, D),
            vmem32(MICRO, BLOCKS, BH, KEYS),
            pltpu.SemaphoreType.DMA((6, 8)),
            pltpu.SemaphoreType.DMA((6, 8)),
            pltpu.SemaphoreType.DMA((4,)),
            pltpu.SemaphoreType.DMA((6,)),
        ],
        compiler_params=params(2, 1),
        name="gather_forward",
    )(lengths, x, small, position_steps(), *weights)


def mlp_both(lengths, x, cot, mixed, small, out_mat, up_mat, down_mat):
    count = x.shape[0]
    rows = count * LEN

    def chunked(width):
        return pl.BlockSpec((1, MLP_ROWS, width), lambda b, i: (b, i, 0))

    return pl.pallas_call(
        mlp_kernel,
        grid=(count, LEN // MLP_ROWS),
        in_specs=[SCALARS, chunked(D), chunked(D), chunked(D), whole((6, D)), whole((D, D)), whole((D, FF)), whole((D, FF))],
        out_specs=[chunked(D), chunked(D), chunked(D), whole((4, 8, D)), whole((D, D)), whole((D, FF)), whole((D, FF))],
        out_shape=[
            bf16(count, LEN, D), f32(count, LEN, D), bf16(count, LEN, D), f32(4, 8, D), bf16(D, D), bf16(D, FF), bf16(D, FF),
        ],
        scratch_shapes=[
            vmem16(rows, FF), vmem16(rows, FF), vmem16(rows, D), vmem16(D, rows), vmem16(D, rows), vmem16(D, rows),
        ],
        compiler_params=params(2),
        name="mlp_both",
    )(lengths, x, cot, mixed, small, out_mat, up_mat, down_mat)


def attention_backward(lengths, qkv, mixed, gmixed, totals, cosine, sine):
    count = qkv.shape[0]
    return pl.pallas_call(
        backward_kernel,
        grid=(count,),
        in_specs=[SCALARS, per_bucket(LEN, 3 * D), per_bucket(LEN, D), per_bucket(LEN, D), per_bucket(LEN, D), per_bucket(LEN, 128), per_bucket(LEN, 128)],
        out_specs=per_bucket(LEN, 3 * D),
        out_shape=bf16(count, LEN, 3 * D),
        scratch_shapes=[vmem32(LEN, D), vmem32(LEN, D)],
        compiler_params=params(1),
        name="attention_backward",
    )(lengths, qkv, mixed, gmixed, totals, cosine, sine)


def backward_tail(lengths, qkv, mixed, gmixed, totals, cosine, sine, x, small, gy1, sums, in_mat, gout, gup, gdown, state):
    widths = (IN_W, OUT_W, FF_W, FF_W)
    dma = pltpu.SemaphoreType.DMA
    count = len(SUMMED)
    grad_shapes = [f32(*state[3 * which].shape) for which in range(4)]

    def per_pair(width):
        return pl.BlockSpec((1, LEN, width), lambda pair, bucket: (bucket, 0, PAIRS - 1 - pair))

    tables = pl.BlockSpec((1, LEN, 128), lambda pair, bucket: (bucket, 0, 0))
    return pl.pallas_call(
        tail_kernel,
        grid=(PAIRS, MICRO),
        in_specs=[SCALARS, per_pair(IN_W), per_pair(128), per_pair(128), per_pair(128), tables, tables]
        + [whole((MICRO, LEN, D)), whole((6, D)), whole((4, 8, D))]
        + [ANYWHERE] * 5
        + [whole(item.shape) for item in state],
        out_specs=[whole(item.shape) for item in grad_shapes] + [whole((MICRO, LEN, D)), whole((8, D)), whole((8, 128))],
        out_shape=grad_shapes + [bf16(MICRO, LEN, D), f32(8, D), f32(8, 128)],
        scratch_shapes=[
            vmem16(MICRO, LEN, 3 * D), vmem32(LEN, 128), vmem32(LEN, 128), vmem16(D, MICRO * LEN), vmem32(MICRO, BLOCKS, BH, KEYS),
            vmem32(MICRO, LEN, D), vmem16(D, 3 * D), vmem16(2, 4, 2, 64, IN_W), vmem32(2, 8, D),
        ]
        + [vmem16(2, 4, 2, 64, width) for width in widths]
        + [vmem16(2, 4, 2, 64, width) for width in widths]
        + [vmem16(*middle_shape(index)) for index in range(count)]
        + [vmem16(4, SUMMED[index][2], SUMMED[index][3]) for index in range(count)]
        + [vmem16(3, SUMMED[index][2], SUMMED[index][3]) for index in range(count)]
        + [vmem32(4, 8, D), vmem32(3, 8, D), vmem32(4, 8, D), vmem32(4, 8, 128), vmem32(3, 8, 128), vmem32(4, 8, 128)]
        + [dma((count, 7)), dma((count, 7)), dma((6,)), dma((6,)), dma((6,)), dma((6,)), dma((3, 2)), dma((2,))],
        compiler_params=params(2, 2),
        name="backward_tail",
    )(lengths, qkv, mixed, gmixed, totals, cosine, sine, x, small, sums, gy1, in_mat, gout, gup, gdown, *state)


def lamb_all(state, grads, small, small_first, small_second, everything, norm_squares, input_grad):
    outs = []
    for which in range(4):
        shape = state[3 * which].shape
        outs += [f32(*shape)] * 3 + [bf16(*shape)]
    outs += [f32(6, D)] * 4 + [f32(2, 10), bf16(MICRO, LEN, D)]
    return pl.pallas_call(
        lamb_kernel,
        out_shape=outs,
        compiler_params=pltpu.CompilerParams(vmem_limit_bytes=VMEM_LIMIT),
        name="lamb_all",
    )(*state, *grads, small, small_first, small_second, everything, norm_squares, input_grad)


def tile_shard(in_proj, out_proj, up_proj, down_proj):
    depth, heads_here, _ = in_proj.shape
    out_cols = out_proj.reshape(heads_here * HEAD_DIM, depth).T
    parts = [in_proj.reshape(depth, -1), out_cols, up_proj, down_proj.T]
    return jnp.concatenate(parts, axis=1).astype(jnp.bfloat16)


def on_device(
    frames, cotangent, clip_lengths, in_proj, out_proj, up_proj, down_proj, small_params,
    in_first, in_second, out_first, out_second, up_first, up_second, down_first, down_second,
    small_first, small_second,
):
    lengths = clip_lengths
    qkv, mixed, totals, cosine, sine, in_full, out_full, up_full, down_full = gather_forward(
        lengths, frames, small_params, (in_proj, out_proj, up_proj, down_proj.T)
    )
    block_out, gy1, gmixed, sums, gout, gup, gdown = mlp_both(
        lengths, frames, cotangent, mixed, small_params, out_full.reshape(D, D), up_full.reshape(D, FF), down_full.reshape(D, FF)
    )
    state = (
        in_proj, in_first, in_second, out_proj, out_first, out_second, up_proj, up_first, up_second, down_proj.T, down_first.T, down_second.T,
    )
    *grads, input_grad, everything, norm_squares = backward_tail(
        lengths, qkv, mixed, gmixed, totals, cosine, sine, frames, small_params, gy1, sums, in_full.reshape(D, 3 * D),
        gout.reshape(4, 2, 64, D), gup.reshape(4, 2, 64, FF), gdown.reshape(4, 2, 64, FF), state,
    )
    *outs, input_grad = lamb_all(state, grads, small_params, small_first, small_second, everything, norm_squares, input_grad)
    outs[12:16] = [item.T for item in outs[12:16]]
    return (block_out, input_grad, *outs)


def on_any_mesh(
    frames, cotangent, clip_lengths, in_proj, out_proj, up_proj, down_proj, small_params,
    in_first, in_second, out_first, out_second, up_first, up_second, down_first, down_second,
    small_first, small_second,
):
    rows_here = frames.shape[1]
    own_buckets = rows_here // LEN
    first_bucket = lax.axis_index("tensor") * own_buckets
    lengths = lax.dynamic_slice_in_dim(clip_lengths, first_bucket, own_buckets, 1).reshape(-1, CLIPS)
    count = MICRO * own_buckets
    x = frames.reshape(count, LEN, D)
    cot = cotangent.reshape(count, LEN, D)
    tensor_size = lax.axis_size("tensor")
    dp_size = lax.axis_size("dp")
    depth = in_proj.shape[0]
    heads_here = in_proj.shape[1]
    ff_here = up_proj.shape[1]

    shard = tile_shard(in_proj, out_proj, up_proj, down_proj)
    gathered = lax.all_gather(shard, ("dp", "tensor"), axis=0)
    gathered = gathered.reshape(dp_size, tensor_size, depth, shard.shape[1])
    gathered = jnp.moveaxis(gathered, 1, 2).reshape(D, tensor_size, shard.shape[1])
    edge0 = heads_here * 192
    edge1 = edge0 + heads_here * HEAD_DIM
    edge2 = edge1 + ff_here
    in_mat = gathered[:, :, :edge0].reshape(D, PAIRS, 2, 3, HEAD_DIM).transpose(0, 1, 3, 2, 4).reshape(D, 3 * D)
    out_mat = gathered[:, :, edge0:edge1].reshape(D, D)
    up_mat = gathered[:, :, edge1:edge2].reshape(D, FF)
    down_mat = gathered[:, :, edge2:].reshape(D, FF)

    cosine, sine = turn_tables(lengths)
    qkv, mixed, totals, enter1 = attention_forward(lengths, x, small_params, cosine, sine, in_mat)
    block_out, grad_y_first, grad_mixed, sums, grad_out, grad_upw, grad_down = mlp_both(
        lengths, x, cot, mixed, small_params, out_mat, up_mat, down_mat
    )

    def weight_grad(left, right):
        return dot(left.reshape(-1, left.shape[-1]), right.reshape(-1, right.shape[-1]), TN).astype(jnp.bfloat16)

    grad_proj = attention_backward(lengths, qkv, mixed, grad_mixed, totals, cosine, sine)
    grad_in = weight_grad(enter1, grad_proj)
    grad_in = grad_in.reshape(D, PAIRS, 3, 2, HEAD_DIM).transpose(0, 1, 3, 2, 4)

    def by_owner(mat):
        return jnp.moveaxis(mat.reshape(dp_size, depth, tensor_size, -1), 2, 1)

    stacked = jnp.concatenate([by_owner(grad_in), by_owner(grad_out), by_owner(grad_upw), by_owner(grad_down)], axis=-1)
    owned = lax.psum_scatter(
        stacked.reshape(dp_size * tensor_size, depth, -1), ("dp", "tensor"), scatter_dimension=0, tiled=False
    ).astype(jnp.float32)

    grad_enter1 = dot(grad_proj.reshape(-1, 3 * D), in_mat, NT).reshape(count, LEN, D)
    normal1, inverse1 = norm_parts(x.astype(jnp.float32))
    input_grad = (grad_y_first + norm_back(grad_enter1 * small_params[0], normal1, inverse1)).astype(jnp.bfloat16)
    late = jnp.sum(sums, axis=1)
    small_terms = jnp.stack(
        [jnp.sum(grad_enter1 * normal1, (0, 1)), jnp.sum(grad_enter1, (0, 1)), late[0], late[1], late[2], late[3]]
    )

    grads = (
        owned[:, :edge0].reshape(in_proj.shape),
        owned[:, edge0:edge1].T.reshape(out_proj.shape),
        owned[:, edge1:edge2],
        owned[:, edge2:].T,
    )
    weights_in = (in_proj, out_proj, up_proj, down_proj)
    firsts = (in_first, out_first, up_first, down_first)
    seconds = (in_second, out_second, up_second, down_second)
    own_squares = jnp.stack([jnp.sum(weight * weight) for weight in weights_in])
    small_grad, weight_squares = lax.psum((small_terms, own_squares), ("dp", "tensor"))
    new_firsts = []
    new_seconds = []
    updates = []
    for weight, gradient, first, second in zip(weights_in, grads, firsts, seconds):
        first = beta_first * first + (1.0 - beta_first) * gradient
        second = beta_second * second + (1.0 - beta_second) * gradient * gradient
        update = (
            first / (1.0 - beta_first**STEP) / (jnp.sqrt(second / (1.0 - beta_second**STEP)) + adam_eps)
            + decay_rate * weight
        )
        new_firsts.append(first)
        new_seconds.append(second)
        updates.append(update)
    update_squares = lax.psum(jnp.stack([jnp.sum(update * update) for update in updates]), ("dp", "tensor"))
    trust_ratio = jnp.sqrt(weight_squares) * lax.rsqrt(update_squares + 1e-12)
    new_weights = [weights_in[index] - learn_rate * trust_ratio[index] * updates[index] for index in range(4)]
    small_first_new = beta_first * small_first + (1.0 - beta_first) * small_grad
    small_second_new = beta_second * small_second + (1.0 - beta_second) * small_grad * small_grad
    small_update = (
        small_first_new / (1.0 - beta_first**STEP) / (jnp.sqrt(small_second_new / (1.0 - beta_second**STEP)) + adam_eps)
        + decay_rate * small_params
    )
    small_weight_sq = jnp.sum(small_params * small_params, axis=1, keepdims=True)
    small_update_sq = jnp.sum(small_update * small_update, axis=1, keepdims=True)
    small_new = small_params - learn_rate * jnp.sqrt(small_weight_sq) * lax.rsqrt(small_update_sq + 1e-12) * small_update
    norms = jnp.stack(
        [
            jnp.concatenate([jnp.sqrt(weight_squares), jnp.sqrt(small_weight_sq).reshape(-1)]),
            jnp.concatenate([jnp.sqrt(update_squares), jnp.sqrt(small_update_sq).reshape(-1)]),
        ]
    )
    outputs = [block_out.reshape(frames.shape), input_grad.reshape(frames.shape)]
    for new, first, second in zip(new_weights, new_firsts, new_seconds):
        outputs += [new, first, second, new.astype(jnp.bfloat16)]
    return tuple(outputs + [small_grad, small_new, small_first_new, small_second_new, norms])


def solution(mesh):
    rows = P(None, ("dp", "tensor"), None)
    in_spec = P("dp", "tensor", None)
    out_spec = P("tensor", None, "dp")
    up_spec = P("dp", "tensor")
    down_spec = P("tensor", "dp")
    shape = dict(mesh.shape)
    small_slice = shape["dp"] == HERE_DP and shape["tensor"] == HERE_TENSOR
    return jax.shard_map(
        on_device if small_slice else on_any_mesh,
        mesh=mesh,
        in_specs=(
            rows, rows, P(None, "dp", None), in_spec, out_spec, up_spec, down_spec, P(),
            in_spec, in_spec, out_spec, out_spec, up_spec, up_spec, down_spec, down_spec, P(), P(),
        ),
        out_specs=(rows, rows) + (in_spec,) * 4 + (out_spec,) * 4 + (up_spec,) * 4 + (down_spec,) * 4 + (P(),) * 5,
        check_vma=False,
    )
```
